32 devices in a mesh: sector: 4 (over z), axial: 8 (over y, x, core).
Axes of the slice: x: 2, y: 2, z: 4, core: 2. Of those that a mesh axis runs over, the one named last changes fastest.
Arguments:
- kbb: float32 [4096, 64, 64], P(('sector', 'axial')), as said below
- interior: bfloat16 [4096, 256, 64], P(('sector', 'axial')), may hold values from -0.075683594 to 0.075683594
- node_lists: int32 [4096, 64], P(('sector', 'axial')), may hold values from -1 to 63
- owners: int32 [4096, 1], P(('sector', 'axial')), may hold values from 0 to 31; in each aligned block of 128 rows (0 to 127, 128 to 255, ...) at most 8 rows name the same one
- patch_ids: int32 [4096], P(('sector', 'axial')), may hold values from 0 to 63
- counts: int32 [32], P(('sector', 'axial')), may hold values from 96 to 128
- capacity: float32 [131072], P(('sector', 'axial')), may hold values from 0.2 to 2
- links: int32 [2, 512, 2], P(None, ('sector', 'axial')), may hold values from 0 to 63
- conduct: float32 [2, 512, 64], P(None, ('sector', 'axial')), may hold values from 0.5 to 4
- loads: float32 [131072, 128], P(('sector', 'axial')), may hold values from -24 to 24
Outputs:
- current_estimate: float32 [131072, 128], P(('sector', 'axial'))
- remaining_imbalance: float32 [131072, 128], P(('sector', 'axial'))
The draws below stay inside these ranges and needn't reach their ends.
Inputs may be any that keep to these rules, and one draw needn't show every extreme that they name: `owners`: no owner is named by more than 8 of one device's slots, live or not, and in every draw some owner is named by exactly 8 of some device's slots. The live slots of a device are its first counts slots; the others are padding. `kbb`: the boundary block is symmetric with non-positive entries off the diagonal whose row sums stay under its diagonal.
All inputs are finite; a program needn't handle non-finite values.
Results may differ from the reference program's by a relative error of at most 0.0003.
Values sent between devices are 32-bit elements; how exact they have to be, the bound alone decides.
No kernel may reach another device: no remote copies, remote signals or barrier semaphores. Data moves between devices by JAX's collectives and lax.ppermute only.
A program may use at most 128 MiB of HBM per device.

```python
import math
import jax
import jax.numpy as jnp
import numpy as np
from jax import lax

BN = 64
NI = 256
ITERS = 3
PATCH_DEV = 64
ELEM_DEV = 128
HEATING_SCENARIO = 128
LINKS = 16
CAP = 8
THERMAL_POINTS = 131072
ELEMS = 4096
LINKS_ALL = 512
N_SECTOR = 4
N_AXIAL = 8
DEVICES = 32


def draw_kbb(key, part):
    first, second = jax.random.split(key)
    spread = jax.random.uniform(first, (ELEMS, BN, BN), jnp.float32, 0.0, 1.6 / BN)
    offdiag = -(spread + jnp.swapaxes(spread, 1, 2)) * 0.5
    extra = jnp.exp(jax.random.uniform(second, (ELEMS, BN), jnp.float32, math.log(0.5), math.log(2.0)))
    unit = jnp.eye(BN, dtype=jnp.float32)
    return offdiag * (1.0 - unit) + unit * (2.0 + extra)[:, :, None]


def plant(drawn, stream_key, smallest, top_value):
    index_at = [jax.random.randint(jax.random.fold_in(stream_key, axis), (), 0, length) for axis, length in enumerate(drawn.shape)]
    main_axis = drawn.shape.index(max(drawn.shape))
    neighbour = index_at[:main_axis] + [(index_at[main_axis] + 1) % drawn.shape[main_axis]] + index_at[main_axis + 1:]
    return drawn.at[tuple(index_at)].set(smallest).at[tuple(neighbour)].set(top_value)


def level_of(rng, extent, cuts, least, high):
    def one(position, shards_of):
        draws = jax.random.uniform(jax.random.fold_in(jax.random.fold_in(rng, 6), position), (shards_of,), jnp.float32, least / len(cuts), high / len(cuts))
        return jnp.repeat(jnp.exp(draws), extent[position] // shards_of).reshape((-1,) + (1,) * (len(extent) - position - 1))

    gain = one(*cuts[0])
    for cut in cuts[1:]:
        gain = gain * one(*cut)
    return gain


def shared_out(own_key, own, number, rows, count, top, most, lean):
    ranking = jax.random.permutation(own_key, count)
    heavy_load, ordinary = shares(count, rows * top, most, lean, True), shares(count, rows * top, most, lean, False)
    places = jnp.arange(count)

    def named(tallies, rotation):
        used = int((tallies > 0).sum())
        fixed = max(1, used // 4)
        passed = fixed + (places - fixed + rotation * (used - fixed)) % max(1, count - fixed)
        return jnp.zeros((count,), jnp.int32).at[ranking[jnp.where(places < fixed, places, passed)]].set(jnp.asarray(tallies, jnp.int32))

    tallies = jnp.where(number % 4 == 0, named(heavy_load, number // 4), named(ordinary, number - number // 4 - 1))
    mixed = jax.random.permutation(jax.random.fold_in(own, 3), count)
    giver, taker = mixed[0:count // 2 * 2:2], mixed[1:count // 2 * 2:2]
    margin = jnp.minimum(tallies[giver] - 1, most - tallies[taker]) // 2
    margin = jnp.where((giver == ranking[0]) | (taker == ranking[0]) | (tallies[taker] == 0), 0, jnp.maximum(margin, 0))
    passed = jax.random.randint(jax.random.fold_in(own, 4), (count // 2,), 0, 1 << 20) % (margin + 1)
    tallies = tallies.at[giver].add(-passed).at[taker].add(passed)
    labels = jnp.searchsorted(jnp.cumsum(tallies), jnp.arange(rows * top), side="right").astype(jnp.int32)
    grid = labels.reshape(top, rows).T
    grid = grid[jax.random.permutation(jax.random.fold_in(own, 1), rows)]
    rotation = jax.random.randint(jax.random.fold_in(own, 2), (rows, 1), 0, top)
    return jnp.take_along_axis(grid, (jnp.arange(top)[None, :] + rotation) % top, axis=1)


def shares(amount, total, limit, skew, full):
    portions = [(1 << 20) // math.isqrt(standing ** skew) + 1 for standing in range(1, amount + 1)]
    largest = limit if full else min(limit, max(-(-total // amount), total * portions[0] // sum(portions)))
    least = 1 if total - largest >= amount - 1 else 0
    holding, spare = [largest] + [least] * (amount - 1), total - largest - least * (amount - 1)
    while spare > 0:
        movable = [i for i in range(1, amount) if holding[i] < largest] or [i for i in range(1, amount) if holding[i] < limit]
        pool, remaining = sum([portions[i] for i in movable]), spare
        for i in movable:
            more = min(limit - holding[i], max(1, remaining * portions[i] // pool), spare)
            holding[i] = holding[i] + more
            spare = spare - more
    return np.array(holding)


def normal_values(rng, shape, scale, most, pieces=(), held_as=jnp.bfloat16):
    values = jax.random.normal(rng, shape, jnp.float32) * scale
    if len(pieces) > 0:
        values = level_of(rng, shape, pieces, -0.22, 0.18) * values
    return jnp.clip(values, min=-most, max=most).astype(held_as)


def setup_inputs(seed: int = 0) -> dict:
    arg_keys = jax.random.split(jax.random.key(seed), 11)
    kbb = draw_kbb(jax.random.fold_in(arg_keys[10], 71), 0)
    interior = jnp.clip(jax.random.uniform(arg_keys[1], (ELEMS, NI, BN), jnp.float32, -0.075683594, 0.075683594) * level_of(arg_keys[1], (ELEMS, NI, BN), ((0, 32),), -0.4, 0.0), -0.075683594, 0.075683594).astype(jnp.bfloat16)
    node_lists = plant(jax.random.randint(arg_keys[2], (ELEMS, BN), -1, BN), jax.random.fold_in(arg_keys[2], 1), -1, BN - 1).astype(jnp.int32)
    owners_keys = jax.random.split(jax.random.fold_in(arg_keys[3], 1), ELEMS // ELEM_DEV)
    owners_turns = jax.random.permutation(jax.random.fold_in(arg_keys[3], 3), ELEMS // ELEM_DEV)
    owners = jax.vmap(lambda own, number: shared_out(jax.random.fold_in(arg_keys[3], 2), own, number, ELEM_DEV, DEVICES, 1, CAP, 2))(owners_keys, owners_turns).reshape((ELEMS, 1))
    patch_ids = plant(jax.random.randint(arg_keys[4], (ELEMS,), 0, PATCH_DEV), jax.random.fold_in(arg_keys[4], 1), 0, PATCH_DEV - 1).astype(jnp.int32)
    counts = plant(jax.random.randint(arg_keys[5], (DEVICES,), 3 * ELEM_DEV // 4, ELEM_DEV + 1), jax.random.fold_in(arg_keys[5], 1), 3 * ELEM_DEV // 4, ELEM_DEV).astype(jnp.int32)
    capacity = jnp.clip(jnp.exp(math.log(2.0) - 2.3025851 * jax.random.uniform(arg_keys[6], (THERMAL_POINTS,), jnp.float32) ** level_of(arg_keys[6], (THERMAL_POINTS,), ((0, 32),), -0.2, 0.2)), 0.2, 2.0)
    links = plant(jax.random.randint(arg_keys[7], (2, LINKS_ALL, 2), 0, PATCH_DEV), jax.random.fold_in(arg_keys[7], 1), 0, PATCH_DEV - 1).astype(jnp.int32)
    conduct = jnp.clip(jnp.exp(math.log(4.0) - 2.0794415 * jax.random.uniform(arg_keys[8], (2, LINKS_ALL, BN), jnp.float32) ** level_of(arg_keys[8], (2, LINKS_ALL, BN), ((1, 32),), -0.2, 0.2)), 0.5, 4.0)
    loads = normal_values(arg_keys[9], (THERMAL_POINTS, HEATING_SCENARIO), 4.0, 24.0, ((0, 32),), jnp.float32)
    return {"kbb": kbb, "interior": interior, "node_lists": node_lists, "owners": owners, "patch_ids": patch_ids, "counts": counts, "capacity": capacity, "links": links, "conduct": conduct, "loads": loads}


def reference(kbb, interior, node_lists, owners, patch_ids, counts, capacity, links, conduct, loads):
    highest = lax.Precision.HIGHEST
    inner = interior.astype(jnp.float32)
    schur = kbb - jnp.einsum('eib,eic->ebc', inner, inner, precision=highest)
    live = (jnp.arange(ELEM_DEV, dtype=jnp.int32)[None, :] < counts[:, None]).reshape(-1).astype(jnp.float32)
    picker = (node_lists[:, :, None] == jnp.arange(BN, dtype=jnp.int32)[None, None, :]).astype(jnp.float32)
    half = jnp.einsum('esj,est->ejt', picker, schur, precision=highest)
    placed = jnp.einsum('ejt,etk->ejk', half, picker, precision=highest)
    segment = owners[:, 0] * PATCH_DEV + patch_ids
    assembled = jax.ops.segment_sum(placed * live[:, None, None], segment, num_segments=DEVICES * PATCH_DEV)
    assembled = assembled.reshape(N_SECTOR, N_AXIAL, PATCH_DEV, BN, BN)
    heat = capacity.reshape(N_SECTOR, N_AXIAL, PATCH_DEV, BN)
    link_table = links.reshape(2, N_SECTOR, N_AXIAL, LINKS, 2)
    gains = conduct.reshape(2, N_SECTOR, N_AXIAL, LINKS, BN)
    pick_rows = jax.vmap(jax.vmap(lambda table, index: table[index]))

    def onehot(index):
        return (index[..., None] == jnp.arange(PATCH_DEV, dtype=jnp.int32)).astype(jnp.float32)

    def spread_field(index, values):
        return jnp.einsum('xylp,xylir->xypir', onehot(index), values, precision=highest)

    def spread_flat(index, values):
        return jnp.einsum('xylp,xyli->xypi', onehot(index), values, precision=highest)

    def sector_up(field):
        return jnp.roll(field, -1, axis=0)

    def sector_down(field):
        return jnp.roll(field, 1, axis=0)

    def axial_up(field):
        return jnp.concatenate([field[:, 1:], jnp.zeros_like(field[:, :1])], axis=1)

    def axial_down(field):
        return jnp.concatenate([jnp.zeros_like(field[:, :1]), field[:, :-1]], axis=1)

    directions = ((0, sector_up, sector_down), (1, axial_up, axial_down))
    diagonal = heat + jnp.diagonal(assembled, axis1=3, axis2=4)
    for which, upper, lower in directions:
        own = link_table[which, ..., 0]
        far = link_table[which, ..., 1]
        diagonal = diagonal + spread_flat(own, gains[which]) + lower(spread_flat(far, gains[which]))

    def apply(field):
        result = heat[..., None] * field + jnp.einsum('xypij,xypjr->xypir', assembled, field, precision=highest)
        for which, upper, lower in directions:
            own = link_table[which, ..., 0]
            far = link_table[which, ..., 1]
            flux = gains[which][..., None] * (pick_rows(field, own) - pick_rows(upper(field), far))
            result = result + spread_field(own, flux) - lower(spread_field(far, flux))
        return result

    source_vector = loads.reshape(N_SECTOR, N_AXIAL, PATCH_DEV, BN, HEATING_SCENARIO)
    current_estimate = jnp.zeros_like(source_vector)
    remaining_imbalance = source_vector
    precond = remaining_imbalance / diagonal[..., None]
    update_vector = precond
    norm_now = jnp.sum(remaining_imbalance * precond, axis=(0, 1, 2, 3))
    for sweep in range(ITERS):
        image = apply(update_vector)
        update_factor = norm_now / jnp.sum(update_vector * image, axis=(0, 1, 2, 3))
        current_estimate = current_estimate + update_factor * update_vector
        remaining_imbalance = remaining_imbalance - update_factor * image
        precond = remaining_imbalance / diagonal[..., None]
        norm_next = jnp.sum(remaining_imbalance * precond, axis=(0, 1, 2, 3))
        update_vector = precond + (norm_next / norm_now) * update_vector
        norm_now = norm_next
    return current_estimate.reshape(THERMAL_POINTS, HEATING_SCENARIO), remaining_imbalance.reshape(THERMAL_POINTS, HEATING_SCENARIO)
```

```python
import functools
import jax
import jax.numpy as jnp
from jax import lax
from jax.experimental import pallas as pl
from jax.experimental.pallas import tpu as pltpu
from jax.sharding import PartitionSpec as P

AXES = ("sector", "axial")
F32 = jnp.float32
BF16 = jnp.bfloat16
VMEM = pl.BlockSpec(memory_space=pltpu.VMEM)
SMEM = pl.BlockSpec(memory_space=pltpu.SMEM)
NT = (((1,), (1,)), ((), ()))
CHUNK = 8


def struct(*shape, dtype=F32):
    return jax.ShapeDtypeStruct(shape, dtype)


def iota(shape, dim):
    return lax.broadcasted_iota(jnp.int32, shape, dim)


def split(value):
    high = value.astype(BF16)
    return high, (value - high.astype(F32)).astype(BF16)


def dot(left, right, dims=(((1,), (0,)), ((), ()))):
    return lax.dot_general(left, right, dims, preferred_element_type=F32)


def pack_kernel(slots_each, owners, patches, counts, kbb, inner, nodes, payload, meta, blocks, node_rows, tally):
    step = pl.program_id(0)
    chunk, bn, _ = inner.shape
    half, quarter = bn // 2, bn // 4
    elems = kbb.shape[2]

    @pl.when(step == 0)
    def _():
        for i in range(half):
            blocks[pl.ds(i, elems, stride=half), :] = jnp.concatenate([kbb[i], kbb[i + half]], axis=0).T
        node_rows[...] = nodes[...].T
        meta[...] = jnp.zeros_like(meta)

        def clear(i, carry):
            tally[i] = 0
            return carry

        lax.fori_loop(0, meta.shape[0] // slots_each, clear, 0)

    row_id = iota((bn, bn), 0)
    col_id = iota((bn, bn), 1)
    lower = (row_id > col_id)[:half, :half]
    upper = (row_id < col_id)[:half, :half]
    lane = iota((1, 128), 1)
    for e in range(chunk):
        index = step * chunk + e
        both = blocks[pl.ds(pl.multiple_of(index * half, half), half), :]
        block = jnp.concatenate([both[:, :bn], both[:, bn:]], axis=0)
        coupling = inner[e]
        block = block - dot(coupling, coupling, NT)
        high, low = split(block)
        pick = (node_rows[pl.ds(index, 1), :] == row_id).astype(F32).astype(BF16)
        left = dot(jnp.concatenate([pick, pick], axis=1), jnp.concatenate([high, low], axis=0))
        high, low = split(left)
        placed = dot(high, pick, NT) + dot(low, pick, NT)
        triangles = jnp.where(lower, placed[:half, :half], jnp.where(upper, placed[half:, half:], 0.0))
        packed = jnp.concatenate([triangles, placed[:half, half:]], axis=1)
        packed = jnp.concatenate([packed[:quarter], packed[quarter:]], axis=1)
        diag = jnp.sum(jnp.where(row_id == col_id, placed, 0.0), axis=0, keepdims=True)
        owner = owners[index]
        rank = tally[owner]
        tally[owner] = rank + 1
        slot = owner * slots_each + rank
        payload[pl.ds(pl.multiple_of(slot * quarter, quarter), quarter), :] = packed
        tag = jnp.where(index < counts[0], patches[index] + 1, 0).astype(F32)
        meta[pl.ds(slot, 1), :] = jnp.where(lane < bn, jnp.concatenate([diag, diag], axis=1), jnp.where(lane == bn, tag, 0.0))


def pack_call(devices, owners, patches, counts, kbb, inner, nodes):
    elems, bn, ni = inner.shape
    slots_each = 2 * elems // devices
    slots = devices * slots_each
    whole = lambda *shape: pl.BlockSpec(shape, lambda i: (0,) * len(shape))
    return pl.pallas_call(
        functools.partial(pack_kernel, slots_each),
        grid=(elems // CHUNK,),
        in_specs=[
            SMEM,
            SMEM,
            SMEM,
            whole(bn, bn, elems),
            pl.BlockSpec((CHUNK, bn, ni), lambda i: (i, 0, 0)),
            whole(bn, elems),
        ],
        out_specs=[whole(slots * bn // 4, 128), whole(slots, 128)],
        out_shape=[struct(slots * bn // 4, 128), struct(slots, 128)],
        scratch_shapes=[
            pltpu.VMEM((elems * bn // 2, 128), F32),
            pltpu.VMEM((elems, bn), jnp.int32),
            pltpu.SMEM((devices,), jnp.int32),
        ],
        name="pack",
    )(owners, patches, counts, kbb, inner, nodes)


def send_values(picked, gains, field, sends):
    count = sends[0].shape[0]
    for which, send in enumerate(sends):

        def one(k, carry):
            send[k] = gains[which * count + k] * field[picked[which * count + k]]
            return carry

        lax.fori_loop(0, count, one, 0, unroll=2)


def take_values(placed, received, result):
    count = received[0].shape[0]
    for which, got in enumerate(received):

        def one(k, carry):
            patch = placed[which * count + k]
            result[patch] = result[patch] - got[k]
            return carry

        lax.fori_loop(0, count, one, 0, unroll=2)


def diagonal_kernel(tags, picked, meta, capacity, gain_rows, loads, inverse, gains, field, s0, s1, s2, s3, total):
    patch_dev, bn = capacity.shape
    total[pl.ds(0, patch_dev), :] = jnp.concatenate([capacity[...], capacity[...]], axis=1)

    def add(i, carry):
        patch = tags[i]
        total[pl.ds(patch, 1), :] = total[pl.ds(patch, 1), :] + meta[pl.ds(i, 1), :]
        return carry

    lax.fori_loop(0, meta.shape[0], add, 0, unroll=4)

    def link(i, carry):
        patch = picked[i]
        total[pl.ds(patch, 1), :] = total[pl.ds(patch, 1), :] + gain_rows[pl.ds(i, 1), :]
        return carry

    lax.fori_loop(0, gain_rows.shape[0], link, 0, unroll=4)
    columns = (1.0 / total[pl.ds(0, patch_dev), :][:, :bn]).T
    for p in range(patch_dev):
        column = jnp.broadcast_to(columns[:, p : p + 1], (bn, 128))
        inverse[p] = column
        field[p] = column * loads[p]
    columns = gain_rows[...][:, :bn].T
    for k in range(gain_rows.shape[0]):
        gains[k] = jnp.broadcast_to(columns[:, k : k + 1], (bn, 128))
    send_values(picked, gains, field, (s0, s1, s2, s3))


def times_blocks(blocks, value):
    high, low = split(value)
    return dot(blocks, jnp.concatenate([high, high, low], axis=0))


def folded(value):
    rows = value.shape[0]
    total = value[0:8]
    for i in range(8, rows, 8):
        total = total + value[i : i + 8]
    return total


def publish(partial, sums):
    rows = [jnp.sum(s[...], axis=0, keepdims=True) for s in sums]
    block = jnp.concatenate(rows + [jnp.zeros((8 - len(rows), 128), F32)], axis=0)

    def one(d, carry):
        partial[d] = block
        return carry

    lax.fori_loop(0, partial.shape[0], one, 0)


def gathered(received):
    return jnp.sum(received[...], axis=0)


def assemble_kernel(
    tags, picked, placed, payload, loads, field, inverse, gains, g0, g1, g2, g3,
    blocks, image, after, s0, s1, s2, s3, partial, packed, sum0, sum1,
):
    patch_dev, bn, _ = loads.shape
    half, quarter = bn // 2, bn // 4
    packed[...] = jnp.zeros_like(packed)

    def add(i, carry):
        patch = tags[i]
        packed[patch] = packed[patch] + payload[pl.ds(pl.multiple_of(i * quarter, quarter), quarter), :]
        return carry

    lax.fori_loop(0, tags.shape[0], add, 0, unroll=4)
    row_id = iota((half, bn), 0)
    col_id = iota((half, bn), 1)

    def build(p, carry):
        both = packed[p]
        rows = jnp.concatenate([both[:, :bn], both[:, bn:]], axis=0)
        top = jnp.where((col_id >= half) | (row_id > col_id), rows, 0.0)
        second = jnp.where((col_id < half) & (row_id < col_id), rows, 0.0)
        second = jnp.concatenate([jnp.zeros((half, half), F32), second[:, :half]], axis=1)
        whole = jnp.concatenate([top, second], axis=0)
        high, low = split(whole + whole.T)
        three = jnp.concatenate([high, low, high], axis=1)
        blocks[p] = three
        image[p] = loads[p] + times_blocks(three, field[p])
        return carry

    lax.fori_loop(0, patch_dev, build, 0, unroll=2)
    take_values(placed, (g0, g1, g2, g3), image)
    sum0[...] = jnp.zeros_like(sum0)
    sum1[...] = jnp.zeros_like(sum1)

    def finish(p, carry):
        here, value = image[p], field[p]
        after[p] = inverse[p] * here
        sum0[...] += folded(loads[p] * value)
        sum1[...] += folded(here * value)
        return carry

    lax.fori_loop(0, patch_dev, finish, 0, unroll=2)
    send_values(picked, gains, after, (s0, s1, s2, s3))
    publish(partial, (sum0, sum1))


def local_kernel(blocks, field, result):
    def one(p, carry):
        result[p] = times_blocks(blocks[p], field[p])
        return carry

    lax.fori_loop(0, field.shape[0], one, 0, unroll=2)


def second_kernel(picked, placed, local, image, inverse, gains, g0, g1, g2, g3, result, after, s0, s1, s2, s3):
    def one(p, carry):
        result[p] = image[p] + local[p]
        return carry

    lax.fori_loop(0, local.shape[0], one, 0, unroll=2)
    take_values(placed, (g0, g1, g2, g3), result)

    def scale(p, carry):
        after[p] = inverse[p] * result[p]
        return carry

    lax.fori_loop(0, local.shape[0], scale, 0, unroll=2)
    send_values(picked, gains, after, (s0, s1, s2, s3))


def first_step_kernel(sums, loads, field, image, second, inverse, left, left_image, left_scaled, partial, a0, a1, a2):
    first = gathered(sums)
    alpha = first[0:1] / first[1:2]
    a0[...] = jnp.zeros_like(a0)
    a1[...] = jnp.zeros_like(a1)
    a2[...] = jnp.zeros_like(a2)

    def one(p, carry):
        r = loads[p] - alpha * image[p]
        w = image[p] - alpha * second[p]
        u = inverse[p] * r
        left[p] = r
        left_image[p] = w
        left_scaled[p] = u
        a0[...] += folded(r * u)
        a1[...] += folded(u * w)
        a2[...] += folded(u * image[p] + field[p] * w)
        return carry

    lax.fori_loop(0, loads.shape[0], one, 0, unroll=2)
    publish(partial, (a0, a1, a2))


def second_step_kernel(
    sums0, sums1, placed, local, g0, g1, g2, g3, field, image, second, r1, w1, u1, inverse,
    r2_out, w2_out, s1_out, p1_out, u2_out, partial, third, a0, a1, a2,
):
    patch_dev = local.shape[0]
    first, then = gathered(sums0), gathered(sums1)
    alpha0 = first[0:1] / first[1:2]
    beta1 = then[0:1] / first[0:1]
    alpha1 = then[0:1] / (then[1:2] + beta1 * (then[2:3] + beta1 * first[1:2]))

    def start(p, carry):
        third[p] = second[p] + local[p]
        return carry

    lax.fori_loop(0, patch_dev, start, 0, unroll=2)
    take_values(placed, (g0, g1, g2, g3), third)
    a0[...] = jnp.zeros_like(a0)
    a1[...] = jnp.zeros_like(a1)
    a2[...] = jnp.zeros_like(a2)

    def one(p, carry):
        n0, w = second[p], w1[p]
        s1 = w + beta1 * image[p]
        z1 = (n0 - alpha0 * third[p]) + beta1 * n0
        r2 = r1[p] - alpha1 * s1
        w2 = w - alpha1 * z1
        u2 = inverse[p] * r2
        p1 = u1[p] + beta1 * field[p]
        r2_out[p] = r2
        w2_out[p] = w2
        s1_out[p] = s1
        p1_out[p] = p1
        u2_out[p] = u2
        a0[...] += folded(r2 * u2)
        a1[...] += folded(u2 * w2)
        a2[...] += folded(u2 * s1 + p1 * w2)
        return carry

    lax.fori_loop(0, patch_dev, one, 0)
    publish(partial, (a0, a1, a2))


def last_kernel(sums0, sums1, sums2, field, r2, w2, s1, p1, u2, estimate, left):
    first, then, last = gathered(sums0), gathered(sums1), gathered(sums2)
    alpha0 = first[0:1] / first[1:2]
    beta1 = then[0:1] / first[0:1]
    curve1 = then[1:2] + beta1 * (then[2:3] + beta1 * first[1:2])
    alpha1 = then[0:1] / curve1
    beta2 = last[0:1] / then[0:1]
    alpha2 = last[0:1] / (last[1:2] + beta2 * (last[2:3] + beta2 * curve1))

    def one(p, carry):
        direction = u2[p] + beta2 * p1[p]
        estimate[p] = alpha0 * field[p] + alpha1 * p1[p] + alpha2 * direction
        left[p] = r2[p] - alpha2 * (w2[p] + beta2 * s1[p])
        return carry

    lax.fori_loop(0, field.shape[0], one, 0, unroll=2)


def call(kernel, name, ins, outs, scratch=(), flops=0):
    ints = lambda a: a.ndim == 1 and a.dtype == jnp.int32
    moved = sum(a.size * a.dtype.itemsize for a in ins) + sum(s.size * s.dtype.itemsize for s in outs)
    return pl.pallas_call(
        kernel,
        in_specs=[SMEM if ints(a) else VMEM for a in ins],
        out_specs=[VMEM] * len(outs),
        out_shape=list(outs),
        scratch_shapes=list(scratch),
        cost_estimate=pl.CostEstimate(flops=flops, bytes_accessed=moved, transcendentals=0),
        name=name,
    )(*ins)


def everywhere(partial):
    return lax.all_to_all(partial, AXES, split_axis=0, concat_axis=0, tiled=True)


def onward(value, axis, wrap):
    n = lax.axis_size(axis)
    return lax.ppermute(value, axis, [(i, (i + 1) % n) for i in range(n) if wrap or i + 1 < n])


def back(value, axis, wrap):
    n = lax.axis_size(axis)
    return lax.ppermute(value, axis, [((i + 1) % n, i) for i in range(n) if wrap or i + 1 < n])


def exchange(s0, s1, s2, s3):
    return (
        onward(s0, "sector", True),
        back(s1, "sector", True),
        onward(s2, "axial", False),
        back(s3, "axial", False),
    )


def shards(kbb, interior, node_lists, owners, patch_ids, counts, capacity, links, conduct, loads):
    elems, bn = node_lists.shape
    devices = lax.axis_size("sector") * lax.axis_size("axial")
    points, cases = loads.shape
    patch_dev = points // bn
    count = conduct.shape[1]

    sent = jnp.concatenate(
        [conduct, links[:, :, 1:].astype(F32), jnp.zeros((2, count, 127 - bn), F32)], axis=2
    )
    from_sector = onward(sent[0], "sector", True)
    from_axial = onward(sent[1], "axial", False)
    own, far = links[:, :, 0], links[:, :, 1]
    far_sector = from_sector[:, bn].astype(jnp.int32)
    far_axial = from_axial[:, bn].astype(jnp.int32)
    picked = jnp.concatenate([own[0], far_sector, own[1], far_axial])
    placed = jnp.concatenate([far_sector, own[0], far_axial, own[1]])
    gain_rows = jnp.concatenate([sent[0], from_sector, sent[1], from_axial])

    payload, meta = pack_call(
        devices, owners.reshape(elems), patch_ids, counts,
        kbb.transpose(1, 2, 0), interior.transpose(0, 2, 1), node_lists.T,
    )
    slots = meta.shape[0]
    meta = everywhere(meta.reshape(devices, slots // devices, 128)).reshape(slots, 128)
    tags = meta[:, bn].astype(jnp.int32)
    tags = jnp.where(tags > 0, tags - 1, patch_dev)
    payload = everywhere(payload.reshape(devices, -1, 128)).reshape(slots * bn // 4, 128)

    loads = loads.reshape(patch_dev, bn, cases)
    vec = struct(patch_dev, bn, cases)
    buf = struct(count, bn, cases)
    total = struct(devices, 8, cases)
    acc = pltpu.VMEM((8, cases), F32)
    inverse, gains, field, *sends = call(
        diagonal_kernel, "diagonal",
        (tags, picked, meta, capacity.reshape(patch_dev, bn), gain_rows, loads),
        (vec, struct(4 * count, bn, cases), vec, buf, buf, buf, buf),
        (pltpu.VMEM((patch_dev + 8, 128), F32),),
    )
    got = exchange(*sends)
    blocks, image, after, *rest = call(
        assemble_kernel, "assemble",
        (tags, picked, placed, payload, loads, field, inverse, gains, *got),
        (struct(patch_dev, bn, 3 * bn, dtype=BF16), vec, vec, buf, buf, buf, buf, total),
        (pltpu.VMEM((patch_dev + 1, bn // 4, 128), F32), acc, acc),
    )
    *sends, partial = rest
    got = exchange(*sends)
    sums0 = everywhere(partial)
    (local,) = call(local_kernel, "local", (blocks, after), (vec,))
    second, after, *sends = call(
        second_kernel, "second",
        (picked, placed, local, image, inverse, gains, *got),
        (vec, vec, buf, buf, buf, buf),
    )
    got = exchange(*sends)
    r1, w1, u1, partial = call(
        first_step_kernel, "first_step",
        (sums0, loads, field, image, second, inverse), (vec, vec, vec, total), (acc, acc, acc),
    )
    sums1 = everywhere(partial)
    (local,) = call(local_kernel, "local", (blocks, after), (vec,))
    r2, w2, s1, p1, u2, partial = call(
        second_step_kernel, "second_step",
        (sums0, sums1, placed, local, *got, field, image, second, r1, w1, u1, inverse),
        (vec, vec, vec, vec, vec, total),
        (pltpu.VMEM((patch_dev, bn, cases), F32), acc, acc, acc),
    )
    sums2 = everywhere(partial)
    estimate, left = call(
        last_kernel, "last", (sums0, sums1, sums2, field, r2, w2, s1, p1, u2), (vec, vec)
    )
    return estimate.reshape(points, cases), left.reshape(points, cases)


def solution(mesh):
    wide = P(AXES, None)
    deep = P(AXES, None, None)
    return jax.shard_map(
        shards,
        mesh=mesh,
        in_specs=(
            deep, deep, wide, wide, P(AXES), P(AXES), P(AXES),
            P(None, AXES, None), P(None, AXES, None), wide,
        ),
        out_specs=(wide, wide),
        check_vma=False,
    )
```

```python
import functools
import jax
import jax.numpy as jnp
from jax import lax
from jax.experimental import pallas as pl
from jax.experimental.pallas import tpu as pltpu
from jax.sharding import PartitionSpec as P

AXES = ("sector", "axial")
F32 = jnp.float32
BF16 = jnp.bfloat16
VMEM = pl.BlockSpec(memory_space=pltpu.VMEM)
HBM = pl.BlockSpec(memory_space=pltpu.HBM)
SMEM = pl.BlockSpec(memory_space=pltpu.SMEM)
NT = (((1,), (1,)), ((), ()))
CHUNK = 16
GROUP = 16
LIMIT = 14 << 20
WIDE = 60 << 20


def struct(*shape, dtype=F32):
    return jax.ShapeDtypeStruct(shape, dtype)


def iota(shape, dim):
    return lax.broadcasted_iota(jnp.int32, shape, dim)


def split(value):
    high = value.astype(BF16)
    return high, (value - high.astype(F32)).astype(BF16)


def dot(left, right, dims=(((1,), (0,)), ((), ()))):
    return lax.dot_general(left, right, dims, preferred_element_type=F32)


def pack_kernel(slots_each, owners, patches, counts, kbb, inner, nodes, payload, meta, blocks, node_rows, tally):
    step = pl.program_id(0)
    chunk, bn, _ = inner.shape
    half, quarter = bn // 2, bn // 4
    elems = kbb.shape[2]

    @pl.when(step == 0)
    def _():
        for i in range(half):
            blocks[pl.ds(i, elems, stride=half), :] = jnp.concatenate([kbb[i], kbb[i + half]], axis=0).T
        node_rows[...] = nodes[...].T
        meta[...] = jnp.zeros_like(meta)

        def clear(i, carry):
            tally[i] = 0
            return carry

        lax.fori_loop(0, meta.shape[0] // slots_each, clear, 0)

    row_id = iota((bn, bn), 0)
    col_id = iota((bn, bn), 1)
    lower = (row_id > col_id)[:half, :half]
    upper = (row_id < col_id)[:half, :half]
    lane = iota((1, 128), 1)
    for first in range(0, chunk, GROUP):
        group = range(GROUP)
        where = [step * chunk + first + e for e in group]
        grams = [dot(inner[first + e], inner[first + e], NT) for e in group]
        picks = [(node_rows[pl.ds(i, 1), :] == row_id).astype(F32).astype(BF16) for i in where]
        pairs = []
        for e in group:
            both = blocks[pl.ds(pl.multiple_of(where[e] * half, half), half), :]
            block = jnp.concatenate([both[:, :bn], both[:, bn:]], axis=0)
            pairs.append(split(block - grams[e]))
        lefts = [dot(jnp.concatenate([picks[e], picks[e]], axis=1), jnp.concatenate(pairs[e], axis=0)) for e in group]
        pairs = [split(left) for left in lefts]
        placed_all = [dot(pairs[e][0], picks[e], NT) + dot(pairs[e][1], picks[e], NT) for e in group]
        for e in group:
            placed, index = placed_all[e], where[e]
            triangles = jnp.where(lower, placed[:half, :half], jnp.where(upper, placed[half:, half:], 0.0))
            packed = jnp.concatenate([triangles, placed[:half, half:]], axis=1)
            packed = jnp.concatenate([packed[:quarter], packed[quarter:]], axis=1)
            diag = jnp.sum(jnp.where(row_id == col_id, placed, 0.0), axis=0, keepdims=True)
            owner = owners[index]
            rank = tally[owner]
            tally[owner] = rank + 1
            slot = owner * slots_each + rank
            payload[pl.ds(pl.multiple_of(slot * quarter, quarter), quarter), :] = packed
            tag = jnp.where(index < counts[0], patches[index] + 1, 0).astype(F32)
            meta[pl.ds(slot, 1), :] = jnp.where(
                lane < bn, jnp.concatenate([diag, diag], axis=1), jnp.where(lane == bn, tag, 0.0)
            )


def pack_call(devices, owners, patches, counts, kbb, inner, nodes):
    elems, bn, ni = inner.shape
    slots_each = 2 * elems // devices
    slots = devices * slots_each
    whole = lambda *shape: pl.BlockSpec(shape, lambda i: (0,) * len(shape))
    return pl.pallas_call(
        functools.partial(pack_kernel, slots_each),
        grid=(elems // CHUNK,),
        in_specs=[
            SMEM,
            SMEM,
            SMEM,
            whole(bn, bn, elems),
            pl.BlockSpec((CHUNK, bn, ni), lambda i: (i, 0, 0)),
            whole(bn, elems),
        ],
        out_specs=[whole(slots * bn // 4, 128), whole(slots, 128)],
        out_shape=[struct(slots * bn // 4, 128), struct(slots, 128)],
        scratch_shapes=[
            pltpu.VMEM((elems * bn // 2, 128), F32),
            pltpu.VMEM((elems, bn), jnp.int32),
            pltpu.SMEM((devices,), jnp.int32),
        ],
        compiler_params=pltpu.CompilerParams(vmem_limit_bytes=WIDE),
        name="pack",
    )(owners, patches, counts, kbb, inner, nodes)


def send_values(picked, gains, field, sends):
    count = sends[0].shape[0]
    for which, send in enumerate(sends):

        def one(k, carry):
            send[k] = gains[which * count + k] * field[picked[which * count + k]]
            return carry

        lax.fori_loop(0, count, one, 0, unroll=4)


def take_values(placed, received, result):
    count = received[0].shape[0]
    for which, got in enumerate(received):

        def one(k, carry):
            patch = placed[which * count + k]
            result[patch] = result[patch] - got[k]
            return carry

        lax.fori_loop(0, count, one, 0, unroll=4)


def gather_kernel(index0, index1, loads, gains, out0, out1, sems):
    bn = loads.shape[1]
    count = out0.shape[0]
    copies = []
    for which, (index, out) in enumerate(((index0, out0), (index1, out1))):
        for k in range(count):
            copies.append(pltpu.make_async_copy(loads.at[index[k]], out.at[k, pl.ds(0, bn)], sems.at[which]))
    for copy in copies:
        copy.start()
    if out0.shape[1] > bn:
        for which, out in enumerate((out0, out1)):
            rows = jnp.concatenate([gains[which], gains[which]], axis=1)
            for k in range(count):
                out[k, pl.ds(bn, 8), :] = jnp.broadcast_to(rows[k : k + 1], (8, 128))
    for copy in copies:
        copy.wait()


def gather_call(index0, index1, loads, gains, extra):
    out = struct(index0.shape[0], loads.shape[1] + extra, loads.shape[2])
    return pl.pallas_call(
        gather_kernel,
        in_specs=[SMEM, SMEM, pl.BlockSpec(memory_space=pl.ANY), VMEM],
        out_specs=[VMEM, VMEM],
        out_shape=[out, out],
        scratch_shapes=[pltpu.SemaphoreType.DMA((2,))],
        compiler_params=pltpu.CompilerParams(vmem_limit_bytes=WIDE),
        name="gather",
    )(index0, index1, loads, gains)


def diagonal_kernel(
    tags, picked, meta, capacity, conduct, g0, g2, loads, inverse, field, gains, t0, t1, t2, t3, total, gain_rows,
):
    patch_dev, bn = capacity.shape
    count = conduct.shape[1]
    for which, got in enumerate((g0, g2)):
        gain_rows[pl.ds(2 * which * count, count), :] = jnp.concatenate([conduct[which], conduct[which]], axis=1)
        for k in range(count):
            gain_rows[pl.ds((2 * which + 1) * count + k, 1), :] = got[k, pl.ds(bn, 1), :]
    total[pl.ds(0, patch_dev), :] = jnp.concatenate([capacity[...], capacity[...]], axis=1)

    def add(i, carry):
        patch = tags[i]
        total[pl.ds(patch, 1), :] = total[pl.ds(patch, 1), :] + meta[pl.ds(i, 1), :]
        return carry

    lax.fori_loop(0, meta.shape[0], add, 0, unroll=4)

    def link(i, carry):
        patch = picked[i]
        total[pl.ds(patch, 1), :] = total[pl.ds(patch, 1), :] + gain_rows[pl.ds(i, 1), :]
        return carry

    lax.fori_loop(0, gain_rows.shape[0], link, 0, unroll=4)
    over = 1.0 / total[pl.ds(0, patch_dev), :]
    total[pl.ds(0, patch_dev), :] = over
    columns = over[:, :bn].T
    for p in range(patch_dev):
        column = jnp.broadcast_to(columns[:, p : p + 1], (bn, 128))
        inverse[p] = column
        field[p] = column * loads[p]
    for which, rows in enumerate((t0, t1, t2, t3)):
        for k in range(count):
            i = which * count + k
            rows[pl.ds(k, 1), :] = total[pl.ds(picked[i], 1), :] * gain_rows[pl.ds(i, 1), :]
    columns = gain_rows[...][:, :bn].T
    for k in range(gain_rows.shape[0]):
        gains[k] = jnp.broadcast_to(columns[:, k : k + 1], (bn, 128))


def edges_kernel(placed, loads, t0, t1, t2, t3, g0, g1, g2, g3, image):
    bn = loads.shape[1]
    count = t0.shape[0]
    image[...] = loads[...]
    for which, (rows, got) in enumerate(((t0, g0), (t1, g1), (t2, g2), (t3, g3))):
        columns = rows[...][:, :bn].T
        for k in range(count):
            patch = placed[which * count + k]
            image[patch] = image[patch] - jnp.broadcast_to(columns[:, k : k + 1], (bn, 128)) * got[k, pl.ds(0, bn), :]


def stacked(value):
    high, low = split(value)
    return jnp.concatenate([high, high, low], axis=0)


def folded(value):
    total = value[0:8]
    for i in range(8, value.shape[0], 8):
        total = total + value[i : i + 8]
    return total


def publish(partial, sums):
    rows = [jnp.sum(s, axis=0, keepdims=True) for s in sums]
    block = jnp.concatenate(rows + [jnp.zeros((8 - len(rows), 128), F32)], axis=0)
    for d in range(partial.shape[0]):
        partial[d] = block


def gathered(received):
    return jnp.sum(received[...], axis=0)


def zeros(n):
    return (jnp.zeros((8, 128), F32),) * n


def assemble_kernel(
    tags, picked, payload, start_in, field_in, inverse_in, loads_in, gains_in,
    image, blocks, after, s0, s1, s2, s3, partial, field, inverse, loads, gains, packed, sems,
):
    patch_dev, bn, _ = image.shape
    half, quarter = bn // 2, bn // 4
    banks = packed.shape[0]
    slots = tags.shape[0]
    pairs = ((start_in, image), (field_in, field), (inverse_in, inverse), (loads_in, loads), (gains_in, gains))
    fetches = [pltpu.make_async_copy(src, dst, sems.at[i]) for i, (src, dst) in enumerate(pairs)]
    for copy in fetches:
        copy.start()
    packed[...] = jnp.zeros_like(packed)

    def add(j, carry):
        for bank in range(banks):
            i = j * banks + bank
            patch = tags[i]
            packed[bank, patch] = packed[bank, patch] + payload[pl.ds(pl.multiple_of(i * quarter, quarter), quarter), :]
        return carry

    lax.fori_loop(0, slots // banks, add, 0, unroll=2)
    fetches[0].wait()
    fetches[1].wait()
    row_id = iota((half, bn), 0)
    col_id = iota((half, bn), 1)
    kept = (col_id >= half) | (row_id > col_id)
    moved = (col_id < half) & (row_id < col_id)

    def build(j, carry):
        group = [j * GROUP + g for g in range(GROUP)]
        wholes = []
        for p in group:
            both = packed[0, p]
            for bank in range(1, banks):
                both = both + packed[bank, p]
            rows = jnp.concatenate([both[:, :bn], both[:, bn:]], axis=0)
            second = jnp.where(moved, rows, 0.0)[:, :half]
            second = jnp.concatenate([jnp.zeros((half, half), F32), second], axis=1)
            wholes.append(jnp.concatenate([jnp.where(kept, rows, 0.0), second], axis=0))
        wholes = [w + w.T for w in wholes]
        threes = []
        for w in wholes:
            high, low = split(w)
            threes.append(jnp.concatenate([high, low, high], axis=1))
        for p, three in zip(group, threes):
            blocks[p] = three
        products = [dot(three, stacked(field[p])) for p, three in zip(group, threes)]
        for p, product in zip(group, products):
            image[p] = image[p] + product
        return carry

    lax.fori_loop(0, patch_dev // GROUP, build, 0)
    for copy in fetches[2:]:
        copy.wait()

    def finish(p, carry):
        here, value = image[p], field[p]
        after[p] = inverse[p] * here
        return carry[0] + folded(loads[p] * value), carry[1] + folded(here * value)

    sums = lax.fori_loop(0, patch_dev, finish, zeros(2), unroll=2)
    send_values(picked, gains, after, (s0, s1, s2, s3))
    publish(partial, sums)


def local_kernel(blocks, field, base, result):
    def some(j, carry):
        group = [j * GROUP + g for g in range(GROUP)]
        products = [dot(blocks[p], stacked(field[p])) for p in group]
        for p, product in zip(group, products):
            result[p] = base[p] + product
        return carry

    lax.fori_loop(0, field.shape[0] // GROUP, some, 0)


def second_kernel(picked, placed, inverse, gains, g0, g1, g2, g3, base, result, after, s0, s1, s2, s3):
    take_values(placed, (g0, g1, g2, g3), result)

    def scale(p, carry):
        after[p] = inverse[p] * result[p]
        return carry

    lax.fori_loop(0, inverse.shape[0], scale, 0, unroll=2)
    send_values(picked, gains, after, (s0, s1, s2, s3))


def first_step_kernel(sums, loads, field, image, second, inverse, left, left_image, partial):
    first = gathered(sums)
    alpha = first[0:1] / first[1:2]

    def one(p, carry):
        r = loads[p] - alpha * image[p]
        w = image[p] - alpha * second[p]
        u = inverse[p] * r
        left[p] = r
        left_image[p] = w
        return (
            carry[0] + folded(r * u),
            carry[1] + folded(u * w),
            carry[2] + folded(u * image[p] + field[p] * w),
        )

    publish(partial, lax.fori_loop(0, loads.shape[0], one, zeros(3), unroll=2))


def second_step_kernel(
    sums0, sums1, placed, g0, g1, g2, g3, field, image, second, r1, w1, inverse, base,
    third, r2_out, w2_out, partial,
):
    first, then = gathered(sums0), gathered(sums1)
    alpha0 = first[0:1] / first[1:2]
    beta1 = then[0:1] / first[0:1]
    alpha1 = then[0:1] / (then[1:2] + beta1 * (then[2:3] + beta1 * first[1:2]))
    take_values(placed, (g0, g1, g2, g3), third)

    def one(p, carry):
        n0, w, r = second[p], w1[p], r1[p]
        s1 = w + beta1 * image[p]
        z1 = (n0 - alpha0 * third[p]) + beta1 * n0
        r2 = r - alpha1 * s1
        w2 = w - alpha1 * z1
        u2 = inverse[p] * r2
        p1 = inverse[p] * r + beta1 * field[p]
        r2_out[p] = r2
        w2_out[p] = w2
        return (
            carry[0] + folded(r2 * u2),
            carry[1] + folded(u2 * w2),
            carry[2] + folded(u2 * s1 + p1 * w2),
        )

    publish(partial, lax.fori_loop(0, field.shape[0], one, zeros(3)))


def last_kernel(sums0, sums1, sums2, field, image, inverse, r1, w1, r2, w2, estimate, left):
    first, then, last = gathered(sums0), gathered(sums1), gathered(sums2)
    alpha0 = first[0:1] / first[1:2]
    beta1 = then[0:1] / first[0:1]
    curve1 = then[1:2] + beta1 * (then[2:3] + beta1 * first[1:2])
    alpha1 = then[0:1] / curve1
    beta2 = last[0:1] / then[0:1]
    alpha2 = last[0:1] / (last[1:2] + beta2 * (last[2:3] + beta2 * curve1))

    def one(p, carry):
        p1 = inverse[p] * r1[p] + beta1 * field[p]
        direction = inverse[p] * r2[p] + beta2 * p1
        estimate[p] = alpha0 * field[p] + alpha1 * p1 + alpha2 * direction
        left[p] = r2[p] - alpha2 * (w2[p] + beta2 * (w1[p] + beta1 * image[p]))
        return carry

    lax.fori_loop(0, field.shape[0], one, 0, unroll=2)


def call(kernel, name, ins, outs, scratch=(), flops=0, alias=None, limit=None, far=()):
    ints = lambda a: a.ndim == 1 and a.dtype == jnp.int32
    moved = sum(a.size * a.dtype.itemsize for a in ins) + sum(s.size * s.dtype.itemsize for s in outs)
    return pl.pallas_call(
        kernel,
        in_specs=[SMEM if ints(a) else HBM if i in far else VMEM for i, a in enumerate(ins)],
        out_specs=[VMEM] * len(outs),
        out_shape=list(outs),
        scratch_shapes=list(scratch),
        input_output_aliases=alias or {},
        cost_estimate=pl.CostEstimate(flops=flops, bytes_accessed=moved, transcendentals=0),
        compiler_params=pltpu.CompilerParams(vmem_limit_bytes=limit or LIMIT),
        name=name,
    )(*[pltpu.with_memory_space_constraint(a, pltpu.HBM) if i in far else a for i, a in enumerate(ins)])


def everywhere(partial):
    return lax.all_to_all(partial, AXES, split_axis=0, concat_axis=0, tiled=True)


def onward(value, axis, wrap):
    n = lax.axis_size(axis)
    return lax.ppermute(value, axis, [(i, (i + 1) % n) for i in range(n) if wrap or i + 1 < n])


def back(value, axis, wrap):
    n = lax.axis_size(axis)
    return lax.ppermute(value, axis, [((i + 1) % n, i) for i in range(n) if wrap or i + 1 < n])


def exchange(s0, s1, s2, s3):
    return (
        onward(s0, "sector", True),
        back(s1, "sector", True),
        onward(s2, "axial", False),
        back(s3, "axial", False),
    )


def shards(kbb, interior, node_lists, owners, patch_ids, counts, capacity, links, conduct, loads):
    elems, bn = node_lists.shape
    devices = lax.axis_size("sector") * lax.axis_size("axial")
    points, cases = loads.shape
    patch_dev = points // bn
    count = conduct.shape[1]
    loads = loads.reshape(patch_dev, bn, cases)
    vec = struct(patch_dev, bn, cases)
    buf = struct(count, bn, cases)
    total = struct(devices, 8, cases)

    table = links.transpose(0, 2, 1)
    own_sector, own_axial = table[0, 0], table[1, 0]
    s0, s2 = gather_call(own_sector, own_axial, loads, conduct, 8)
    owners, far_sector, far_axial, s0, s2 = lax.optimization_barrier((owners, table[0, 1], table[1, 1], s0, s2))
    g0, g2 = onward(s0, "sector", True), onward(s2, "axial", False)
    far_sector, far_axial = onward(far_sector, "sector", True), onward(far_axial, "axial", False)
    payload, meta = pack_call(
        devices, owners.reshape(elems), patch_ids, counts,
        kbb.transpose(1, 2, 0), interior.transpose(0, 2, 1), node_lists.T,
    )
    slots = meta.shape[0]
    payload, meta, g0, g2, far_sector, far_axial = lax.optimization_barrier(
        (payload, meta, g0, g2, far_sector, far_axial)
    )
    s1, s3 = gather_call(far_sector, far_axial, loads, conduct, 0)
    meta, s1, s3 = lax.optimization_barrier((meta, s1, s3))
    g1, g3 = back(s1, "sector", True), back(s3, "axial", False)
    meta = everywhere(meta.reshape(devices, slots // devices, 128)).reshape(slots, 128)
    payload, g1, g3 = lax.optimization_barrier((payload, g1, g3))
    payload = everywhere(payload.reshape(devices, -1, 128)).reshape(slots * bn // 4, 128)
    picked = jnp.concatenate([own_sector, far_sector, own_axial, far_axial])
    placed = jnp.concatenate([far_sector, own_sector, far_axial, own_axial])
    tags = meta[:, bn].astype(jnp.int32)
    tags = jnp.where(tags > 0, tags - 1, patch_dev)
    row = struct(count, 128)
    inverse, field, gains, *rows = call(
        diagonal_kernel, "diagonal",
        (tags, picked, meta, capacity.reshape(patch_dev, bn), conduct, g0, g2, loads),
        (vec, vec, struct(4 * count, bn, cases), row, row, row, row),
        (pltpu.VMEM((patch_dev + 8, 128), F32), pltpu.VMEM((4 * count, 128), F32)), limit=WIDE,
    )
    rows = exchange(*rows)
    (start,) = call(edges_kernel, "edges", (placed, loads, *rows, g0, g1, g2, g3), (vec,), limit=WIDE)
    image, blocks, after, *rest = call(
        assemble_kernel, "assemble",
        (tags, picked, payload, start, field, inverse, loads, gains),
        (vec, struct(patch_dev, bn, 3 * bn, dtype=BF16), vec, buf, buf, buf, buf, total,
         vec, vec, vec, struct(4 * count, bn, cases)),
        (pltpu.VMEM((4, patch_dev + 1, bn // 4, 128), F32), pltpu.SemaphoreType.DMA((5,))),
        far=(3, 4, 5, 6, 7),
    )
    *sends, partial, field, inverse, loads, gains = rest
    got = exchange(*sends)
    sums0 = everywhere(partial)
    after, sums0 = lax.optimization_barrier((after, sums0))
    (base,) = call(local_kernel, "local", (blocks, after, image), (vec,))
    second, after, *sends = call(
        second_kernel, "second", (picked, placed, inverse, gains, *got, base),
        (vec, vec, buf, buf, buf, buf), alias={8: 0},
    )
    got = exchange(*sends)
    r1, w1, partial = call(
        first_step_kernel, "first_step", (sums0, loads, field, image, second, inverse), (vec, vec, total)
    )
    sums1 = everywhere(partial)
    after, sums1 = lax.optimization_barrier((after, sums1))
    (base,) = call(local_kernel, "local", (blocks, after, second), (vec,))
    _, r2, w2, partial = call(
        second_step_kernel, "second_step",
        (sums0, sums1, placed, *got, field, image, second, r1, w1, inverse, base),
        (vec, vec, vec, total), alias={13: 0},
    )
    sums2 = everywhere(partial)
    estimate, left = call(
        last_kernel, "last", (sums0, sums1, sums2, field, image, inverse, r1, w1, r2, w2), (vec, vec)
    )
    return estimate.reshape(points, cases), left.reshape(points, cases)


def solution(mesh):
    wide = P(AXES, None)
    deep = P(AXES, None, None)
    return jax.shard_map(
        shards,
        mesh=mesh,
        in_specs=(
            deep, deep, wide, wide, P(AXES), P(AXES), P(AXES),
            P(None, AXES, None), P(None, AXES, None), wide,
        ),
        out_specs=(wide, wide),
        check_vma=False,
    )
```

```python
import functools
import jax
import jax.numpy as jnp
from jax import lax
from jax.experimental import pallas as pl
from jax.experimental.pallas import tpu as pltpu
from jax.sharding import PartitionSpec as P

AXES = ("sector", "axial")
F32 = jnp.float32
BF16 = jnp.bfloat16
VMEM = pl.BlockSpec(memory_space=pltpu.VMEM)
HBM = pl.BlockSpec(memory_space=pltpu.HBM)
SMEM = pl.BlockSpec(memory_space=pltpu.SMEM)
NT = (((1,), (1,)), ((), ()))
CHUNK = 32
GROUP = 16
LIMIT = 14 << 20
WIDE = 60 << 20
STRIPES = 4


def struct(*shape, dtype=F32):
    return jax.ShapeDtypeStruct(shape, dtype)


def iota(shape, dim):
    return lax.broadcasted_iota(jnp.int32, shape, dim)


def split(value):
    high = value.astype(BF16)
    return high, (value - high.astype(F32)).astype(BF16)


def dot(left, right, dims=(((1,), (0,)), ((), ()))):
    return lax.dot_general(left, right, dims, preferred_element_type=F32)


def pack_kernel(slots_each, owners, patches, counts, kbb, inner, nodes, payload, meta, blocks, node_rows, tally):
    step = pl.program_id(0)
    chunk, bn, _ = inner.shape
    half, quarter = bn // 2, bn // 4
    elems = kbb.shape[2]

    @pl.when(step == 0)
    def _():
        for i in range(half):
            blocks[pl.ds(i, elems, stride=half), :] = jnp.concatenate([kbb[i], kbb[i + half]], axis=0).T
        node_rows[...] = nodes[...].T
        meta[...] = jnp.zeros_like(meta)

        def clear(i, carry):
            tally[i] = 0
            return carry

        lax.fori_loop(0, meta.shape[0] // slots_each, clear, 0)

    row_id = iota((bn, bn), 0)
    col_id = iota((bn, bn), 1)
    lower = (row_id > col_id)[:half, :half]
    upper = (row_id < col_id)[:half, :half]
    lane = iota((1, 128), 1)
    for first in range(0, chunk, GROUP):
        group = range(GROUP)
        where = [step * chunk + first + e for e in group]
        grams = [dot(inner[first + e], inner[first + e], NT) for e in group]
        picks = [(node_rows[pl.ds(i, 1), :] == row_id).astype(F32).astype(BF16) for i in where]
        pairs = []
        for e in group:
            both = blocks[pl.ds(pl.multiple_of(where[e] * half, half), half), :]
            block = jnp.concatenate([both[:, :bn], both[:, bn:]], axis=0)
            pairs.append(split(block - grams[e]))
        lefts = [dot(jnp.concatenate([picks[e], picks[e]], axis=1), jnp.concatenate(pairs[e], axis=0)) for e in group]
        pairs = [split(left) for left in lefts]
        placed_all = [dot(pairs[e][0], picks[e], NT) + dot(pairs[e][1], picks[e], NT) for e in group]
        for e in group:
            placed, index = placed_all[e], where[e]
            triangles = jnp.where(lower, placed[:half, :half], jnp.where(upper, placed[half:, half:], 0.0))
            packed = jnp.concatenate([triangles, placed[:half, half:]], axis=1)
            packed = jnp.concatenate([packed[:quarter], packed[quarter:]], axis=1)
            diag = jnp.sum(jnp.where(row_id == col_id, placed, 0.0), axis=0, keepdims=True)
            owner = owners[index]
            rank = tally[owner]
            tally[owner] = rank + 1
            slot = owner * slots_each + rank
            payload[pl.ds(pl.multiple_of(slot * quarter, quarter), quarter), :] = packed
            tag = jnp.where(index < counts[0], patches[index] + 1, 0).astype(F32)
            meta[pl.ds(slot, 1), :] = jnp.where(
                lane < bn, jnp.concatenate([diag, diag], axis=1), jnp.where(lane == bn, tag, 0.0)
            )


def pack_call(devices, owners, patches, counts, kbb, inner, nodes):
    elems, bn, ni = inner.shape
    slots_each = 2 * elems // devices
    slots = devices * slots_each
    whole = lambda *shape: pl.BlockSpec(shape, lambda i: (0,) * len(shape))
    return pl.pallas_call(
        functools.partial(pack_kernel, slots_each),
        grid=(elems // CHUNK,),
        in_specs=[
            SMEM,
            SMEM,
            SMEM,
            whole(bn, bn, elems),
            pl.BlockSpec((CHUNK, bn, ni), lambda i: (i, 0, 0)),
            whole(bn, elems),
        ],
        out_specs=[whole(slots * bn // 4, 128), whole(slots, 128)],
        out_shape=[struct(slots * bn // 4, 128), struct(slots, 128)],
        scratch_shapes=[
            pltpu.VMEM((elems * bn // 2, 128), F32),
            pltpu.VMEM((elems, bn), jnp.int32),
            pltpu.SMEM((devices,), jnp.int32),
        ],
        compiler_params=pltpu.CompilerParams(vmem_limit_bytes=WIDE),
        name="pack",
    )(owners, patches, counts, kbb, inner, nodes)


def send_values(picked, gains, field, sends):
    count = sends[0].shape[0]
    for which, send in enumerate(sends):

        def one(k, carry):
            send[k] = gains[which * count + k] * field[picked[which * count + k]]
            return carry

        lax.fori_loop(0, count, one, 0, unroll=4)


def take_values(placed, received, result):
    count = received[0].shape[0]
    for which, got in enumerate(received):

        def one(k, carry):
            patch = placed[which * count + k]
            result[patch] = result[patch] - got[k]
            return carry

        lax.fori_loop(0, count, one, 0, unroll=4)


def gather_kernel(index0, index1, far0, far1, loads, gains, out0, out1, sems):
    bn = loads.shape[1]
    count = out0.shape[0]
    copies = []
    for which, (index, out) in enumerate(((index0, out0), (index1, out1))):
        for k in range(count):
            copies.append(pltpu.make_async_copy(loads.at[index[k]], out.at[k, pl.ds(0, bn)], sems.at[which]))
    for copy in copies:
        copy.start()
    if out0.shape[1] > bn:
        lane = iota((1, 128), 1)
        for which, (far, out) in enumerate(((far0, out0), (far1, out1))):
            rows = jnp.concatenate([gains[which], gains[which]], axis=1)
            for k in range(count):
                row = jnp.where(lane < bn, rows[k : k + 1], far[k].astype(F32))
                out[k, pl.ds(bn, 8), :] = jnp.broadcast_to(row, (8, 128))
    for copy in copies:
        copy.wait()


def gather_call(index0, index1, far0, far1, loads, gains, extra):
    out = struct(index0.shape[0], loads.shape[1] + extra, loads.shape[2])
    return pl.pallas_call(
        gather_kernel,
        in_specs=[SMEM, SMEM, SMEM, SMEM, pl.BlockSpec(memory_space=pl.ANY), VMEM],
        out_specs=[VMEM, VMEM],
        out_shape=[out, out],
        scratch_shapes=[pltpu.SemaphoreType.DMA((2,))],
        compiler_params=pltpu.CompilerParams(vmem_limit_bytes=WIDE),
        name="gather",
    )(index0, index1, far0, far1, loads, gains)


def diagonal_kernel(
    tags, picked, meta, capacity, conduct, g0, g2, loads, inverse, field, gains, t0, t1, t2, t3, total, gain_rows,
):
    patch_dev, bn = capacity.shape
    count = conduct.shape[1]
    for which, got in enumerate((g0, g2)):
        gain_rows[pl.ds(2 * which * count, count), :] = jnp.concatenate([conduct[which], conduct[which]], axis=1)
        for k in range(count):
            gain_rows[pl.ds((2 * which + 1) * count + k, 1), :] = got[k, pl.ds(bn, 1), :]
    total[pl.ds(0, patch_dev), :] = jnp.concatenate([capacity[...], capacity[...]], axis=1)

    def add(i, carry):
        patch = tags[i]
        total[pl.ds(patch, 1), :] = total[pl.ds(patch, 1), :] + meta[pl.ds(i, 1), :]
        return carry

    lax.fori_loop(0, meta.shape[0], add, 0, unroll=4)

    def link(i, carry):
        patch = picked[i]
        total[pl.ds(patch, 1), :] = total[pl.ds(patch, 1), :] + gain_rows[pl.ds(i, 1), :]
        return carry

    lax.fori_loop(0, gain_rows.shape[0], link, 0, unroll=4)
    over = 1.0 / total[pl.ds(0, patch_dev), :]
    total[pl.ds(0, patch_dev), :] = over
    columns = over[:, :bn].T
    for p in range(patch_dev):
        column = jnp.broadcast_to(columns[:, p : p + 1], (bn, 128))
        inverse[p] = column
        field[p] = column * loads[p]
    for which, rows in enumerate((t0, t1, t2, t3)):
        for k in range(count):
            i = which * count + k
            rows[pl.ds(k, 1), :] = total[pl.ds(picked[i], 1), :] * gain_rows[pl.ds(i, 1), :]
    columns = gain_rows[...][:, :bn].T
    for k in range(gain_rows.shape[0]):
        gains[k] = jnp.broadcast_to(columns[:, k : k + 1], (bn, 128))


def edges_kernel(placed, loads, t0, t1, t2, t3, g0, g1, g2, g3, image):
    bn = loads.shape[1]
    count = t0.shape[0]
    image[...] = loads[...]
    for which, (rows, got) in enumerate(((t0, g0), (t1, g1), (t2, g2), (t3, g3))):
        columns = rows[...][:, :bn].T
        for k in range(count):
            patch = placed[which * count + k]
            image[patch] = image[patch] - jnp.broadcast_to(columns[:, k : k + 1], (bn, 128)) * got[k, pl.ds(0, bn), :]


def stacked(value):
    high, low = split(value)
    return jnp.concatenate([high, high, low], axis=0)


def folded(value):
    total = value[0:8]
    for i in range(8, value.shape[0], 8):
        total = total + value[i : i + 8]
    return total


def publish(partial, sums):
    rows = [jnp.sum(s, axis=0, keepdims=True) for s in sums]
    block = jnp.concatenate(rows + [jnp.zeros((8 - len(rows), 128), F32)], axis=0)
    for d in range(partial.shape[0]):
        partial[d] = block


def gathered(received):
    return jnp.sum(received[...], axis=0)


def zeros(n):
    return (jnp.zeros((8, 128), F32),) * n


def assemble_kernel(
    tags, picked, payload, start_in, field_in, inverse_in, gains_in,
    image, blocks, after, s0, s1, s2, s3, field, inverse, gains, packed, sems,
):
    patch_dev, bn, _ = image.shape
    half, quarter = bn // 2, bn // 4
    banks = packed.shape[0]
    slots = tags.shape[0]
    pairs = ((start_in, image), (field_in, field), (inverse_in, inverse), (gains_in, gains))
    fetches = [pltpu.make_async_copy(src, dst, sems.at[i]) for i, (src, dst) in enumerate(pairs)]
    for copy in fetches:
        copy.start()
    packed[...] = jnp.zeros_like(packed)

    def add(j, carry):
        for bank in range(banks):
            i = j * banks + bank
            patch = tags[i]
            packed[bank, patch] = packed[bank, patch] + payload[pl.ds(pl.multiple_of(i * quarter, quarter), quarter), :]
        return carry

    lax.fori_loop(0, slots // banks, add, 0, unroll=2)
    fetches[0].wait()
    fetches[1].wait()
    row_id = iota((half, bn), 0)
    col_id = iota((half, bn), 1)
    kept = (col_id >= half) | (row_id > col_id)
    moved = (col_id < half) & (row_id < col_id)

    def build(j, carry):
        group = [j * GROUP + g for g in range(GROUP)]
        wholes = []
        for p in group:
            both = packed[0, p]
            for bank in range(1, banks):
                both = both + packed[bank, p]
            rows = jnp.concatenate([both[:, :bn], both[:, bn:]], axis=0)
            second = jnp.where(moved, rows, 0.0)[:, :half]
            second = jnp.concatenate([jnp.zeros((half, half), F32), second], axis=1)
            wholes.append(jnp.concatenate([jnp.where(kept, rows, 0.0), second], axis=0))
        wholes = [w + w.T for w in wholes]
        threes = []
        for w in wholes:
            high, low = split(w)
            threes.append(jnp.concatenate([high, low, high], axis=1))
        for p, three in zip(group, threes):
            blocks[p] = three
        products = [dot(three, stacked(field[p])) for p, three in zip(group, threes)]
        for p, product in zip(group, products):
            image[p] = image[p] + product
        return carry

    lax.fori_loop(0, patch_dev // GROUP, build, 0)
    for copy in fetches[2:]:
        copy.wait()

    def finish(p, carry):
        after[p] = inverse[p] * image[p]
        return carry

    lax.fori_loop(0, patch_dev, finish, 0, unroll=2)
    send_values(picked, gains, after, (s0, s1, s2, s3))


def times_all(blocks, field, base, result):
    def some(j, carry):
        group = [j * GROUP + g for g in range(GROUP)]
        products = [dot(blocks[p], stacked(field[p])) for p in group]
        for p, product in zip(group, products):
            result[p] = base[p] + product
        return carry

    lax.fori_loop(0, field.shape[0] // GROUP, some, 0)


def first_local_kernel(blocks, after, image, loads, field, result, partial):
    times_all(blocks, after, image, result)

    def one(p, carry):
        value = field[p]
        return carry[0] + folded(loads[p] * value), carry[1] + folded(image[p] * value)

    publish(partial, lax.fori_loop(0, loads.shape[0], one, zeros(2), unroll=2))


def second_kernel(picked, placed, inverse, gains, g0, g1, g2, g3, base, result, after, s0, s1, s2, s3):
    take_values(placed, (g0, g1, g2, g3), result)

    def scale(p, carry):
        after[p] = inverse[p] * result[p]
        return carry

    lax.fori_loop(0, inverse.shape[0], scale, 0, unroll=2)
    send_values(picked, gains, after, (s0, s1, s2, s3))


def first_step_kernel(
    sums, blocks, after, loads, field, image, second, inverse, result, left, left_image, partial
):
    times_all(blocks, after, second, result)
    first = gathered(sums)
    alpha = first[0:1] / first[1:2]

    def one(p, carry):
        r = loads[p] - alpha * image[p]
        w = image[p] - alpha * second[p]
        u = inverse[p] * r
        left[p] = r
        left_image[p] = w
        return (
            carry[0] + folded(r * u),
            carry[1] + folded(u * w),
            carry[2] + folded(u * image[p] + field[p] * w),
        )

    publish(partial, lax.fori_loop(0, loads.shape[0], one, zeros(3), unroll=2))


def second_step_kernel(
    sums0, sums1, placed, g0, g1, g2, g3, field, image, second, r1, w1, inverse, base,
    third, r2_out, w2_out, partial,
):
    first, then = gathered(sums0), gathered(sums1)
    alpha0 = first[0:1] / first[1:2]
    beta1 = then[0:1] / first[0:1]
    alpha1 = then[0:1] / (then[1:2] + beta1 * (then[2:3] + beta1 * first[1:2]))
    take_values(placed, (g0, g1, g2, g3), third)

    def one(p, carry):
        n0, w, r = second[p], w1[p], r1[p]
        s1 = w + beta1 * image[p]
        z1 = (n0 - alpha0 * third[p]) + beta1 * n0
        r2 = r - alpha1 * s1
        w2 = w - alpha1 * z1
        u2 = inverse[p] * r2
        p1 = inverse[p] * r + beta1 * field[p]
        r2_out[p] = r2
        w2_out[p] = w2
        return (
            carry[0] + folded(r2 * u2),
            carry[1] + folded(u2 * w2),
            carry[2] + folded(u2 * s1 + p1 * w2),
        )

    publish(partial, lax.fori_loop(0, field.shape[0], one, zeros(3)))


def last_kernel(
    sums0, sums1, sums2, field, image, inverse, r1, w1, r2, w2, estimate_out, left_out, estimate, left, sems
):
    first, then, last = gathered(sums0), gathered(sums1), gathered(sums2)
    alpha0 = first[0:1] / first[1:2]
    beta1 = then[0:1] / first[0:1]
    curve1 = then[1:2] + beta1 * (then[2:3] + beta1 * first[1:2])
    alpha1 = then[0:1] / curve1
    beta2 = last[0:1] / then[0:1]
    alpha2 = last[0:1] / (last[1:2] + beta2 * (last[2:3] + beta2 * curve1))

    def one(p, carry):
        p1 = inverse[p] * r1[p] + beta1 * field[p]
        direction = inverse[p] * r2[p] + beta2 * p1
        estimate[p] = alpha0 * field[p] + alpha1 * p1 + alpha2 * direction
        left[p] = r2[p] - alpha2 * (w2[p] + beta2 * (w1[p] + beta1 * image[p]))
        return carry

    size = field.shape[0] // STRIPES
    copies = []
    for c in range(STRIPES):
        lax.fori_loop(c * size, (c + 1) * size, one, 0, unroll=2)
        part = pl.ds(c * size, size)
        for i, (src, dst) in enumerate(((estimate, estimate_out), (left, left_out))):
            copies.append(pltpu.make_async_copy(src.at[part], dst.at[part], sems.at[i, c]))
            copies[-1].start()
    for copy in copies:
        copy.wait()


def call(kernel, name, ins, outs, scratch=(), flops=0, alias=None, limit=None, far=(), out=VMEM):
    ints = lambda a: a.ndim == 1 and a.dtype == jnp.int32
    moved = sum(a.size * a.dtype.itemsize for a in ins) + sum(s.size * s.dtype.itemsize for s in outs)
    return pl.pallas_call(
        kernel,
        in_specs=[SMEM if ints(a) else HBM if i in far else VMEM for i, a in enumerate(ins)],
        out_specs=[out] * len(outs),
        out_shape=list(outs),
        scratch_shapes=list(scratch),
        input_output_aliases=alias or {},
        cost_estimate=pl.CostEstimate(flops=flops, bytes_accessed=moved, transcendentals=0),
        compiler_params=pltpu.CompilerParams(vmem_limit_bytes=limit or LIMIT),
        name=name,
    )(*[pltpu.with_memory_space_constraint(a, pltpu.HBM) if i in far else a for i, a in enumerate(ins)])


def everywhere(partial):
    return lax.all_to_all(partial, AXES, split_axis=0, concat_axis=0, tiled=True)


def onward(value, axis, wrap):
    n = lax.axis_size(axis)
    return lax.ppermute(value, axis, [(i, (i + 1) % n) for i in range(n) if wrap or i + 1 < n])


def back(value, axis, wrap):
    n = lax.axis_size(axis)
    return lax.ppermute(value, axis, [((i + 1) % n, i) for i in range(n) if wrap or i + 1 < n])


def exchange(s0, s1, s2, s3):
    return (
        onward(s0, "sector", True),
        back(s1, "sector", True),
        onward(s2, "axial", False),
        back(s3, "axial", False),
    )


def shards(kbb, interior, node_lists, owners, patch_ids, counts, capacity, links, conduct, loads):
    elems, bn = node_lists.shape
    devices = lax.axis_size("sector") * lax.axis_size("axial")
    points, cases = loads.shape
    patch_dev = points // bn
    count = conduct.shape[1]
    loads = loads.reshape(patch_dev, bn, cases)
    vec = struct(patch_dev, bn, cases)
    buf = struct(count, bn, cases)
    total = struct(devices, 8, cases)

    table = links.transpose(0, 2, 1)
    own_sector, own_axial = table[0, 0], table[1, 0]
    s0, s2 = gather_call(own_sector, own_axial, table[0, 1], table[1, 1], loads, conduct, 8)
    owners, s0, s2 = lax.optimization_barrier((owners, s0, s2))
    g0, g2 = onward(s0, "sector", True), onward(s2, "axial", False)
    payload, meta = pack_call(
        devices, owners.reshape(elems), patch_ids, counts,
        kbb.transpose(1, 2, 0), interior.transpose(0, 2, 1), node_lists.T,
    )
    slots = meta.shape[0]
    payload, meta, g0, g2 = lax.optimization_barrier((payload, meta, g0, g2))
    far_sector, far_axial = g0[:, bn, bn].astype(jnp.int32), g2[:, bn, bn].astype(jnp.int32)
    s1, s3 = gather_call(far_sector, far_axial, far_sector, far_axial, loads, conduct, 0)
    meta, s1, s3 = lax.optimization_barrier((meta, s1, s3))
    g1, g3 = back(s1, "sector", True), back(s3, "axial", False)
    meta = everywhere(meta.reshape(devices, slots // devices, 128)).reshape(slots, 128)
    payload, g1, g3 = lax.optimization_barrier((payload, g1, g3))
    payload = everywhere(payload.reshape(devices, -1, 128)).reshape(slots * bn // 4, 128)
    picked = jnp.concatenate([own_sector, far_sector, own_axial, far_axial])
    placed = jnp.concatenate([far_sector, own_sector, far_axial, own_axial])
    tags = meta[:, bn].astype(jnp.int32)
    tags = jnp.where(tags > 0, tags - 1, patch_dev)
    row = struct(count, 128)
    inverse, field, gains, *rows = call(
        diagonal_kernel, "diagonal",
        (tags, picked, meta, capacity.reshape(patch_dev, bn), conduct, g0, g2, loads),
        (vec, vec, struct(4 * count, bn, cases), row, row, row, row),
        (pltpu.VMEM((patch_dev + 8, 128), F32), pltpu.VMEM((4 * count, 128), F32)), limit=WIDE,
    )
    rows = exchange(*rows)
    (start,) = call(edges_kernel, "edges", (placed, loads, *rows, g0, g1, g2, g3), (vec,), limit=WIDE)
    image, blocks, after, *rest = call(
        assemble_kernel, "assemble",
        (tags, picked, payload, start, field, inverse, gains),
        (vec, struct(patch_dev, bn, 3 * bn, dtype=BF16), vec, buf, buf, buf, buf,
         vec, vec, struct(4 * count, bn, cases)),
        (pltpu.VMEM((4, patch_dev + 1, bn // 4, 128), F32), pltpu.SemaphoreType.DMA((4,))),
        far=(3, 4, 5, 6),
    )
    *sends, field, inverse, gains = rest
    got = exchange(*sends)
    base, partial = call(first_local_kernel, "first_local", (blocks, after, image, loads, field), (vec, total))
    sums0 = everywhere(partial)
    base, sums0 = lax.optimization_barrier((base, sums0))
    second, after, *sends = call(
        second_kernel, "second", (picked, placed, inverse, gains, *got, base),
        (vec, vec, buf, buf, buf, buf), alias={8: 0},
    )
    got = exchange(*sends)
    base, r1, w1, partial = call(
        first_step_kernel, "first_step",
        (sums0, blocks, after, loads, field, image, second, inverse), (vec, vec, vec, total),
    )
    sums1 = everywhere(partial)
    base, sums1 = lax.optimization_barrier((base, sums1))
    _, r2, w2, partial = call(
        second_step_kernel, "second_step",
        (sums0, sums1, placed, *got, field, image, second, r1, w1, inverse, base),
        (vec, vec, vec, total), alias={13: 0},
    )
    sums2 = everywhere(partial)
    estimate, left = call(
        last_kernel, "last", (sums0, sums1, sums2, field, image, inverse, r1, w1, r2, w2), (vec, vec),
        (pltpu.VMEM(loads.shape, F32), pltpu.VMEM(loads.shape, F32), pltpu.SemaphoreType.DMA((2, STRIPES))),
        out=pl.BlockSpec(memory_space=pl.ANY),
    )
    return estimate.reshape(points, cases), left.reshape(points, cases)


def solution(mesh):
    wide = P(AXES, None)
    deep = P(AXES, None, None)
    return jax.shard_map(
        shards,
        mesh=mesh,
        in_specs=(
            deep, deep, wide, wide, P(AXES), P(AXES), P(AXES),
            P(None, AXES, None), P(None, AXES, None), wide,
        ),
        out_specs=(wide, wide),
        check_vma=False,
    )
```

```python
import functools
import jax
import jax.numpy as jnp
from jax import lax
from jax.experimental import pallas as pl
from jax.experimental.pallas import tpu as pltpu
from jax.sharding import PartitionSpec as P

AXES = ("sector", "axial")
F32 = jnp.float32
BF16 = jnp.bfloat16
VMEM = pl.BlockSpec(memory_space=pltpu.VMEM)
HBM = pl.BlockSpec(memory_space=pltpu.HBM)
SMEM = pl.BlockSpec(memory_space=pltpu.SMEM)
NT = (((1,), (1,)), ((), ()))
CHUNK = 32
GROUP = 16
LIMIT = 14 << 20
WIDE = 60 << 20
STRIPES = 4


def struct(*shape, dtype=F32):
    return jax.ShapeDtypeStruct(shape, dtype)


def iota(shape, dim):
    return lax.broadcasted_iota(jnp.int32, shape, dim)


def split(value):
    high = value.astype(BF16)
    return high, (value - high.astype(F32)).astype(BF16)


def dot(left, right, dims=(((1,), (0,)), ((), ()))):
    return lax.dot_general(left, right, dims, preferred_element_type=F32)


def pack_kernel(slots_each, owners, patches, counts, kbb, inner, nodes, payload, meta, blocks, node_rows, tally):
    step = pl.program_id(0)
    chunk, bn, _ = inner.shape
    half, quarter = bn // 2, bn // 4
    elems = kbb.shape[2]

    @pl.when(step == 0)
    def _():
        for i in range(half):
            blocks[pl.ds(i, elems, stride=half), :] = jnp.concatenate([kbb[i], kbb[i + half]], axis=0).T
        node_rows[...] = nodes[...].T
        meta[...] = jnp.zeros_like(meta)

        def clear(i, carry):
            tally[i] = 0
            return carry

        lax.fori_loop(0, meta.shape[0] // slots_each, clear, 0)

    row_id = iota((bn, bn), 0)
    col_id = iota((bn, bn), 1)
    lower = (row_id > col_id)[:half, :half]
    upper = (row_id < col_id)[:half, :half]
    lane = iota((1, 128), 1)
    for first in range(0, chunk, GROUP):
        group = range(GROUP)
        where = [step * chunk + first + e for e in group]
        grams = [dot(inner[first + e], inner[first + e], NT) for e in group]
        picks = [(node_rows[pl.ds(i, 1), :] == row_id).astype(F32).astype(BF16) for i in where]
        pairs = []
        for e in group:
            both = blocks[pl.ds(pl.multiple_of(where[e] * half, half), half), :]
            block = jnp.concatenate([both[:, :bn], both[:, bn:]], axis=0)
            pairs.append(split(block - grams[e]))
        lefts = [dot(jnp.concatenate([picks[e], picks[e]], axis=1), jnp.concatenate(pairs[e], axis=0)) for e in group]
        pairs = [split(left) for left in lefts]
        placed_all = [dot(pairs[e][0], picks[e], NT) + dot(pairs[e][1], picks[e], NT) for e in group]
        for e in group:
            placed, index = placed_all[e], where[e]
            triangles = jnp.where(lower, placed[:half, :half], jnp.where(upper, placed[half:, half:], 0.0))
            packed = jnp.concatenate([triangles, placed[:half, half:]], axis=1)
            packed = jnp.concatenate([packed[:quarter], packed[quarter:]], axis=1)
            diag = jnp.sum(jnp.where(row_id == col_id, placed, 0.0), axis=0, keepdims=True)
            owner = owners[index]
            rank = tally[owner]
            tally[owner] = rank + 1
            slot = owner * slots_each + rank
            payload[pl.ds(pl.multiple_of(slot * quarter, quarter), quarter), :] = packed
            tag = jnp.where(index < counts[0], patches[index] + 1, 0).astype(F32)
            meta[pl.ds(slot, 1), :] = jnp.where(
                lane < bn, jnp.concatenate([diag, diag], axis=1), jnp.where(lane == bn, tag, 0.0)
            )


def pack_call(devices, owners, patches, counts, kbb, inner, nodes):
    elems, bn, ni = inner.shape
    slots_each = 2 * elems // devices
    slots = devices * slots_each
    whole = lambda *shape: pl.BlockSpec(shape, lambda i: (0,) * len(shape))
    return pl.pallas_call(
        functools.partial(pack_kernel, slots_each),
        grid=(elems // CHUNK,),
        in_specs=[
            SMEM,
            SMEM,
            SMEM,
            whole(bn, bn, elems),
            pl.BlockSpec((CHUNK, bn, ni), lambda i: (i, 0, 0)),
            whole(bn, elems),
        ],
        out_specs=[whole(slots * bn // 4, 128), whole(slots, 128)],
        out_shape=[struct(slots * bn // 4, 128), struct(slots, 128)],
        scratch_shapes=[
            pltpu.VMEM((elems * bn // 2, 128), F32),
            pltpu.VMEM((elems, bn), jnp.int32),
            pltpu.SMEM((devices,), jnp.int32),
        ],
        compiler_params=pltpu.CompilerParams(vmem_limit_bytes=WIDE),
        name="pack",
    )(owners, patches, counts, kbb, inner, nodes)


def send_values(picked, gains, field, sends):
    count = sends[0].shape[0]
    for which, send in enumerate(sends):

        def one(k, carry):
            send[k] = gains[which * count + k] * field[picked[which * count + k]]
            return carry

        lax.fori_loop(0, count, one, 0, unroll=4)


def take_values(placed, received, result):
    count = received[0].shape[0]
    for which, got in enumerate(received):

        def one(k, carry):
            patch = placed[which * count + k]
            result[patch] = result[patch] - got[k]
            return carry

        lax.fori_loop(0, count, one, 0, unroll=4)


def gather_kernel(index0, index1, far0, far1, loads, gains, out0, out1, sems):
    bn = loads.shape[1]
    count = out0.shape[0]
    copies = []
    for which, (index, out) in enumerate(((index0, out0), (index1, out1))):
        for k in range(count):
            copies.append(pltpu.make_async_copy(loads.at[index[k]], out.at[k, pl.ds(0, bn)], sems.at[which]))
    for copy in copies:
        copy.start()
    if out0.shape[1] > bn:
        lane = iota((1, 128), 1)
        for which, (far, out) in enumerate(((far0, out0), (far1, out1))):
            rows = jnp.concatenate([gains[which], gains[which]], axis=1)
            for k in range(count):
                row = jnp.where(lane < bn, rows[k : k + 1], far[k].astype(F32))
                out[k, pl.ds(bn, 8), :] = jnp.broadcast_to(row, (8, 128))
    for copy in copies:
        copy.wait()


def gather_call(index0, index1, far0, far1, loads, gains, extra):
    out = struct(index0.shape[0], loads.shape[1] + extra, loads.shape[2])
    return pl.pallas_call(
        gather_kernel,
        in_specs=[SMEM, SMEM, SMEM, SMEM, pl.BlockSpec(memory_space=pl.ANY), VMEM],
        out_specs=[VMEM, VMEM],
        out_shape=[out, out],
        scratch_shapes=[pltpu.SemaphoreType.DMA((2,))],
        compiler_params=pltpu.CompilerParams(vmem_limit_bytes=WIDE),
        name="gather",
    )(index0, index1, far0, far1, loads, gains)


def diagonal_kernel(
    tags, picked, meta, capacity, conduct, g0, g2, loads, inverse, field, gains, t0, t1, t2, t3, total, gain_rows,
):
    patch_dev, bn = capacity.shape
    count = conduct.shape[1]
    for which, got in enumerate((g0, g2)):
        gain_rows[pl.ds(2 * which * count, count), :] = jnp.concatenate([conduct[which], conduct[which]], axis=1)
        for k in range(count):
            gain_rows[pl.ds((2 * which + 1) * count + k, 1), :] = got[k, pl.ds(bn, 1), :]
    total[pl.ds(0, patch_dev), :] = jnp.concatenate([capacity[...], capacity[...]], axis=1)

    def add(i, carry):
        patch = tags[i]
        total[pl.ds(patch, 1), :] = total[pl.ds(patch, 1), :] + meta[pl.ds(i, 1), :]
        return carry

    lax.fori_loop(0, meta.shape[0], add, 0, unroll=4)

    def link(i, carry):
        patch = picked[i]
        total[pl.ds(patch, 1), :] = total[pl.ds(patch, 1), :] + gain_rows[pl.ds(i, 1), :]
        return carry

    lax.fori_loop(0, gain_rows.shape[0], link, 0, unroll=4)
    over = 1.0 / total[pl.ds(0, patch_dev), :]
    total[pl.ds(0, patch_dev), :] = over
    columns = over[:, :bn].T
    for p in range(patch_dev):
        column = jnp.broadcast_to(columns[:, p : p + 1], (bn, 128))
        inverse[p] = column
        field[p] = column * loads[p]
    for which, rows in enumerate((t0, t1, t2, t3)):
        for k in range(count):
            i = which * count + k
            rows[pl.ds(k, 1), :] = total[pl.ds(picked[i], 1), :] * gain_rows[pl.ds(i, 1), :]
    columns = gain_rows[...][:, :bn].T
    for k in range(gain_rows.shape[0]):
        gains[k] = jnp.broadcast_to(columns[:, k : k + 1], (bn, 128))


def edges_kernel(placed, loads, t0, t1, t2, t3, g0, g1, g2, g3, image, u1, u3):
    bn = loads.shape[1]
    count = t0.shape[0]
    image[...] = loads[...]
    for which, (rows, got) in enumerate(((t0, g0), (t1, g1), (t2, g2), (t3, g3))):
        columns = rows[...][:, :bn].T
        for k in range(count):
            patch = placed[which * count + k]
            value = jnp.broadcast_to(columns[:, k : k + 1], (bn, 128)) * got[k, pl.ds(0, bn), :]
            image[patch] = image[patch] - value
            if which % 2:
                (u1, u3)[which // 2][k] = value


def stacked(value):
    high, low = split(value)
    return jnp.concatenate([high, high, low], axis=0)


def folded(value):
    total = value[0:8]
    for i in range(8, value.shape[0], 8):
        total = total + value[i : i + 8]
    return total


def publish(partial, sums):
    rows = [jnp.sum(s, axis=0, keepdims=True) for s in sums]
    block = jnp.concatenate(rows + [jnp.zeros((8 - len(rows), 128), F32)], axis=0)
    for d in range(partial.shape[0]):
        partial[d] = block


def gathered(received):
    return jnp.sum(received[...], axis=0)


def zeros(n):
    return (jnp.zeros((8, 128), F32),) * n


def assemble_kernel(
    tags, picked, payload, start_in, field_in, inverse_in, gains_in,
    image, blocks, after, s0, s1, s2, s3, field, inverse, gains, packed, sems,
):
    patch_dev, bn, _ = image.shape
    half, quarter = bn // 2, bn // 4
    banks = packed.shape[0]
    slots = tags.shape[0]
    pairs = ((start_in, image), (field_in, field), (inverse_in, inverse), (gains_in, gains))
    fetches = [pltpu.make_async_copy(src, dst, sems.at[i]) for i, (src, dst) in enumerate(pairs)]
    for copy in fetches:
        copy.start()
    packed[...] = jnp.zeros_like(packed)

    def add(j, carry):
        for bank in range(banks):
            i = j * banks + bank
            patch = tags[i]
            packed[bank, patch] = packed[bank, patch] + payload[pl.ds(pl.multiple_of(i * quarter, quarter), quarter), :]
        return carry

    lax.fori_loop(0, slots // banks, add, 0, unroll=2)
    fetches[0].wait()
    fetches[1].wait()
    row_id = iota((half, bn), 0)
    col_id = iota((half, bn), 1)
    kept = (col_id >= half) | (row_id > col_id)
    moved = (col_id < half) & (row_id < col_id)

    def build(j, carry):
        group = [j * GROUP + g for g in range(GROUP)]
        wholes = []
        for p in group:
            both = packed[0, p]
            for bank in range(1, banks):
                both = both + packed[bank, p]
            rows = jnp.concatenate([both[:, :bn], both[:, bn:]], axis=0)
            second = jnp.where(moved, rows, 0.0)[:, :half]
            second = jnp.concatenate([jnp.zeros((half, half), F32), second], axis=1)
            wholes.append(jnp.concatenate([jnp.where(kept, rows, 0.0), second], axis=0))
        wholes = [w + w.T for w in wholes]
        threes = []
        for w in wholes:
            high, low = split(w)
            threes.append(jnp.concatenate([high, low, high], axis=1))
        for p, three in zip(group, threes):
            blocks[p] = three
        products = [dot(three, stacked(field[p])) for p, three in zip(group, threes)]
        for p, product in zip(group, products):
            image[p] = image[p] + product
        return carry

    lax.fori_loop(0, patch_dev // GROUP, build, 0)
    for copy in fetches[2:]:
        copy.wait()

    def finish(p, carry):
        after[p] = inverse[p] * image[p]
        return carry

    lax.fori_loop(0, patch_dev, finish, 0, unroll=2)
    send_values(picked, gains, after, (s0, s1, s2, s3))


def times_all(blocks, field, base, result):
    def some(j, carry):
        group = [j * GROUP + g for g in range(GROUP)]
        products = [dot(blocks[p], stacked(field[p])) for p in group]
        for p, product in zip(group, products):
            result[p] = base[p] + product
        return carry

    lax.fori_loop(0, field.shape[0] // GROUP, some, 0)


def first_local_kernel(blocks, after, image, loads, field, result, partial):
    times_all(blocks, after, image, result)

    def one(p, carry):
        value = field[p]
        return carry[0] + folded(loads[p] * value), carry[1] + folded(image[p] * value)

    publish(partial, lax.fori_loop(0, loads.shape[0], one, zeros(2), unroll=2))


def second_kernel(picked, placed, inverse, gains, g0, g1, g2, g3, base, result, after, s0, s1, s2, s3):
    take_values(placed, (g0, g1, g2, g3), result)

    def scale(p, carry):
        after[p] = inverse[p] * result[p]
        return carry

    lax.fori_loop(0, inverse.shape[0], scale, 0, unroll=2)
    send_values(picked, gains, after, (s0, s1, s2, s3))


def first_step_kernel(
    sums, blocks, after, loads, field, image, second, inverse, result, left, left_image, partial
):
    times_all(blocks, after, second, result)
    first = gathered(sums)
    alpha = first[0:1] / first[1:2]

    def one(p, carry):
        r = loads[p] - alpha * image[p]
        w = image[p] - alpha * second[p]
        u = inverse[p] * r
        left[p] = r
        left_image[p] = w
        return (
            carry[0] + folded(r * u),
            carry[1] + folded(u * w),
            carry[2] + folded(u * image[p] + field[p] * w),
        )

    publish(partial, lax.fori_loop(0, loads.shape[0], one, zeros(3), unroll=2))


def second_step_kernel(
    sums0, sums1, placed, u1, u3, m1, m3, q1, q3, field, image, second, after, r1, w1, inverse, base,
    r2_out, w2_out, partial,
):
    first, then = gathered(sums0), gathered(sums1)
    alpha0 = first[0:1] / first[1:2]
    beta1 = then[0:1] / first[0:1]
    alpha1 = then[0:1] / (then[1:2] + beta1 * (then[2:3] + beta1 * first[1:2]))
    both = alpha0 * alpha1
    count = u1.shape[0]

    def one(p, carry):
        w, r = w1[p], r1[p]
        s1 = w + beta1 * image[p]
        r2 = r - alpha1 * s1
        w2 = w - alpha1 * ((1.0 + beta1) * second[p]) + both * base[p]
        u2 = inverse[p] * r2
        p1 = inverse[p] * r + beta1 * field[p]
        r2_out[p] = r2
        w2_out[p] = w2
        return (
            carry[0] + folded(r2 * u2),
            carry[1] + folded(u2 * w2),
            carry[2] + folded(u2 * s1 + p1 * w2),
        )

    sums = lax.fori_loop(0, field.shape[0], one, zeros(3), unroll=2)
    links = zeros(2)
    for which, (far_u, far_m, far_q) in ((1, (u1, m1, q1)), (3, (u3, m3, q3))):

        def link(k, carry):
            p = placed[which * count + k]
            u, m, q = far_u[k], far_m[k], far_q[k]
            u2 = inverse[p] * r2_out[p]
            p1 = inverse[p] * r1[p] + beta1 * field[p]
            far_p1 = (1.0 + beta1) * u - alpha0 * m
            far_u2 = u - (alpha0 + alpha1 * (1.0 + beta1)) * m + both * q
            here = after[p]
            return carry[0] + folded(u2 * q + far_u2 * here), carry[1] + folded(p1 * q + far_p1 * here)

        links = lax.fori_loop(0, count, link, links, unroll=2)
    publish(partial, (sums[0], sums[1] - both * links[0], sums[2] - both * links[1]))


def last_kernel(
    sums0, sums1, sums2, placed, g0, g1, g2, g3, field, image, inverse, r1, w1, r2, w2,
    estimate_out, left_out, estimate, left, sems,
):
    first, then, last = gathered(sums0), gathered(sums1), gathered(sums2)
    alpha0 = first[0:1] / first[1:2]
    beta1 = then[0:1] / first[0:1]
    curve1 = then[1:2] + beta1 * (then[2:3] + beta1 * first[1:2])
    alpha1 = then[0:1] / curve1
    beta2 = last[0:1] / then[0:1]
    alpha2 = last[0:1] / (last[1:2] + beta2 * (last[2:3] + beta2 * curve1))
    part = alpha2 * alpha0 * alpha1
    size = field.shape[0] // STRIPES
    copies = []

    def residual(p, carry):
        left[p] = r2[p] - alpha2 * (w2[p] + beta2 * (w1[p] + beta1 * image[p]))
        return carry

    lax.fori_loop(0, field.shape[0], residual, 0, unroll=2)
    count = g0.shape[0]
    for which, got in enumerate((g0, g1, g2, g3)):

        def link(k, carry):
            patch = placed[which * count + k]
            left[patch] = left[patch] + part * got[k]
            return carry

        lax.fori_loop(0, count, link, 0, unroll=4)

    def iterate(p, carry):
        p1 = inverse[p] * r1[p] + beta1 * field[p]
        estimate[p] = alpha0 * field[p] + alpha1 * p1 + alpha2 * (inverse[p] * r2[p] + beta2 * p1)
        return carry

    copies.append(pltpu.make_async_copy(left, left_out, sems.at[STRIPES]))
    copies[-1].start()
    for c in range(STRIPES):
        lax.fori_loop(c * size, (c + 1) * size, iterate, 0, unroll=2)
        rows = pl.ds(c * size, size)
        copies.append(pltpu.make_async_copy(estimate.at[rows], estimate_out.at[rows], sems.at[c]))
        copies[-1].start()
    for copy in copies:
        copy.wait()


def call(kernel, name, ins, outs, scratch=(), flops=0, alias=None, limit=None, far=(), out=VMEM):
    ints = lambda a: a.ndim == 1 and a.dtype == jnp.int32
    moved = sum(a.size * a.dtype.itemsize for a in ins) + sum(s.size * s.dtype.itemsize for s in outs)
    return pl.pallas_call(
        kernel,
        in_specs=[SMEM if ints(a) else HBM if i in far else VMEM for i, a in enumerate(ins)],
        out_specs=[out] * len(outs),
        out_shape=list(outs),
        scratch_shapes=list(scratch),
        input_output_aliases=alias or {},
        cost_estimate=pl.CostEstimate(flops=flops, bytes_accessed=moved, transcendentals=0),
        compiler_params=pltpu.CompilerParams(vmem_limit_bytes=limit or LIMIT),
        name=name,
    )(*[pltpu.with_memory_space_constraint(a, pltpu.HBM) if i in far else a for i, a in enumerate(ins)])


def everywhere(partial):
    return lax.all_to_all(partial, AXES, split_axis=0, concat_axis=0, tiled=True)


def onward(value, axis, wrap):
    n = lax.axis_size(axis)
    return lax.ppermute(value, axis, [(i, (i + 1) % n) for i in range(n) if wrap or i + 1 < n])


def back(value, axis, wrap):
    n = lax.axis_size(axis)
    return lax.ppermute(value, axis, [((i + 1) % n, i) for i in range(n) if wrap or i + 1 < n])


def exchange(s0, s1, s2, s3):
    return (
        onward(s0, "sector", True),
        back(s1, "sector", True),
        onward(s2, "axial", False),
        back(s3, "axial", False),
    )


def shards(kbb, interior, node_lists, owners, patch_ids, counts, capacity, links, conduct, loads):
    elems, bn = node_lists.shape
    devices = lax.axis_size("sector") * lax.axis_size("axial")
    points, cases = loads.shape
    patch_dev = points // bn
    count = conduct.shape[1]
    loads = loads.reshape(patch_dev, bn, cases)
    vec = struct(patch_dev, bn, cases)
    buf = struct(count, bn, cases)
    total = struct(devices, 8, cases)

    table = links.transpose(0, 2, 1)
    own_sector, own_axial = table[0, 0], table[1, 0]
    s0, s2 = gather_call(own_sector, own_axial, table[0, 1], table[1, 1], loads, conduct, 8)
    owners, s0, s2 = lax.optimization_barrier((owners, s0, s2))
    g0, g2 = onward(s0, "sector", True), onward(s2, "axial", False)
    payload, meta = pack_call(
        devices, owners.reshape(elems), patch_ids, counts,
        kbb.transpose(1, 2, 0), interior.transpose(0, 2, 1), node_lists.T,
    )
    slots = meta.shape[0]
    payload, meta, g0, g2 = lax.optimization_barrier((payload, meta, g0, g2))
    far_sector, far_axial = g0[:, bn, bn].astype(jnp.int32), g2[:, bn, bn].astype(jnp.int32)
    s1, s3 = gather_call(far_sector, far_axial, far_sector, far_axial, loads, conduct, 0)
    meta, s1, s3 = lax.optimization_barrier((meta, s1, s3))
    g1, g3 = back(s1, "sector", True), back(s3, "axial", False)
    meta = everywhere(meta.reshape(devices, slots // devices, 128)).reshape(slots, 128)
    payload, g1, g3 = lax.optimization_barrier((payload, g1, g3))
    payload = everywhere(payload.reshape(devices, -1, 128)).reshape(slots * bn // 4, 128)
    picked = jnp.concatenate([own_sector, far_sector, own_axial, far_axial])
    placed = jnp.concatenate([far_sector, own_sector, far_axial, own_axial])
    tags = meta[:, bn].astype(jnp.int32)
    tags = jnp.where(tags > 0, tags - 1, patch_dev)
    row = struct(count, 128)
    inverse, field, gains, *rows = call(
        diagonal_kernel, "diagonal",
        (tags, picked, meta, capacity.reshape(patch_dev, bn), conduct, g0, g2, loads),
        (vec, vec, struct(4 * count, bn, cases), row, row, row, row),
        (pltpu.VMEM((patch_dev + 8, 128), F32), pltpu.VMEM((4 * count, 128), F32)), limit=WIDE,
    )
    rows = exchange(*rows)
    start, far_u1, far_u3 = call(
        edges_kernel, "edges", (placed, loads, *rows, g0, g1, g2, g3), (vec, buf, buf), limit=WIDE
    )
    image, blocks, after, *rest = call(
        assemble_kernel, "assemble",
        (tags, picked, payload, start, field, inverse, gains),
        (vec, struct(patch_dev, bn, 3 * bn, dtype=BF16), vec, buf, buf, buf, buf,
         vec, vec, struct(4 * count, bn, cases)),
        (pltpu.VMEM((4, patch_dev + 1, bn // 4, 128), F32), pltpu.SemaphoreType.DMA((4,))),
        far=(3, 4, 5, 6),
    )
    *sends, field, inverse, gains = rest
    got = exchange(*sends)
    base, partial = call(first_local_kernel, "first_local", (blocks, after, image, loads, field), (vec, total))
    sums0 = everywhere(partial)
    base, sums0 = lax.optimization_barrier((base, sums0))
    m1, m3 = got[1], got[3]
    second, after, *sends = call(
        second_kernel, "second", (picked, placed, inverse, gains, *got, base),
        (vec, vec, buf, buf, buf, buf), alias={8: 0},
    )
    s0, s1, s2, s3 = sends
    q1, q3 = back(s1, "sector", True), back(s3, "axial", False)
    base, r1, w1, partial = call(
        first_step_kernel, "first_step",
        (sums0, blocks, after, loads, field, image, second, inverse), (vec, vec, vec, total),
    )
    sums1 = everywhere(partial)
    s0, s2, base, sums1 = lax.optimization_barrier((s0, s2, base, sums1))
    q0, q2 = onward(s0, "sector", True), onward(s2, "axial", False)
    r2, w2, partial = call(
        second_step_kernel, "second_step",
        (sums0, sums1, placed, far_u1, far_u3, m1, m3, q1, q3, field, image, second, after, r1, w1, inverse, base),
        (vec, vec, total),
    )
    sums2 = everywhere(partial)
    estimate, left = call(
        last_kernel, "last",
        (sums0, sums1, sums2, placed, q0, q1, q2, q3, field, image, inverse, r1, w1, r2, w2), (vec, vec),
        (pltpu.VMEM(loads.shape, F32), pltpu.VMEM(loads.shape, F32), pltpu.SemaphoreType.DMA((STRIPES + 1,))),
        out=pl.BlockSpec(memory_space=pl.ANY),
    )
    return estimate.reshape(points, cases), left.reshape(points, cases)


def solution(mesh):
    wide = P(AXES, None)
    deep = P(AXES, None, None)
    return jax.shard_map(
        shards,
        mesh=mesh,
        in_specs=(
            deep, deep, wide, wide, P(AXES), P(AXES), P(AXES),
            P(None, AXES, None), P(None, AXES, None), wide,
        ),
        out_specs=(wide, wide),
        check_vma=False,
    )
```

```python
import functools
import jax
import jax.numpy as jnp
from jax import lax
from jax.experimental import pallas as pl
from jax.experimental.pallas import tpu as pltpu
from jax.sharding import PartitionSpec as P

AXES = ("sector", "axial")
F32 = jnp.float32
BF16 = jnp.bfloat16
VMEM = pl.BlockSpec(memory_space=pltpu.VMEM)
HBM = pl.BlockSpec(memory_space=pltpu.HBM)
SMEM = pl.BlockSpec(memory_space=pltpu.SMEM)
NT = (((1,), (1,)), ((), ()))
CHUNK = 32
GROUP = 16
LIMIT = 14 << 20
WIDE = 60 << 20
STRIPES = 4


def struct(*shape, dtype=F32):
    return jax.ShapeDtypeStruct(shape, dtype)


def iota(shape, dim):
    return lax.broadcasted_iota(jnp.int32, shape, dim)


def split(value):
    high = value.astype(BF16)
    return high, (value - high.astype(F32)).astype(BF16)


def dot(left, right, dims=(((1,), (0,)), ((), ()))):
    return lax.dot_general(left, right, dims, preferred_element_type=F32)


def pack_kernel(slots_each, owners, patches, counts, kbb, inner, nodes, payload, meta, blocks, node_rows, tally):
    step = pl.program_id(0)
    chunk, bn, _ = inner.shape
    half, quarter = bn // 2, bn // 4
    elems = kbb.shape[2]

    @pl.when(step == 0)
    def _():
        for i in range(half):
            blocks[pl.ds(i, elems, stride=half), :] = jnp.concatenate([kbb[i], kbb[i + half]], axis=0).T
        node_rows[...] = nodes[...].T
        meta[...] = jnp.zeros_like(meta)

        def clear(i, carry):
            tally[i] = 0
            return carry

        lax.fori_loop(0, meta.shape[0] // slots_each, clear, 0)

    row_id = iota((bn, bn), 0)
    col_id = iota((bn, bn), 1)
    lower = (row_id > col_id)[:half, :half]
    upper = (row_id < col_id)[:half, :half]
    lane = iota((1, 128), 1)
    for first in range(0, chunk, GROUP):
        group = range(GROUP)
        where = [step * chunk + first + e for e in group]
        grams = [dot(inner[first + e], inner[first + e], NT) for e in group]
        picks = [(node_rows[pl.ds(i, 1), :] == row_id).astype(F32).astype(BF16) for i in where]
        pairs = []
        for e in group:
            both = blocks[pl.ds(pl.multiple_of(where[e] * half, half), half), :]
            block = jnp.concatenate([both[:, :bn], both[:, bn:]], axis=0)
            pairs.append(split(block - grams[e]))
        lefts = [dot(jnp.concatenate([picks[e], picks[e]], axis=1), jnp.concatenate(pairs[e], axis=0)) for e in group]
        pairs = [split(left) for left in lefts]
        placed_all = [dot(pairs[e][0], picks[e], NT) + dot(pairs[e][1], picks[e], NT) for e in group]
        for e in group:
            placed, index = placed_all[e], where[e]
            triangles = jnp.where(lower, placed[:half, :half], jnp.where(upper, placed[half:, half:], 0.0))
            packed = jnp.concatenate([triangles, placed[:half, half:]], axis=1)
            packed = jnp.concatenate([packed[:quarter], packed[quarter:]], axis=1)
            diag = jnp.sum(jnp.where(row_id == col_id, placed, 0.0), axis=0, keepdims=True)
            owner = owners[index]
            rank = tally[owner]
            tally[owner] = rank + 1
            slot = owner * slots_each + rank
            payload[pl.ds(pl.multiple_of(slot * quarter, quarter), quarter), :] = packed
            tag = jnp.where(index < counts[0], patches[index] + 1, 0).astype(F32)
            meta[pl.ds(slot, 1), :] = jnp.where(
                lane < bn, jnp.concatenate([diag, diag], axis=1), jnp.where(lane == bn, tag, 0.0)
            )


def pack_call(devices, owners, patches, counts, kbb, inner, nodes):
    elems, bn, ni = inner.shape
    slots_each = 2 * elems // devices
    slots = devices * slots_each
    whole = lambda *shape: pl.BlockSpec(shape, lambda i: (0,) * len(shape))
    return pl.pallas_call(
        functools.partial(pack_kernel, slots_each),
        grid=(elems // CHUNK,),
        in_specs=[
            SMEM,
            SMEM,
            SMEM,
            whole(bn, bn, elems),
            pl.BlockSpec((CHUNK, bn, ni), lambda i: (i, 0, 0)),
            whole(bn, elems),
        ],
        out_specs=[whole(slots * bn // 4, 128), whole(slots, 128)],
        out_shape=[struct(slots * bn // 4, 128), struct(slots, 128)],
        scratch_shapes=[
            pltpu.VMEM((elems * bn // 2, 128), F32),
            pltpu.VMEM((elems, bn), jnp.int32),
            pltpu.SMEM((devices,), jnp.int32),
        ],
        compiler_params=pltpu.CompilerParams(vmem_limit_bytes=WIDE),
        name="pack",
    )(owners, patches, counts, kbb, inner, nodes)


def send_values(picked, gains, field, sends):
    count = sends[0].shape[0]
    for which, send in enumerate(sends):

        def one(k, carry):
            send[k] = gains[which * count + k] * field[picked[which * count + k]]
            return carry

        lax.fori_loop(0, count, one, 0, unroll=4)


def take_values(placed, received, result):
    count = received[0].shape[0]
    for which, got in enumerate(received):

        def one(k, carry):
            patch = placed[which * count + k]
            result[patch] = result[patch] - got[k]
            return carry

        lax.fori_loop(0, count, one, 0, unroll=4)


def own_kernel(table, loads, gains, out0, out1, sems):
    bn = loads.shape[1]
    count = out0.shape[0]
    copies = []
    for which, out in enumerate((out0, out1)):
        for k in range(count):
            copies.append(
                pltpu.make_async_copy(loads.at[table[which, 0, k]], out.at[k, pl.ds(0, bn)], sems.at[which])
            )
    for copy in copies:
        copy.start()
    lane = iota((1, 128), 1)
    for which, out in enumerate((out0, out1)):
        rows = jnp.concatenate([gains[which], gains[which]], axis=1)
        for k in range(count):
            row = jnp.where(lane < bn, rows[k : k + 1], table[which, 1, k].astype(F32))
            out[k, pl.ds(bn, 8), :] = jnp.broadcast_to(row, (8, 128))
    for copy in copies:
        copy.wait()


def far_kernel(index, loads, out, sem):
    copies = []
    for k in range(out.shape[0]):
        at = index[0, 1, k] if len(index.shape) == 3 else index[k]
        copies.append(pltpu.make_async_copy(loads.at[at], out.at[k], sem))
    for copy in copies:
        copy.start()
    for copy in copies:
        copy.wait()


def own_call(table, loads, gains):
    out = struct(table.shape[2], loads.shape[1] + 8, loads.shape[2])
    return pl.pallas_call(
        own_kernel,
        in_specs=[SMEM, pl.BlockSpec(memory_space=pl.ANY), VMEM],
        out_specs=[VMEM, VMEM],
        out_shape=[out, out],
        scratch_shapes=[pltpu.SemaphoreType.DMA((2,))],
        compiler_params=pltpu.CompilerParams(vmem_limit_bytes=WIDE),
        name="own",
    )(table, loads, gains)


def far_call(index, loads):
    return pl.pallas_call(
        far_kernel,
        in_specs=[SMEM, pl.BlockSpec(memory_space=pl.ANY)],
        out_specs=VMEM,
        out_shape=struct(index.shape[-1], *loads.shape[1:]),
        scratch_shapes=[pltpu.SemaphoreType.DMA(())],
        compiler_params=pltpu.CompilerParams(vmem_limit_bytes=WIDE),
        name="far",
    )(index, loads)


def diagonal_kernel(tags, picked, meta, capacity, conduct, g0, g2, over, gain_rows, t0, t1, t2, t3, total):
    patch_dev, bn = capacity.shape
    count = conduct.shape[1]
    for which, got in enumerate((g0, g2)):
        gain_rows[pl.ds(2 * which * count, count), :] = jnp.concatenate([conduct[which], conduct[which]], axis=1)
        for k in range(count):
            gain_rows[pl.ds((2 * which + 1) * count + k, 1), :] = got[k, pl.ds(bn, 1), :]
    total[pl.ds(0, patch_dev), :] = jnp.concatenate([capacity[...], capacity[...]], axis=1)

    def add(i, carry):
        patch = tags[i]
        total[pl.ds(patch, 1), :] = total[pl.ds(patch, 1), :] + meta[pl.ds(i, 1), :]
        return carry

    lax.fori_loop(0, meta.shape[0], add, 0, unroll=4)

    def link(i, carry):
        patch = picked[i]
        total[pl.ds(patch, 1), :] = total[pl.ds(patch, 1), :] + gain_rows[pl.ds(i, 1), :]
        return carry

    lax.fori_loop(0, gain_rows.shape[0], link, 0, unroll=4)
    over[...] = 1.0 / total[pl.ds(0, patch_dev), :]
    for which, rows in enumerate((t0, t1, t2, t3)):
        for k in range(count):
            i = which * count + k
            rows[pl.ds(k, 1), :] = over[pl.ds(picked[i], 1), :] * gain_rows[pl.ds(i, 1), :]


def expand_kernel(over, gain_rows, loads, inverse, field, gains):
    bn = loads.shape[1]
    columns = over[...][:, :bn].T
    for p in range(over.shape[0]):
        column = jnp.broadcast_to(columns[:, p : p + 1], (bn, 128))
        inverse[p] = column
        field[p] = column * loads[p]
    columns = gain_rows[...][:, :bn].T
    for k in range(gain_rows.shape[0]):
        gains[k] = jnp.broadcast_to(columns[:, k : k + 1], (bn, 128))


def edges_kernel(t0, t1, t2, t3, g0, g1, g2, g3, p0, p1, p2, p3):
    count, bn, _ = p0.shape
    for rows, got, product in ((t0, g0, p0), (t1, g1, p1), (t2, g2, p2), (t3, g3, p3)):
        columns = rows[...][:, :bn].T
        for k in range(count):
            product[k] = jnp.broadcast_to(columns[:, k : k + 1], (bn, 128)) * got[k, pl.ds(0, bn), :]


def stacked(value):
    high, low = split(value)
    return jnp.concatenate([high, high, low], axis=0)


def folded(value):
    total = value[0:8]
    for i in range(8, value.shape[0], 8):
        total = total + value[i : i + 8]
    return total


def publish(partial, sums):
    rows = [jnp.sum(s, axis=0, keepdims=True) for s in sums]
    block = jnp.concatenate(rows + [jnp.zeros((8 - len(rows), 128), F32)], axis=0)
    for d in range(partial.shape[0]):
        partial[d] = block


def gathered(received):
    return jnp.sum(received[...], axis=0)


def zeros(n):
    return (jnp.zeros((8, 128), F32),) * n


def assemble_kernel(
    tags, picked, placed, payload, loads_in, field_in, inverse_in, gains_in, p0_in, p1_in, p2_in, p3_in,
    image, blocks, after, s0, s1, s2, s3, field, inverse, gains, packed, p0, p1, p2, p3, sems,
):
    patch_dev, bn, _ = image.shape
    half, quarter = bn // 2, bn // 4
    banks = packed.shape[0]
    slots = tags.shape[0]
    products = ((p0_in, p0), (p1_in, p1), (p2_in, p2), (p3_in, p3))
    pairs = ((loads_in, image), (field_in, field), *products, (inverse_in, inverse), (gains_in, gains))
    fetches = [pltpu.make_async_copy(src, dst, sems.at[i]) for i, (src, dst) in enumerate(pairs)]
    for copy in fetches:
        copy.start()
    packed[...] = jnp.zeros_like(packed)

    def add(j, carry):
        for bank in range(banks):
            i = j * banks + bank
            patch = tags[i]
            packed[bank, patch] = packed[bank, patch] + payload[pl.ds(pl.multiple_of(i * quarter, quarter), quarter), :]
        return carry

    lax.fori_loop(0, slots // banks, add, 0, unroll=2)
    fetches[0].wait()
    fetches[1].wait()
    row_id = iota((half, bn), 0)
    col_id = iota((half, bn), 1)
    kept = (col_id >= half) | (row_id > col_id)
    moved = (col_id < half) & (row_id < col_id)

    def build(j, carry):
        group = [j * GROUP + g for g in range(GROUP)]
        wholes = []
        for p in group:
            both = packed[0, p]
            for bank in range(1, banks):
                both = both + packed[bank, p]
            rows = jnp.concatenate([both[:, :bn], both[:, bn:]], axis=0)
            second = jnp.where(moved, rows, 0.0)[:, :half]
            second = jnp.concatenate([jnp.zeros((half, half), F32), second], axis=1)
            wholes.append(jnp.concatenate([jnp.where(kept, rows, 0.0), second], axis=0))
        wholes = [w + w.T for w in wholes]
        threes = []
        for w in wholes:
            high, low = split(w)
            threes.append(jnp.concatenate([high, low, high], axis=1))
        for p, three in zip(group, threes):
            blocks[p] = three
        products = [dot(three, stacked(field[p])) for p, three in zip(group, threes)]
        for p, product in zip(group, products):
            image[p] = image[p] + product
        return carry

    lax.fori_loop(0, patch_dev // GROUP, build, 0)
    for copy in fetches[2:]:
        copy.wait()
    take_values(placed, (p0, p1, p2, p3), image)

    def finish(p, carry):
        after[p] = inverse[p] * image[p]
        return carry

    lax.fori_loop(0, patch_dev, finish, 0, unroll=2)
    send_values(picked, gains, after, (s0, s1, s2, s3))


def times_all(blocks, field, base, result):
    def some(j, carry):
        group = [j * GROUP + g for g in range(GROUP)]
        products = [dot(blocks[p], stacked(field[p])) for p in group]
        for p, product in zip(group, products):
            result[p] = base[p] + product
        return carry

    lax.fori_loop(0, field.shape[0] // GROUP, some, 0)


def first_local_kernel(blocks, after, image, loads, field, result, partial):
    times_all(blocks, after, image, result)

    def one(p, carry):
        value = field[p]
        return carry[0] + folded(loads[p] * value), carry[1] + folded(image[p] * value)

    publish(partial, lax.fori_loop(0, loads.shape[0], one, zeros(2), unroll=2))


def second_kernel(picked, placed, inverse, gains, g0, g1, g2, g3, base, result, after, s0, s1, s2, s3):
    take_values(placed, (g0, g1, g2, g3), result)

    def scale(p, carry):
        after[p] = inverse[p] * result[p]
        return carry

    lax.fori_loop(0, inverse.shape[0], scale, 0, unroll=2)
    send_values(picked, gains, after, (s0, s1, s2, s3))


def first_step_kernel(
    sums, blocks, after, loads, field, image, second, inverse, result, left, left_image, partial
):
    times_all(blocks, after, second, result)
    first = gathered(sums)
    alpha = first[0:1] / first[1:2]

    def one(p, carry):
        r = loads[p] - alpha * image[p]
        w = image[p] - alpha * second[p]
        u = inverse[p] * r
        left[p] = r
        left_image[p] = w
        return (
            carry[0] + folded(r * u),
            carry[1] + folded(u * w),
            carry[2] + folded(u * image[p] + field[p] * w),
        )

    publish(partial, lax.fori_loop(0, loads.shape[0], one, zeros(3), unroll=2))


def second_step_kernel(
    sums0, sums1, placed, u1, u3, m1, m3, q1, q3, field, image, second, after, r1, w1, inverse, base,
    r2_out, w2_out, partial,
):
    first, then = gathered(sums0), gathered(sums1)
    alpha0 = first[0:1] / first[1:2]
    beta1 = then[0:1] / first[0:1]
    alpha1 = then[0:1] / (then[1:2] + beta1 * (then[2:3] + beta1 * first[1:2]))
    both = alpha0 * alpha1
    count = u1.shape[0]

    def one(p, carry):
        w, r = w1[p], r1[p]
        s1 = w + beta1 * image[p]
        r2 = r - alpha1 * s1
        w2 = w - alpha1 * ((1.0 + beta1) * second[p]) + both * base[p]
        u2 = inverse[p] * r2
        p1 = inverse[p] * r + beta1 * field[p]
        r2_out[p] = r2
        w2_out[p] = w2
        return (
            carry[0] + folded(r2 * u2),
            carry[1] + folded(u2 * w2),
            carry[2] + folded(u2 * s1 + p1 * w2),
        )

    sums = lax.fori_loop(0, field.shape[0], one, zeros(3), unroll=2)
    links = zeros(2)
    for which, (far_u, far_m, far_q) in ((1, (u1, m1, q1)), (3, (u3, m3, q3))):

        def link(k, carry):
            p = placed[which * count + k]
            u, m, q = far_u[k], far_m[k], far_q[k]
            u2 = inverse[p] * r2_out[p]
            p1 = inverse[p] * r1[p] + beta1 * field[p]
            far_p1 = (1.0 + beta1) * u - alpha0 * m
            far_u2 = u - (alpha0 + alpha1 * (1.0 + beta1)) * m + both * q
            here = after[p]
            return carry[0] + folded(u2 * q + far_u2 * here), carry[1] + folded(p1 * q + far_p1 * here)

        links = lax.fori_loop(0, count, link, links, unroll=2)
    publish(partial, (sums[0], sums[1] - both * links[0], sums[2] - both * links[1]))


def last_kernel(
    sums0, sums1, sums2, placed, g0, g1, g2, g3, field, image, inverse, r1, w1, r2, w2,
    estimate_out, left_out, estimate, left, sems,
):
    first, then, last = gathered(sums0), gathered(sums1), gathered(sums2)
    alpha0 = first[0:1] / first[1:2]
    beta1 = then[0:1] / first[0:1]
    curve1 = then[1:2] + beta1 * (then[2:3] + beta1 * first[1:2])
    alpha1 = then[0:1] / curve1
    beta2 = last[0:1] / then[0:1]
    alpha2 = last[0:1] / (last[1:2] + beta2 * (last[2:3] + beta2 * curve1))
    part = alpha2 * alpha0 * alpha1
    size = field.shape[0] // STRIPES
    copies = []

    def residual(p, carry):
        left[p] = r2[p] - alpha2 * (w2[p] + beta2 * (w1[p] + beta1 * image[p]))
        return carry

    lax.fori_loop(0, field.shape[0], residual, 0, unroll=2)
    count = g0.shape[0]
    for which, got in enumerate((g0, g1, g2, g3)):

        def link(k, carry):
            patch = placed[which * count + k]
            left[patch] = left[patch] + part * got[k]
            return carry

        lax.fori_loop(0, count, link, 0, unroll=4)

    def iterate(p, carry):
        p1 = inverse[p] * r1[p] + beta1 * field[p]
        estimate[p] = alpha0 * field[p] + alpha1 * p1 + alpha2 * (inverse[p] * r2[p] + beta2 * p1)
        return carry

    copies.append(pltpu.make_async_copy(left, left_out, sems.at[STRIPES]))
    copies[-1].start()
    for c in range(STRIPES):
        lax.fori_loop(c * size, (c + 1) * size, iterate, 0, unroll=2)
        rows = pl.ds(c * size, size)
        copies.append(pltpu.make_async_copy(estimate.at[rows], estimate_out.at[rows], sems.at[c]))
        copies[-1].start()
    for copy in copies:
        copy.wait()


def call(kernel, name, ins, outs, scratch=(), flops=0, alias=None, limit=None, far=(), out=VMEM):
    ints = lambda a: a.ndim == 1 and a.dtype == jnp.int32
    moved = sum(a.size * a.dtype.itemsize for a in ins) + sum(s.size * s.dtype.itemsize for s in outs)
    return pl.pallas_call(
        kernel,
        in_specs=[SMEM if ints(a) else HBM if i in far else VMEM for i, a in enumerate(ins)],
        out_specs=[out] * len(outs),
        out_shape=list(outs),
        scratch_shapes=list(scratch),
        input_output_aliases=alias or {},
        cost_estimate=pl.CostEstimate(flops=flops, bytes_accessed=moved, transcendentals=0),
        compiler_params=pltpu.CompilerParams(vmem_limit_bytes=limit or LIMIT),
        name=name,
    )(*[pltpu.with_memory_space_constraint(a, pltpu.HBM) if i in far else a for i, a in enumerate(ins)])


def everywhere(partial):
    return lax.all_to_all(partial, AXES, split_axis=0, concat_axis=0, tiled=True)


def onward(value, axis, wrap):
    n = lax.axis_size(axis)
    return lax.ppermute(value, axis, [(i, (i + 1) % n) for i in range(n) if wrap or i + 1 < n])


def back(value, axis, wrap):
    n = lax.axis_size(axis)
    return lax.ppermute(value, axis, [((i + 1) % n, i) for i in range(n) if wrap or i + 1 < n])


def exchange(s0, s1, s2, s3):
    return (
        onward(s0, "sector", True),
        back(s1, "sector", True),
        onward(s2, "axial", False),
        back(s3, "axial", False),
    )


def shards(kbb, interior, node_lists, owners, patch_ids, counts, capacity, links, conduct, loads):
    elems, bn = node_lists.shape
    devices = lax.axis_size("sector") * lax.axis_size("axial")
    points, cases = loads.shape
    patch_dev = points // bn
    count = conduct.shape[1]
    loads = loads.reshape(patch_dev, bn, cases)
    vec = struct(patch_dev, bn, cases)
    buf = struct(count, bn, cases)
    total = struct(devices, 8, cases)

    table = links.transpose(0, 2, 1)
    s0, s2 = own_call(table, loads, conduct)
    owners, later, s0, s2 = lax.optimization_barrier((owners, table, s0, s2))
    g0, g2 = onward(s0, "sector", True), onward(s2, "axial", False)
    behind = onward(later, "sector", True)
    payload, meta = pack_call(
        devices, owners.reshape(elems), patch_ids, counts,
        kbb.transpose(1, 2, 0), interior.transpose(0, 2, 1), node_lists.T,
    )
    slots = meta.shape[0]
    payload, meta, behind = lax.optimization_barrier((payload, meta, behind))
    s1 = far_call(behind, loads)
    meta, s1 = lax.optimization_barrier((meta, s1))
    g1 = back(s1, "sector", True)
    payload, g0, g2 = lax.optimization_barrier((payload, g0, g2))
    far_axial = g2[:, bn, bn].astype(jnp.int32)
    s3 = far_call(far_axial, loads)
    meta = everywhere(meta.reshape(devices, slots // devices, 128)).reshape(slots, 128)
    payload, g1, s3 = lax.optimization_barrier((payload, g1, s3))
    g3 = back(s3, "axial", False)
    payload = everywhere(payload.reshape(devices, -1, 128)).reshape(slots * bn // 4, 128)
    own_sector, own_axial, far_sector = later[0, 0], later[1, 0], behind[0, 1]
    picked = jnp.concatenate([own_sector, far_sector, own_axial, far_axial])
    placed = jnp.concatenate([far_sector, own_sector, far_axial, own_axial])
    tags = meta[:, bn].astype(jnp.int32)
    tags = jnp.where(tags > 0, tags - 1, patch_dev)
    row = struct(count, 128)
    table_out = struct(patch_dev, 128)
    over, gain_rows, *rows = call(
        diagonal_kernel, "diagonal",
        (tags, picked, meta, capacity.reshape(patch_dev, bn), conduct, g0, g2),
        (table_out, struct(4 * count, 128), row, row, row, row),
        (pltpu.VMEM((patch_dev + 8, 128), F32),), limit=WIDE,
    )
    rows = exchange(*rows)
    inverse, field, gains = call(
        expand_kernel, "expand", (over, gain_rows, loads), (vec, vec, struct(4 * count, bn, cases)), limit=WIDE
    )
    edges = call(edges_kernel, "edges", (*rows, g0, g1, g2, g3), (buf, buf, buf, buf), limit=WIDE)
    far_u1, far_u3 = edges[1], edges[3]
    image, blocks, after, *rest = call(
        assemble_kernel, "assemble",
        (tags, picked, placed, payload, loads, field, inverse, gains, *edges),
        (vec, struct(patch_dev, bn, 3 * bn, dtype=BF16), vec, buf, buf, buf, buf,
         vec, vec, struct(4 * count, bn, cases)),
        (pltpu.VMEM((4, patch_dev + 1, bn // 4, 128), F32), *[pltpu.VMEM((count, bn, cases), F32)] * 4,
         pltpu.SemaphoreType.DMA((8,))),
        far=(4, 5, 6, 7, 8, 9, 10, 11),
    )
    *sends, field, inverse, gains = rest
    got = exchange(*sends)
    base, partial = call(first_local_kernel, "first_local", (blocks, after, image, loads, field), (vec, total))
    sums0 = everywhere(partial)
    base, sums0 = lax.optimization_barrier((base, sums0))
    m1, m3 = got[1], got[3]
    second, after, *sends = call(
        second_kernel, "second", (picked, placed, inverse, gains, *got, base),
        (vec, vec, buf, buf, buf, buf), alias={8: 0},
    )
    s0, s1, s2, s3 = sends
    q1, q3 = back(s1, "sector", True), back(s3, "axial", False)
    base, r1, w1, partial = call(
        first_step_kernel, "first_step",
        (sums0, blocks, after, loads, field, image, second, inverse), (vec, vec, vec, total),
    )
    sums1 = everywhere(partial)
    s0, s2, base, sums1 = lax.optimization_barrier((s0, s2, base, sums1))
    q0, q2 = onward(s0, "sector", True), onward(s2, "axial", False)
    r2, w2, partial = call(
        second_step_kernel, "second_step",
        (sums0, sums1, placed, far_u1, far_u3, m1, m3, q1, q3, field, image, second, after, r1, w1, inverse, base),
        (vec, vec, total),
    )
    sums2 = everywhere(partial)
    r2, w2, sums2 = lax.optimization_barrier((r2, w2, sums2))
    estimate, left = call(
        last_kernel, "last",
        (sums0, sums1, sums2, placed, q0, q1, q2, q3, field, image, inverse, r1, w1, r2, w2), (vec, vec),
        (pltpu.VMEM(loads.shape, F32), pltpu.VMEM(loads.shape, F32), pltpu.SemaphoreType.DMA((STRIPES + 1,))),
        out=pl.BlockSpec(memory_space=pl.ANY),
    )
    return estimate.reshape(points, cases), left.reshape(points, cases)


def solution(mesh):
    wide = P(AXES, None)
    deep = P(AXES, None, None)
    return jax.shard_map(
        shards,
        mesh=mesh,
        in_specs=(
            deep, deep, wide, wide, P(AXES), P(AXES), P(AXES),
            P(None, AXES, None), P(None, AXES, None), wide,
        ),
        out_specs=(wide, wide),
        check_vma=False,
    )
```

```python
import functools
import jax
import jax.numpy as jnp
from jax import lax
from jax.experimental import pallas as pl
from jax.experimental.pallas import tpu as pltpu
from jax.sharding import PartitionSpec as P

AXES = ("sector", "axial")
F32 = jnp.float32
BF16 = jnp.bfloat16
VMEM = pl.BlockSpec(memory_space=pltpu.VMEM)
HBM = pl.BlockSpec(memory_space=pltpu.HBM)
SMEM = pl.BlockSpec(memory_space=pltpu.SMEM)
NT = (((1,), (1,)), ((), ()))
CHUNK = 32
GROUP = 16
LIMIT = 14 << 20
WIDE = 60 << 20
STRIPES = 4


def struct(*shape, dtype=F32):
    return jax.ShapeDtypeStruct(shape, dtype)


def iota(shape, dim):
    return lax.broadcasted_iota(jnp.int32, shape, dim)


def split(value):
    high = value.astype(BF16)
    return high, (value - high.astype(F32)).astype(BF16)


def dot(left, right, dims=(((1,), (0,)), ((), ()))):
    return lax.dot_general(left, right, dims, preferred_element_type=F32)


def pack_kernel(slots_each, owners, patches, counts, kbb, inner, nodes, payload, meta, blocks, node_rows, tally):
    step = pl.program_id(0)
    chunk, bn, _ = inner.shape
    half, quarter = bn // 2, bn // 4
    elems = kbb.shape[2]

    @pl.when(step == 0)
    def _():
        for i in range(half):
            blocks[pl.ds(i, elems, stride=half), :] = jnp.concatenate([kbb[i], kbb[i + half]], axis=0).T
        node_rows[...] = nodes[...].T
        meta[...] = jnp.zeros_like(meta)

        def clear(i, carry):
            tally[i] = 0
            return carry

        lax.fori_loop(0, meta.shape[0] // slots_each, clear, 0)

    row_id = iota((bn, bn), 0)
    col_id = iota((bn, bn), 1)
    lower = (row_id > col_id)[:half, :half]
    upper = (row_id < col_id)[:half, :half]
    lane = iota((1, 128), 1)
    for first in range(0, chunk, GROUP):
        group = range(GROUP)
        where = [step * chunk + first + e for e in group]
        grams = [dot(inner[first + e], inner[first + e], NT) for e in group]
        picks = [(node_rows[pl.ds(i, 1), :] == row_id).astype(F32).astype(BF16) for i in where]
        pairs = []
        for e in group:
            both = blocks[pl.ds(pl.multiple_of(where[e] * half, half), half), :]
            block = jnp.concatenate([both[:, :bn], both[:, bn:]], axis=0)
            pairs.append(split(block - grams[e]))
        lefts = [dot(jnp.concatenate([picks[e], picks[e]], axis=1), jnp.concatenate(pairs[e], axis=0)) for e in group]
        pairs = [split(left) for left in lefts]
        placed_all = [dot(pairs[e][0], picks[e], NT) + dot(pairs[e][1], picks[e], NT) for e in group]
        for e in group:
            placed, index = placed_all[e], where[e]
            triangles = jnp.where(lower, placed[:half, :half], jnp.where(upper, placed[half:, half:], 0.0))
            packed = jnp.concatenate([triangles, placed[:half, half:]], axis=1)
            packed = jnp.concatenate([packed[:quarter], packed[quarter:]], axis=1)
            diag = jnp.sum(jnp.where(row_id == col_id, placed, 0.0), axis=0, keepdims=True)
            owner = owners[index]
            rank = tally[owner]
            tally[owner] = rank + 1
            slot = owner * slots_each + rank
            payload[pl.ds(pl.multiple_of(slot * quarter, quarter), quarter), :] = packed
            tag = jnp.where(index < counts[0], patches[index] + 1, 0).astype(F32)
            meta[pl.ds(slot, 1), :] = jnp.where(
                lane < bn, jnp.concatenate([diag, diag], axis=1), jnp.where(lane == bn, tag, 0.0)
            )


def pack_call(devices, owners, patches, counts, kbb, inner, nodes):
    elems, bn, ni = inner.shape
    slots_each = 2 * elems // devices
    slots = devices * slots_each
    whole = lambda *shape: pl.BlockSpec(shape, lambda i: (0,) * len(shape))
    return pl.pallas_call(
        functools.partial(pack_kernel, slots_each),
        grid=(elems // CHUNK,),
        in_specs=[
            SMEM,
            SMEM,
            SMEM,
            whole(bn, bn, elems),
            pl.BlockSpec((CHUNK, bn, ni), lambda i: (i, 0, 0)),
            whole(bn, elems),
        ],
        out_specs=[whole(slots * bn // 4, 128), whole(slots, 128)],
        out_shape=[struct(slots * bn // 4, 128), struct(slots, 128)],
        scratch_shapes=[
            pltpu.VMEM((elems * bn // 2, 128), F32),
            pltpu.VMEM((elems, bn), jnp.int32),
            pltpu.SMEM((devices,), jnp.int32),
        ],
        compiler_params=pltpu.CompilerParams(vmem_limit_bytes=WIDE),
        name="pack",
    )(owners, patches, counts, kbb, inner, nodes)


def send_values(picked, gains, field, sends):
    count = sends[0].shape[0]
    for which, send in enumerate(sends):

        def one(k, carry):
            send[k] = gains[which * count + k] * field[picked[which * count + k]]
            return carry

        lax.fori_loop(0, count, one, 0, unroll=4)


def take_values(placed, received, result):
    count = received[0].shape[0]
    for which, got in enumerate(received):

        def one(k, carry):
            patch = placed[which * count + k]
            result[patch] = result[patch] - got[k]
            return carry

        lax.fori_loop(0, count, one, 0, unroll=4)


def own_kernel(table, loads, gains, out0, out1, sems):
    bn = loads.shape[1]
    count = out0.shape[0]
    copies = []
    for which, out in enumerate((out0, out1)):
        for k in range(count):
            copies.append(
                pltpu.make_async_copy(loads.at[table[which, 0, k]], out.at[k, pl.ds(0, bn)], sems.at[which])
            )
    for copy in copies:
        copy.start()
    lane = iota((1, 128), 1)
    for which, out in enumerate((out0, out1)):
        rows = jnp.concatenate([gains[which], gains[which]], axis=1)
        for k in range(count):
            row = jnp.where(lane < bn, rows[k : k + 1], table[which, 1, k].astype(F32))
            out[k, pl.ds(bn, 8), :] = jnp.broadcast_to(row, (8, 128))
    for copy in copies:
        copy.wait()


def far_kernel(index, loads, out, sem):
    copies = []
    for k in range(out.shape[0]):
        at = index[0, 1, k] if len(index.shape) == 3 else index[k]
        copies.append(pltpu.make_async_copy(loads.at[at], out.at[k], sem))
    for copy in copies:
        copy.start()
    for copy in copies:
        copy.wait()


def own_call(table, loads, gains):
    out = struct(table.shape[2], loads.shape[1] + 8, loads.shape[2])
    return pl.pallas_call(
        own_kernel,
        in_specs=[SMEM, pl.BlockSpec(memory_space=pl.ANY), VMEM],
        out_specs=[VMEM, VMEM],
        out_shape=[out, out],
        scratch_shapes=[pltpu.SemaphoreType.DMA((2,))],
        compiler_params=pltpu.CompilerParams(vmem_limit_bytes=WIDE),
        name="own",
    )(table, loads, gains)


def far_call(index, loads):
    return pl.pallas_call(
        far_kernel,
        in_specs=[SMEM, pl.BlockSpec(memory_space=pl.ANY)],
        out_specs=VMEM,
        out_shape=struct(index.shape[-1], *loads.shape[1:]),
        scratch_shapes=[pltpu.SemaphoreType.DMA(())],
        compiler_params=pltpu.CompilerParams(vmem_limit_bytes=WIDE),
        name="far",
    )(index, loads)


def diagonal_kernel(tags, picked, meta, capacity, conduct, g0, g2, over, gain_rows, t0, t1, t2, t3, total):
    patch_dev, bn = capacity.shape
    count = conduct.shape[1]
    for which, got in enumerate((g0, g2)):
        gain_rows[pl.ds(2 * which * count, count), :] = jnp.concatenate([conduct[which], conduct[which]], axis=1)
        for k in range(count):
            gain_rows[pl.ds((2 * which + 1) * count + k, 1), :] = got[k, pl.ds(bn, 1), :]
    total[pl.ds(0, patch_dev), :] = jnp.concatenate([capacity[...], capacity[...]], axis=1)

    def add(i, carry):
        patch = tags[i]
        total[pl.ds(patch, 1), :] = total[pl.ds(patch, 1), :] + meta[pl.ds(i, 1), :]
        return carry

    lax.fori_loop(0, meta.shape[0], add, 0, unroll=4)

    def link(i, carry):
        patch = picked[i]
        total[pl.ds(patch, 1), :] = total[pl.ds(patch, 1), :] + gain_rows[pl.ds(i, 1), :]
        return carry

    lax.fori_loop(0, gain_rows.shape[0], link, 0, unroll=4)
    over[...] = 1.0 / total[pl.ds(0, patch_dev), :]
    for which, rows in enumerate((t0, t1, t2, t3)):
        for k in range(count):
            i = which * count + k
            rows[pl.ds(k, 1), :] = over[pl.ds(picked[i], 1), :] * gain_rows[pl.ds(i, 1), :]


def expand_kernel(over, gain_rows, loads, inverse, field, gains):
    bn = loads.shape[1]
    columns = over[...][:, :bn].T
    for p in range(over.shape[0]):
        column = jnp.broadcast_to(columns[:, p : p + 1], (bn, 128))
        inverse[p] = column
        field[p] = column * loads[p]
    columns = gain_rows[...][:, :bn].T
    for k in range(gain_rows.shape[0]):
        gains[k] = jnp.broadcast_to(columns[:, k : k + 1], (bn, 128))


def edges_kernel(t0, t1, t2, t3, g0, g1, g2, g3, p0, p1, p2, p3):
    count, bn, _ = p0.shape
    for rows, got, product in ((t0, g0, p0), (t1, g1, p1), (t2, g2, p2), (t3, g3, p3)):
        columns = rows[...][:, :bn].T
        for k in range(count):
            product[k] = jnp.broadcast_to(columns[:, k : k + 1], (bn, 128)) * got[k, pl.ds(0, bn), :]


def stacked(value):
    high, low = split(value)
    return jnp.concatenate([high, high, low], axis=0)


def folded(value):
    total = value[0:8]
    for i in range(8, value.shape[0], 8):
        total = total + value[i : i + 8]
    return total


def publish(partial, sums):
    rows = [jnp.sum(s, axis=0, keepdims=True) for s in sums]
    block = jnp.concatenate(rows + [jnp.zeros((partial.shape[1] - len(rows), 128), F32)], axis=0)
    for d in range(partial.shape[0]):
        partial[d] = block


def gathered(received):
    return jnp.sum(received[...], axis=0)


def zeros(n):
    return (jnp.zeros((8, 128), F32),) * n


def assemble_kernel(
    tags, picked, placed, payload, loads_in, field_in, inverse_in, gains_in, p0_in, p1_in, p2_in, p3_in,
    image, blocks, after, s0, s1, s2, s3, field, inverse, gains, packed, p0, p1, p2, p3, sems,
):
    patch_dev, bn, _ = image.shape
    half, quarter = bn // 2, bn // 4
    banks = packed.shape[0]
    slots = tags.shape[0]
    products = ((p0_in, p0), (p1_in, p1), (p2_in, p2), (p3_in, p3))
    pairs = ((loads_in, image), (field_in, field), *products, (inverse_in, inverse), (gains_in, gains))
    fetches = [pltpu.make_async_copy(src, dst, sems.at[i]) for i, (src, dst) in enumerate(pairs)]
    for copy in fetches:
        copy.start()
    packed[...] = jnp.zeros_like(packed)

    def add(j, carry):
        for bank in range(banks):
            i = j * banks + bank
            patch = tags[i]
            packed[bank, patch] = packed[bank, patch] + payload[pl.ds(pl.multiple_of(i * quarter, quarter), quarter), :]
        return carry

    lax.fori_loop(0, slots // banks, add, 0, unroll=2)
    fetches[0].wait()
    fetches[1].wait()
    row_id = iota((half, bn), 0)
    col_id = iota((half, bn), 1)
    kept = (col_id >= half) | (row_id > col_id)
    moved = (col_id < half) & (row_id < col_id)

    def build(j, carry):
        group = [j * GROUP + g for g in range(GROUP)]
        wholes = []
        for p in group:
            both = packed[0, p]
            for bank in range(1, banks):
                both = both + packed[bank, p]
            rows = jnp.concatenate([both[:, :bn], both[:, bn:]], axis=0)
            second = jnp.where(moved, rows, 0.0)[:, :half]
            second = jnp.concatenate([jnp.zeros((half, half), F32), second], axis=1)
            wholes.append(jnp.concatenate([jnp.where(kept, rows, 0.0), second], axis=0))
        wholes = [w + w.T for w in wholes]
        threes = []
        for w in wholes:
            high, low = split(w)
            threes.append(jnp.concatenate([high, low, high], axis=1))
        for p, three in zip(group, threes):
            blocks[p] = three
        products = [dot(three, stacked(field[p])) for p, three in zip(group, threes)]
        for p, product in zip(group, products):
            image[p] = image[p] + product
        return carry

    lax.fori_loop(0, patch_dev // GROUP, build, 0)
    for copy in fetches[2:]:
        copy.wait()
    take_values(placed, (p0, p1, p2, p3), image)

    def finish(p, carry):
        after[p] = inverse[p] * image[p]
        return carry

    lax.fori_loop(0, patch_dev, finish, 0, unroll=2)
    send_values(picked, gains, after, (s0, s1, s2, s3))


def times_all(blocks, field, base, result):
    def some(j, carry):
        group = [j * GROUP + g for g in range(GROUP)]
        products = [dot(blocks[p], stacked(field[p])) for p in group]
        for p, product in zip(group, products):
            result[p] = base[p] + product
        return carry

    lax.fori_loop(0, field.shape[0] // GROUP, some, 0)


def first_local_kernel(blocks, after, image, loads, field, result, partial):
    times_all(blocks, after, image, result)

    def one(p, carry):
        value = field[p]
        return carry[0] + folded(loads[p] * value), carry[1] + folded(image[p] * value)

    publish(partial, lax.fori_loop(0, loads.shape[0], one, zeros(2), unroll=2))


def second_kernel(picked, placed, inverse, gains, g0, g1, g2, g3, base, result, after, s0, s1, s2, s3):
    take_values(placed, (g0, g1, g2, g3), result)

    def scale(p, carry):
        after[p] = inverse[p] * result[p]
        return carry

    lax.fori_loop(0, inverse.shape[0], scale, 0, unroll=2)
    send_values(picked, gains, after, (s0, s1, s2, s3))


SUMS = 14


def first_step_kernel(sums, blocks, after, loads, field, image, second, inverse, result, left, left_image, totals):
    times_all(blocks, after, second, result)
    first = gathered(sums)
    alpha = first[0:1] / first[1:2]
    bn = loads.shape[1]

    def one(p, carry):
        carry = list(carry)
        for i in range(0, bn, 8):
            rows = pl.ds(i, 8)
            w0, n0, u0, over = image[p, rows], second[p, rows], field[p, rows], inverse[p, rows]
            r1 = loads[p, rows] - alpha * w0
            w1 = w0 - alpha * n0
            n1 = n0 - alpha * result[p, rows]
            left[p, rows] = r1
            left_image[p, rows] = w1
            u1, m1, m0 = over * r1, over * w1, over * w0
            terms = (
                r1 * u1, u1 * w1, u1 * w0, u0 * w1, w1 * m1, w1 * m0, w0 * m0,
                u1 * n1, u1 * n0, m1 * n1, m1 * n0 + m0 * n1, m0 * n0, u0 * n1, u0 * n0,
            )
            carry = [c + t for c, t in zip(carry, terms)]
        return tuple(carry)

    for i, value in enumerate(lax.fori_loop(0, loads.shape[0], one, zeros(SUMS))):
        totals[i] = value


def links_kernel(
    sums0, placed, totals, far_u0, far_u2, far_m0, far_m2, far_q0, far_q2, field, image, after, r1, w1, inverse, partial
):
    first = gathered(sums0)
    alpha = first[0:1] / first[1:2]
    count = far_u0.shape[0]
    sums = zeros(4)
    for which, (far_u, far_m, far_q) in ((1, (far_u0, far_m0, far_q0)), (3, (far_u2, far_m2, far_q2))):

        def link(k, carry):
            p = placed[which * count + k]
            u, m, q = far_u[k], far_m[k], far_q[k]
            over, here = inverse[p], after[p]
            ends = (
                (field[p], u),
                (over * image[p], m),
                (over * r1[p], u - alpha * m),
                (over * w1[p], m - alpha * q),
            )
            return tuple(c + folded(own * q + far * here) for c, (own, far) in zip(carry, ends))

        sums = lax.fori_loop(0, count, link, sums, unroll=2)
    u0n, m0n, u1n, m1n = (alpha * value for value in sums)
    added = {7: u1n, 9: m1n, 10: m0n, 12: u0n}
    publish(partial, [totals[i] + added[i] if i in added else totals[i] for i in range(SUMS)])


def last_kernel(
    sums0, sums1, placed, g0, g1, g2, g3, field, image, inverse, second, base, r1, w1,
    estimate_out, left_out, estimate, left, sems,
):
    first, then = gathered(sums0), gathered(sums1)
    alpha0 = first[0:1] / first[1:2]
    (r1u1, u1w1, u1w0, u0w1, w1m1, w1m0, w0m0, u1n1, u1n0, m1n1, mixed, m0n0, u0n1, u0n0) = (
        then[i : i + 1] for i in range(SUMS)
    )
    beta1 = r1u1 / first[0:1]
    curve1 = u1w1 + beta1 * (u1w0 + u0w1 + beta1 * first[1:2])
    a = r1u1 / curve1
    c = a * beta1
    r2u2 = r1u1 - 2.0 * (a * u1w1 + c * u1w0) + a * a * w1m1 + 2.0 * a * c * w1m0 + c * c * w0m0
    u2w2 = u1w1 - a * (u1n1 + w1m1) - c * (u1n0 + w1m0) + a * a * m1n1 + a * c * mixed + c * c * m0n0
    cross = (u1w1 - a * w1m1 - c * w1m0) + beta1 * (u1w0 - a * w1m0 - c * w0m0)
    cross = cross + (u1w1 - a * u1n1 - c * u1n0) + beta1 * (u0w1 - a * u0n1 - c * u0n0)
    beta2 = r2u2 / r1u1
    alpha2 = r2u2 / (u2w2 + beta2 * (cross + beta2 * curve1))
    steps = a + alpha2 * beta2
    for_u0 = alpha0 + steps * beta1
    part = alpha2 * alpha0 * a
    size = field.shape[0] // STRIPES
    copies = []

    def one(p, carry):
        w1p, w0p = w1[p], image[p]
        r2 = r1[p] - a * w1p - c * w0p
        estimate[p] = for_u0 * field[p] + inverse[p] * (steps * r1[p] + alpha2 * r2)
        n0 = second[p]
        w2 = w1p - a * (n0 - alpha0 * base[p]) - c * n0
        left[p] = r2 - alpha2 * (w2 + beta2 * (w1p + beta1 * w0p))
        return carry

    for k in range(STRIPES):
        lax.fori_loop(k * size, (k + 1) * size, one, 0, unroll=2)
        rows = pl.ds(k * size, size)
        copies.append(pltpu.make_async_copy(estimate.at[rows], estimate_out.at[rows], sems.at[k]))
        copies[-1].start()
    count = g0.shape[0]
    for which, got in enumerate((g0, g1, g2, g3)):

        def link(k, carry):
            patch = placed[which * count + k]
            left[patch] = left[patch] + part * got[k]
            return carry

        lax.fori_loop(0, count, link, 0, unroll=4)
    copies.append(pltpu.make_async_copy(left, left_out, sems.at[STRIPES]))
    copies[-1].start()
    for copy in copies:
        copy.wait()


def call(kernel, name, ins, outs, scratch=(), flops=0, alias=None, limit=None, far=(), out=VMEM):
    ints = lambda a: a.ndim == 1 and a.dtype == jnp.int32
    moved = sum(a.size * a.dtype.itemsize for a in ins) + sum(s.size * s.dtype.itemsize for s in outs)
    return pl.pallas_call(
        kernel,
        in_specs=[SMEM if ints(a) else HBM if i in far else VMEM for i, a in enumerate(ins)],
        out_specs=[out] * len(outs),
        out_shape=list(outs),
        scratch_shapes=list(scratch),
        input_output_aliases=alias or {},
        cost_estimate=pl.CostEstimate(flops=flops, bytes_accessed=moved, transcendentals=0),
        compiler_params=pltpu.CompilerParams(vmem_limit_bytes=limit or LIMIT),
        name=name,
    )(*[pltpu.with_memory_space_constraint(a, pltpu.HBM) if i in far else a for i, a in enumerate(ins)])


def everywhere(partial):
    return lax.all_to_all(partial, AXES, split_axis=0, concat_axis=0, tiled=True)


def onward(value, axis, wrap):
    n = lax.axis_size(axis)
    return lax.ppermute(value, axis, [(i, (i + 1) % n) for i in range(n) if wrap or i + 1 < n])


def back(value, axis, wrap):
    n = lax.axis_size(axis)
    return lax.ppermute(value, axis, [((i + 1) % n, i) for i in range(n) if wrap or i + 1 < n])


def exchange(s0, s1, s2, s3):
    return (
        onward(s0, "sector", True),
        back(s1, "sector", True),
        onward(s2, "axial", False),
        back(s3, "axial", False),
    )


def shards(kbb, interior, node_lists, owners, patch_ids, counts, capacity, links, conduct, loads):
    elems, bn = node_lists.shape
    devices = lax.axis_size("sector") * lax.axis_size("axial")
    points, cases = loads.shape
    patch_dev = points // bn
    count = conduct.shape[1]
    loads = loads.reshape(patch_dev, bn, cases)
    vec = struct(patch_dev, bn, cases)
    buf = struct(count, bn, cases)
    total = struct(devices, 8, cases)

    table = links.transpose(0, 2, 1)
    s0, s2 = own_call(table, loads, conduct)
    owners, later, s0, s2 = lax.optimization_barrier((owners, table, s0, s2))
    g0, g2 = onward(s0, "sector", True), onward(s2, "axial", False)
    behind = onward(later, "sector", True)
    payload, meta = pack_call(
        devices, owners.reshape(elems), patch_ids, counts,
        kbb.transpose(1, 2, 0), interior.transpose(0, 2, 1), node_lists.T,
    )
    slots = meta.shape[0]
    payload, meta, behind = lax.optimization_barrier((payload, meta, behind))
    s1 = far_call(behind, loads)
    meta, s1 = lax.optimization_barrier((meta, s1))
    g1 = back(s1, "sector", True)
    payload, g0, g2 = lax.optimization_barrier((payload, g0, g2))
    far_axial = g2[:, bn, bn].astype(jnp.int32)
    s3 = far_call(far_axial, loads)
    meta = everywhere(meta.reshape(devices, slots // devices, 128)).reshape(slots, 128)
    payload, g1, s3 = lax.optimization_barrier((payload, g1, s3))
    g3 = back(s3, "axial", False)
    payload = everywhere(payload.reshape(devices, -1, 128)).reshape(slots * bn // 4, 128)
    own_sector, own_axial, far_sector = later[0, 0], later[1, 0], behind[0, 1]
    picked = jnp.concatenate([own_sector, far_sector, own_axial, far_axial])
    placed = jnp.concatenate([far_sector, own_sector, far_axial, own_axial])
    tags = meta[:, bn].astype(jnp.int32)
    tags = jnp.where(tags > 0, tags - 1, patch_dev)
    row = struct(count, 128)
    table_out = struct(patch_dev, 128)
    over, gain_rows, *rows = call(
        diagonal_kernel, "diagonal",
        (tags, picked, meta, capacity.reshape(patch_dev, bn), conduct, g0, g2),
        (table_out, struct(4 * count, 128), row, row, row, row),
        (pltpu.VMEM((patch_dev + 8, 128), F32),), limit=WIDE,
    )
    rows = exchange(*rows)
    inverse, field, gains = call(
        expand_kernel, "expand", (over, gain_rows, loads), (vec, vec, struct(4 * count, bn, cases)), limit=WIDE
    )
    edges = call(edges_kernel, "edges", (*rows, g0, g1, g2, g3), (buf, buf, buf, buf), limit=WIDE)
    far_u1, far_u3 = edges[1], edges[3]
    image, blocks, after, *rest = call(
        assemble_kernel, "assemble",
        (tags, picked, placed, payload, loads, field, inverse, gains, *edges),
        (vec, struct(patch_dev, bn, 3 * bn, dtype=BF16), vec, buf, buf, buf, buf,
         vec, vec, struct(4 * count, bn, cases)),
        (pltpu.VMEM((4, patch_dev + 1, bn // 4, 128), F32), *[pltpu.VMEM((count, bn, cases), F32)] * 4,
         pltpu.SemaphoreType.DMA((8,))),
        far=(4, 5, 6, 7, 8, 9, 10, 11),
    )
    *sends, field, inverse, gains = rest
    got = exchange(*sends)
    base, partial = call(first_local_kernel, "first_local", (blocks, after, image, loads, field), (vec, total))
    sums0 = everywhere(partial)
    base, sums0 = lax.optimization_barrier((base, sums0))
    m1, m3 = got[1], got[3]
    second, after, *sends = call(
        second_kernel, "second", (picked, placed, inverse, gains, *got, base),
        (vec, vec, buf, buf, buf, buf), alias={8: 0},
    )
    s0, s1, s2, s3 = sends
    q1, q3 = back(s1, "sector", True), back(s3, "axial", False)
    q0, q2 = onward(s0, "sector", True), onward(s2, "axial", False)
    base, r1, w1, totals = call(
        first_step_kernel, "first_step",
        (sums0, blocks, after, loads, field, image, second, inverse), (vec, vec, vec, struct(16, 8, cases)),
    )
    (partial,) = call(
        links_kernel, "links",
        (sums0, placed, totals, far_u1, far_u3, m1, m3, q1, q3, field, image, after, r1, w1, inverse),
        (struct(devices, 16, cases),),
    )
    sums1 = everywhere(partial)
    base, sums1 = lax.optimization_barrier((base, sums1))
    estimate, left = call(
        last_kernel, "last",
        (sums0, sums1, placed, q0, q1, q2, q3, field, image, inverse, second, base, r1, w1), (vec, vec),
        (pltpu.VMEM(loads.shape, F32), pltpu.VMEM(loads.shape, F32), pltpu.SemaphoreType.DMA((STRIPES + 1,))),
        out=pl.BlockSpec(memory_space=pl.ANY),
    )
    return estimate.reshape(points, cases), left.reshape(points, cases)


def solution(mesh):
    wide = P(AXES, None)
    deep = P(AXES, None, None)
    return jax.shard_map(
        shards,
        mesh=mesh,
        in_specs=(
            deep, deep, wide, wide, P(AXES), P(AXES), P(AXES),
            P(None, AXES, None), P(None, AXES, None), wide,
        ),
        out_specs=(wide, wide),
        check_vma=False,
    )
```

```python
import functools
import jax
import jax.numpy as jnp
from jax import lax
from jax.experimental import pallas as pl
from jax.experimental.pallas import tpu as pltpu
from jax.sharding import PartitionSpec as P

AXES = ("sector", "axial")
F32 = jnp.float32
BF16 = jnp.bfloat16
VMEM = pl.BlockSpec(memory_space=pltpu.VMEM)
HBM = pl.BlockSpec(memory_space=pltpu.HBM)
SMEM = pl.BlockSpec(memory_space=pltpu.SMEM)
NT = (((1,), (1,)), ((), ()))
CHUNK = 64
GROUP = 16
LIMIT = 14 << 20
WIDE = 60 << 20
STRIPES = 4


def struct(*shape, dtype=F32):
    return jax.ShapeDtypeStruct(shape, dtype)


def iota(shape, dim):
    return lax.broadcasted_iota(jnp.int32, shape, dim)


def split(value):
    high = value.astype(BF16)
    return high, (value - high.astype(F32)).astype(BF16)


def dot(left, right, dims=(((1,), (0,)), ((), ()))):
    return lax.dot_general(left, right, dims, preferred_element_type=F32)


def pack_kernel(slots_each, owners, patches, counts, kbb, inner, nodes, payload, meta, blocks, node_rows, tally):
    step = pl.program_id(0)
    chunk, bn, _ = inner.shape
    half, quarter = bn // 2, bn // 4
    elems = kbb.shape[2]

    @pl.when(step == 0)
    def _():
        for i in range(half):
            blocks[pl.ds(i, elems, stride=half), :] = jnp.concatenate([kbb[i], kbb[i + half]], axis=0).T
        node_rows[...] = nodes[...].T
        meta[...] = jnp.zeros_like(meta)

        def clear(i, carry):
            tally[i] = 0
            return carry

        lax.fori_loop(0, meta.shape[0] // slots_each, clear, 0)

    row_id = iota((bn, bn), 0)
    col_id = iota((bn, bn), 1)
    lower = (row_id > col_id)[:half, :half]
    upper = (row_id < col_id)[:half, :half]
    lane = iota((1, 128), 1)
    for first in range(0, chunk, GROUP):
        group = range(GROUP)
        where = [step * chunk + first + e for e in group]
        grams = [dot(inner[first + e], inner[first + e], NT) for e in group]
        picks = [(node_rows[pl.ds(i, 1), :] == row_id).astype(F32).astype(BF16) for i in where]
        pairs = []
        for e in group:
            both = blocks[pl.ds(pl.multiple_of(where[e] * half, half), half), :]
            block = jnp.concatenate([both[:, :bn], both[:, bn:]], axis=0)
            pairs.append(split(block - grams[e]))
        lefts = [dot(jnp.concatenate([picks[e], picks[e]], axis=1), jnp.concatenate(pairs[e], axis=0)) for e in group]
        pairs = [split(left) for left in lefts]
        placed_all = [dot(pairs[e][0], picks[e], NT) + dot(pairs[e][1], picks[e], NT) for e in group]
        for e in group:
            placed, index = placed_all[e], where[e]
            triangles = jnp.where(lower, placed[:half, :half], jnp.where(upper, placed[half:, half:], 0.0))
            packed = jnp.concatenate([triangles, placed[:half, half:]], axis=1)
            packed = jnp.concatenate([packed[:quarter], packed[quarter:]], axis=1)
            diag = jnp.sum(jnp.where(row_id == col_id, placed, 0.0), axis=0, keepdims=True)
            owner = owners[index]
            rank = tally[owner]
            tally[owner] = rank + 1
            slot = owner * slots_each + rank
            payload[pl.ds(pl.multiple_of(slot * quarter, quarter), quarter), :] = packed
            tag = jnp.where(index < counts[0], patches[index] + 1, 0).astype(F32)
            meta[pl.ds(slot, 1), :] = jnp.where(
                lane < bn, jnp.concatenate([diag, diag], axis=1), jnp.where(lane == bn, tag, 0.0)
            )


def pack_call(devices, owners, patches, counts, kbb, inner, nodes):
    elems, bn, ni = inner.shape
    slots_each = 2 * elems // devices
    slots = devices * slots_each
    whole = lambda *shape: pl.BlockSpec(shape, lambda i: (0,) * len(shape))
    return pl.pallas_call(
        functools.partial(pack_kernel, slots_each),
        grid=(elems // CHUNK,),
        in_specs=[
            SMEM,
            SMEM,
            SMEM,
            whole(bn, bn, elems),
            pl.BlockSpec((CHUNK, bn, ni), lambda i: (i, 0, 0)),
            whole(bn, elems),
        ],
        out_specs=[whole(slots * bn // 4, 128), whole(slots, 128)],
        out_shape=[struct(slots * bn // 4, 128), struct(slots, 128)],
        scratch_shapes=[
            pltpu.VMEM((elems * bn // 2, 128), F32),
            pltpu.VMEM((elems, bn), jnp.int32),
            pltpu.SMEM((devices,), jnp.int32),
        ],
        compiler_params=pltpu.CompilerParams(vmem_limit_bytes=WIDE),
        name="pack",
    )(owners, patches, counts, kbb, inner, nodes)


def send_values(picked, gains, field, sends):
    count = sends[0].shape[0]
    for which, send in enumerate(sends):

        def one(k, carry):
            send[k] = gains[which * count + k] * field[picked[which * count + k]]
            return carry

        lax.fori_loop(0, count, one, 0, unroll=4)


def take_values(placed, received, result):
    count = received[0].shape[0]
    for which, got in enumerate(received):

        def one(k, carry):
            patch = placed[which * count + k]
            result[patch] = result[patch] - got[k]
            return carry

        lax.fori_loop(0, count, one, 0, unroll=4)


def own_kernel(table, loads, gains, out0, out1, sems):
    bn = loads.shape[1]
    count = out0.shape[0]
    copies = []
    for which, out in enumerate((out0, out1)):
        for k in range(count):
            copies.append(
                pltpu.make_async_copy(loads.at[table[which, 0, k]], out.at[k, pl.ds(0, bn)], sems.at[which])
            )
    for copy in copies:
        copy.start()
    lane = iota((1, 128), 1)
    for which, out in enumerate((out0, out1)):
        rows = jnp.concatenate([gains[which], gains[which]], axis=1)
        for k in range(count):
            row = jnp.where(lane < bn, rows[k : k + 1], table[which, 1, k].astype(F32))
            out[k, pl.ds(bn, 8), :] = jnp.broadcast_to(row, (8, 128))
    for copy in copies:
        copy.wait()


def far_kernel(index, loads, out, sem):
    copies = []
    for k in range(out.shape[0]):
        at = index[0, 1, k] if len(index.shape) == 3 else index[k]
        copies.append(pltpu.make_async_copy(loads.at[at], out.at[k], sem))
    for copy in copies:
        copy.start()
    for copy in copies:
        copy.wait()


def own_call(table, loads, gains):
    out = struct(table.shape[2], loads.shape[1] + 8, loads.shape[2])
    return pl.pallas_call(
        own_kernel,
        in_specs=[SMEM, pl.BlockSpec(memory_space=pl.ANY), VMEM],
        out_specs=[VMEM, VMEM],
        out_shape=[out, out],
        scratch_shapes=[pltpu.SemaphoreType.DMA((2,))],
        compiler_params=pltpu.CompilerParams(vmem_limit_bytes=WIDE),
        name="own",
    )(table, loads, gains)


def far_call(index, loads):
    return pl.pallas_call(
        far_kernel,
        in_specs=[SMEM, pl.BlockSpec(memory_space=pl.ANY)],
        out_specs=VMEM,
        out_shape=struct(index.shape[-1], *loads.shape[1:]),
        scratch_shapes=[pltpu.SemaphoreType.DMA(())],
        compiler_params=pltpu.CompilerParams(vmem_limit_bytes=WIDE),
        name="far",
    )(index, loads)


def diagonal_kernel(tags, picked, meta, capacity, conduct, g0, g2, over, gain_rows, t0, t1, t2, t3, total):
    patch_dev, bn = capacity.shape
    count = conduct.shape[1]
    for which, got in enumerate((g0, g2)):
        gain_rows[pl.ds(2 * which * count, count), :] = jnp.concatenate([conduct[which], conduct[which]], axis=1)
        for k in range(count):
            gain_rows[pl.ds((2 * which + 1) * count + k, 1), :] = got[k, pl.ds(bn, 1), :]
    total[pl.ds(0, patch_dev), :] = jnp.concatenate([capacity[...], capacity[...]], axis=1)

    def add(i, carry):
        patch = tags[i]
        total[pl.ds(patch, 1), :] = total[pl.ds(patch, 1), :] + meta[pl.ds(i, 1), :]
        return carry

    lax.fori_loop(0, meta.shape[0], add, 0, unroll=4)

    def link(i, carry):
        patch = picked[i]
        total[pl.ds(patch, 1), :] = total[pl.ds(patch, 1), :] + gain_rows[pl.ds(i, 1), :]
        return carry

    lax.fori_loop(0, gain_rows.shape[0], link, 0, unroll=4)
    over[...] = 1.0 / total[pl.ds(0, patch_dev), :]
    for which, rows in enumerate((t0, t1, t2, t3)):
        for k in range(count):
            i = which * count + k
            rows[pl.ds(k, 1), :] = over[pl.ds(picked[i], 1), :] * gain_rows[pl.ds(i, 1), :]


def expand_kernel(over, gain_rows, loads, inverse, field, gains):
    bn = loads.shape[1]
    columns = over[...][:, :bn].T
    for p in range(over.shape[0]):
        column = jnp.broadcast_to(columns[:, p : p + 1], (bn, 128))
        inverse[p] = column
        field[p] = column * loads[p]
    columns = gain_rows[...][:, :bn].T
    for k in range(gain_rows.shape[0]):
        gains[k] = jnp.broadcast_to(columns[:, k : k + 1], (bn, 128))


def edges_kernel(t0, t1, t2, t3, g0, g1, g2, g3, p0, p1, p2, p3):
    count, bn, _ = p0.shape
    for rows, got, product in ((t0, g0, p0), (t1, g1, p1), (t2, g2, p2), (t3, g3, p3)):
        columns = rows[...][:, :bn].T
        for k in range(count):
            product[k] = jnp.broadcast_to(columns[:, k : k + 1], (bn, 128)) * got[k, pl.ds(0, bn), :]


def stacked(value):
    high, low = split(value)
    return jnp.concatenate([high, high, low], axis=0)


def folded(value):
    total = value[0:8]
    for i in range(8, value.shape[0], 8):
        total = total + value[i : i + 8]
    return total


def publish(partial, sums):
    rows = [jnp.sum(s, axis=0, keepdims=True) for s in sums]
    block = jnp.concatenate(rows + [jnp.zeros((partial.shape[1] - len(rows), 128), F32)], axis=0)
    for d in range(partial.shape[0]):
        partial[d] = block


def gathered(received):
    return jnp.sum(received[...], axis=0)


def zeros(n):
    return (jnp.zeros((8, 128), F32),) * n


def three_parts(folds):
    half, bn = folds[0].shape[0] * 2, folds[0].shape[1] // 2
    row_id = iota((half, bn), 0)
    col_id = iota((half, bn), 1)
    kept = (col_id >= half) | (row_id > col_id)
    moved = (col_id < half) & (row_id < col_id)
    wholes = []
    for both in folds:
        rows = jnp.concatenate([both[:, :bn], both[:, bn:]], axis=0)
        second = jnp.where(moved, rows, 0.0)[:, :half]
        second = jnp.concatenate([jnp.zeros((half, half), F32), second], axis=1)
        wholes.append(jnp.concatenate([jnp.where(kept, rows, 0.0), second], axis=0))
    wholes = [w + w.T for w in wholes]
    pairs = [split(w) for w in wholes]
    return [jnp.concatenate([high, low, high], axis=1) for high, low in pairs]


def lead_kernel(
    tags, picked, placed, payload, loads_in, field_in, inverse_in, gains_in, p0_in, p1_in, p2_in, p3_in,
    image, folded_blocks, s0, s1, field, inverse, gains, packed, p0, p1, p2, p3, sems,
):
    patch_dev, bn, _ = image.shape
    quarter = bn // 4
    banks = packed.shape[0]
    products = ((p0_in, p0), (p1_in, p1), (p2_in, p2), (p3_in, p3))
    pairs = ((loads_in, image), *products, (field_in, field), (inverse_in, inverse), (gains_in, gains))
    fetches = [pltpu.make_async_copy(src, dst, sems.at[i]) for i, (src, dst) in enumerate(pairs)]
    for copy in fetches:
        copy.start()
    packed[...] = jnp.zeros_like(packed)

    def add(j, carry):
        for bank in range(banks):
            i = j * banks + bank
            patch = tags[i]
            packed[bank, patch] = packed[bank, patch] + payload[pl.ds(pl.multiple_of(i * quarter, quarter), quarter), :]
        return carry

    lax.fori_loop(0, tags.shape[0] // banks, add, 0, unroll=4)

    def join(p, carry):
        both = packed[0, p]
        for bank in range(1, banks):
            both = both + packed[bank, p]
        folded_blocks[p] = both
        return carry

    lax.fori_loop(0, patch_dev, join, 0, unroll=4)
    for copy in fetches[:6]:
        copy.wait()
    take_values(placed, (p0, p1, p2, p3), image)
    count = s0.shape[0]
    for which, send in enumerate((s0, s1)):
        for first in range(0, count, GROUP):
            group = [which * count + first + g for g in range(min(GROUP, count - first))]
            patches = [picked[i] for i in group]
            threes = three_parts([folded_blocks[p] for p in patches])
            values = [dot(three, stacked(field[p])) for p, three in zip(patches, threes)]
            if which == 0 and first == 0:
                fetches[6].wait()
                fetches[7].wait()
            for i, p, product in zip(group, patches, values):
                send[i - which * count] = gains[i] * (inverse[p] * (image[p] + product))


def assemble_kernel(picked, folded_blocks, start, field, inverse, gains, image, blocks, after, s2, s3):
    patch_dev = start.shape[0]

    def build(j, carry):
        group = [j * GROUP + g for g in range(GROUP)]
        threes = three_parts([folded_blocks[p] for p in group])
        products = [dot(three, stacked(field[p])) for p, three in zip(group, threes)]
        for p, three, product in zip(group, threes, products):
            blocks[p] = three
            here = start[p] + product
            image[p] = here
            after[p] = inverse[p] * here
        return carry

    lax.fori_loop(0, patch_dev // GROUP, build, 0)
    count = s2.shape[0]
    for which, send in ((2, s2), (3, s3)):

        def one(k, carry):
            send[k] = gains[which * count + k] * after[picked[which * count + k]]
            return carry

        lax.fori_loop(0, count, one, 0, unroll=4)


def times_all(blocks, field, base, result):
    def some(j, carry):
        group = [j * GROUP + g for g in range(GROUP)]
        products = [dot(blocks[p], stacked(field[p])) for p in group]
        for p, product in zip(group, products):
            result[p] = base[p] + product
        return carry

    lax.fori_loop(0, field.shape[0] // GROUP, some, 0)


def first_local_kernel(blocks, after, image, loads, field, result, partial):
    times_all(blocks, after, image, result)

    def one(p, carry):
        value = field[p]
        return carry[0] + folded(loads[p] * value), carry[1] + folded(image[p] * value)

    publish(partial, lax.fori_loop(0, loads.shape[0], one, zeros(2), unroll=2))


def second_kernel(picked, placed, inverse, gains, g0, g1, g2, g3, base, result, after, s0, s1, s2, s3):
    take_values(placed, (g0, g1, g2, g3), result)

    def scale(p, carry):
        after[p] = inverse[p] * result[p]
        return carry

    lax.fori_loop(0, inverse.shape[0], scale, 0, unroll=2)
    send_values(picked, gains, after, (s0, s1, s2, s3))


SUMS = 14


def first_step_kernel(sums, blocks, after, loads, field, image, second, inverse, result, left, left_image, totals):
    times_all(blocks, after, second, result)
    first = gathered(sums)
    alpha = first[0:1] / first[1:2]
    bn = loads.shape[1]

    def one(p, carry):
        carry = list(carry)
        for i in range(0, bn, 8):
            rows = pl.ds(i, 8)
            w0, n0, u0, over = image[p, rows], second[p, rows], field[p, rows], inverse[p, rows]
            r1 = loads[p, rows] - alpha * w0
            w1 = w0 - alpha * n0
            n1 = n0 - alpha * result[p, rows]
            left[p, rows] = r1
            left_image[p, rows] = w1
            u1, m1, m0 = over * r1, over * w1, over * w0
            terms = (
                r1 * u1, u1 * w1, u1 * w0, u0 * w1, w1 * m1, w1 * m0, w0 * m0,
                u1 * n1, u1 * n0, m1 * n1, m1 * n0 + m0 * n1, m0 * n0, u0 * n1, u0 * n0,
            )
            carry = [c + t for c, t in zip(carry, terms)]
        return tuple(carry)

    for i, value in enumerate(lax.fori_loop(0, loads.shape[0], one, zeros(SUMS))):
        totals[i] = value


def links_kernel(
    sums0, placed, totals, far_u0, far_u2, far_m0, far_m2, far_q0, far_q2, field, image, after, r1, w1, inverse, partial
):
    first = gathered(sums0)
    alpha = first[0:1] / first[1:2]
    count = far_u0.shape[0]
    sums = zeros(4)
    for which, (far_u, far_m, far_q) in ((1, (far_u0, far_m0, far_q0)), (3, (far_u2, far_m2, far_q2))):

        def link(k, carry):
            p = placed[which * count + k]
            u, m, q = far_u[k], far_m[k], far_q[k]
            over, here = inverse[p], after[p]
            ends = (
                (field[p], u),
                (over * image[p], m),
                (over * r1[p], u - alpha * m),
                (over * w1[p], m - alpha * q),
            )
            return tuple(c + folded(own * q + far * here) for c, (own, far) in zip(carry, ends))

        sums = lax.fori_loop(0, count, link, sums, unroll=2)
    u0n, m0n, u1n, m1n = (alpha * value for value in sums)
    added = {7: u1n, 9: m1n, 10: m0n, 12: u0n}
    publish(partial, [totals[i] + added[i] if i in added else totals[i] for i in range(SUMS)])


def last_kernel(
    sums0, sums1, placed, g0, g1, g2, g3, field, image, inverse, second, base, r1, w1,
    estimate_out, left_out, estimate, left, sems,
):
    first, then = gathered(sums0), gathered(sums1)
    alpha0 = first[0:1] / first[1:2]
    (r1u1, u1w1, u1w0, u0w1, w1m1, w1m0, w0m0, u1n1, u1n0, m1n1, mixed, m0n0, u0n1, u0n0) = (
        then[i : i + 1] for i in range(SUMS)
    )
    beta1 = r1u1 / first[0:1]
    curve1 = u1w1 + beta1 * (u1w0 + u0w1 + beta1 * first[1:2])
    a = r1u1 / curve1
    c = a * beta1
    r2u2 = r1u1 - 2.0 * (a * u1w1 + c * u1w0) + a * a * w1m1 + 2.0 * a * c * w1m0 + c * c * w0m0
    u2w2 = u1w1 - a * (u1n1 + w1m1) - c * (u1n0 + w1m0) + a * a * m1n1 + a * c * mixed + c * c * m0n0
    cross = (u1w1 - a * w1m1 - c * w1m0) + beta1 * (u1w0 - a * w1m0 - c * w0m0)
    cross = cross + (u1w1 - a * u1n1 - c * u1n0) + beta1 * (u0w1 - a * u0n1 - c * u0n0)
    beta2 = r2u2 / r1u1
    alpha2 = r2u2 / (u2w2 + beta2 * (cross + beta2 * curve1))
    steps = a + alpha2 * beta2
    for_u0 = alpha0 + steps * beta1
    part = alpha2 * alpha0 * a
    size = field.shape[0] // STRIPES
    copies = []

    def one(p, carry):
        w1p, w0p = w1[p], image[p]
        r2 = r1[p] - a * w1p - c * w0p
        estimate[p] = for_u0 * field[p] + inverse[p] * (steps * r1[p] + alpha2 * r2)
        n0 = second[p]
        w2 = w1p - a * (n0 - alpha0 * base[p]) - c * n0
        left[p] = r2 - alpha2 * (w2 + beta2 * (w1p + beta1 * w0p))
        return carry

    for k in range(STRIPES):
        lax.fori_loop(k * size, (k + 1) * size, one, 0, unroll=2)
        rows = pl.ds(k * size, size)
        copies.append(pltpu.make_async_copy(estimate.at[rows], estimate_out.at[rows], sems.at[k]))
        copies[-1].start()
    count = g0.shape[0]
    for which, got in enumerate((g0, g1, g2, g3)):

        def link(k, carry):
            patch = placed[which * count + k]
            left[patch] = left[patch] + part * got[k]
            return carry

        lax.fori_loop(0, count, link, 0, unroll=4)
    copies.append(pltpu.make_async_copy(left, left_out, sems.at[STRIPES]))
    copies[-1].start()
    for copy in copies:
        copy.wait()


def call(kernel, name, ins, outs, scratch=(), flops=0, alias=None, limit=None, far=(), out=VMEM):
    ints = lambda a: a.ndim == 1 and a.dtype == jnp.int32
    moved = sum(a.size * a.dtype.itemsize for a in ins) + sum(s.size * s.dtype.itemsize for s in outs)
    return pl.pallas_call(
        kernel,
        in_specs=[SMEM if ints(a) else HBM if i in far else VMEM for i, a in enumerate(ins)],
        out_specs=[out] * len(outs),
        out_shape=list(outs),
        scratch_shapes=list(scratch),
        input_output_aliases=alias or {},
        cost_estimate=pl.CostEstimate(flops=flops, bytes_accessed=moved, transcendentals=0),
        compiler_params=pltpu.CompilerParams(vmem_limit_bytes=limit or LIMIT),
        name=name,
    )(*[pltpu.with_memory_space_constraint(a, pltpu.HBM) if i in far else a for i, a in enumerate(ins)])


def everywhere(partial):
    return lax.all_to_all(partial, AXES, split_axis=0, concat_axis=0, tiled=True)


def onward(value, axis, wrap):
    n = lax.axis_size(axis)
    return lax.ppermute(value, axis, [(i, (i + 1) % n) for i in range(n) if wrap or i + 1 < n])


def back(value, axis, wrap):
    n = lax.axis_size(axis)
    return lax.ppermute(value, axis, [((i + 1) % n, i) for i in range(n) if wrap or i + 1 < n])


def exchange(s0, s1, s2, s3):
    return (
        onward(s0, "sector", True),
        back(s1, "sector", True),
        onward(s2, "axial", False),
        back(s3, "axial", False),
    )


def shards(kbb, interior, node_lists, owners, patch_ids, counts, capacity, links, conduct, loads):
    elems, bn = node_lists.shape
    devices = lax.axis_size("sector") * lax.axis_size("axial")
    points, cases = loads.shape
    patch_dev = points // bn
    count = conduct.shape[1]
    loads = loads.reshape(patch_dev, bn, cases)
    vec = struct(patch_dev, bn, cases)
    buf = struct(count, bn, cases)
    total = struct(devices, 8, cases)

    table = links.transpose(0, 2, 1)
    s0, s2 = own_call(table, loads, conduct)
    owners, later, s0, s2 = lax.optimization_barrier((owners, table, s0, s2))
    g0, g2 = onward(s0, "sector", True), onward(s2, "axial", False)
    behind = onward(later, "sector", True)
    payload, meta = pack_call(
        devices, owners.reshape(elems), patch_ids, counts,
        kbb.transpose(1, 2, 0), interior.transpose(0, 2, 1), node_lists.T,
    )
    slots = meta.shape[0]
    payload, meta, behind = lax.optimization_barrier((payload, meta, behind))
    s1 = far_call(behind, loads)
    meta, s1 = lax.optimization_barrier((meta, s1))
    g1 = back(s1, "sector", True)
    payload, g0, g2 = lax.optimization_barrier((payload, g0, g2))
    far_axial = g2[:, bn, bn].astype(jnp.int32)
    s3 = far_call(far_axial, loads)
    meta = everywhere(meta.reshape(devices, slots // devices, 128)).reshape(slots, 128)
    payload, g1, s3 = lax.optimization_barrier((payload, g1, s3))
    g3 = back(s3, "axial", False)
    payload = everywhere(payload.reshape(devices, -1, 128)).reshape(slots * bn // 4, 128)
    own_sector, own_axial, far_sector = later[0, 0], later[1, 0], behind[0, 1]
    picked = jnp.concatenate([own_sector, far_sector, own_axial, far_axial])
    placed = jnp.concatenate([far_sector, own_sector, far_axial, own_axial])
    tags = meta[:, bn].astype(jnp.int32)
    tags = jnp.where(tags > 0, tags - 1, patch_dev)
    row = struct(count, 128)
    table_out = struct(patch_dev, 128)
    over, gain_rows, *rows = call(
        diagonal_kernel, "diagonal",
        (tags, picked, meta, capacity.reshape(patch_dev, bn), conduct, g0, g2),
        (table_out, struct(4 * count, 128), row, row, row, row),
        (pltpu.VMEM((patch_dev + 8, 128), F32),), limit=WIDE,
    )
    rows = exchange(*rows)
    inverse, field, gains = call(
        expand_kernel, "expand", (over, gain_rows, loads), (vec, vec, struct(4 * count, bn, cases)), limit=WIDE
    )
    edges = call(edges_kernel, "edges", (*rows, g0, g1, g2, g3), (buf, buf, buf, buf), limit=WIDE)
    far_u1, far_u3 = edges[1], edges[3]
    start, folded_blocks, s0, s1, field, inverse, gains = call(
        lead_kernel, "lead",
        (tags, picked, placed, payload, loads, field, inverse, gains, *edges),
        (vec, struct(patch_dev, bn // 4, 128), buf, buf, vec, vec, struct(4 * count, bn, cases)),
        (pltpu.VMEM((4, patch_dev + 1, bn // 4, 128), F32), *[pltpu.VMEM((count, bn, cases), F32)] * 4,
         pltpu.SemaphoreType.DMA((8,))),
        far=(4, 5, 6, 7, 8, 9, 10, 11),
    )
    got0, got1 = onward(s0, "sector", True), back(s1, "sector", True)
    image, blocks, after, s2, s3 = call(
        assemble_kernel, "assemble", (picked, folded_blocks, start, field, inverse, gains),
        (vec, struct(patch_dev, bn, 3 * bn, dtype=BF16), vec, buf, buf),
    )
    got = (got0, got1, onward(s2, "axial", False), back(s3, "axial", False))
    base, partial = call(first_local_kernel, "first_local", (blocks, after, image, loads, field), (vec, total))
    sums0 = everywhere(partial)
    base, sums0 = lax.optimization_barrier((base, sums0))
    m1, m3 = got[1], got[3]
    second, after, *sends = call(
        second_kernel, "second", (picked, placed, inverse, gains, *got, base),
        (vec, vec, buf, buf, buf, buf), alias={8: 0},
    )
    s0, s1, s2, s3 = sends
    q1, q3 = back(s1, "sector", True), back(s3, "axial", False)
    q0, q2 = onward(s0, "sector", True), onward(s2, "axial", False)
    base, r1, w1, totals = call(
        first_step_kernel, "first_step",
        (sums0, blocks, after, loads, field, image, second, inverse), (vec, vec, vec, struct(16, 8, cases)),
    )
    (partial,) = call(
        links_kernel, "links",
        (sums0, placed, totals, far_u1, far_u3, m1, m3, q1, q3, field, image, after, r1, w1, inverse),
        (struct(devices, 16, cases),),
    )
    sums1 = everywhere(partial)
    base, sums1 = lax.optimization_barrier((base, sums1))
    estimate, left = call(
        last_kernel, "last",
        (sums0, sums1, placed, q0, q1, q2, q3, field, image, inverse, second, base, r1, w1), (vec, vec),
        (pltpu.VMEM(loads.shape, F32), pltpu.VMEM(loads.shape, F32), pltpu.SemaphoreType.DMA((STRIPES + 1,))),
        out=pl.BlockSpec(memory_space=pl.ANY),
    )
    return estimate.reshape(points, cases), left.reshape(points, cases)


def solution(mesh):
    wide = P(AXES, None)
    deep = P(AXES, None, None)
    return jax.shard_map(
        shards,
        mesh=mesh,
        in_specs=(
            deep, deep, wide, wide, P(AXES), P(AXES), P(AXES),
            P(None, AXES, None), P(None, AXES, None), wide,
        ),
        out_specs=(wide, wide),
        check_vma=False,
    )
```

```python
import functools
import jax
import jax.numpy as jnp
from jax import lax
from jax.experimental import pallas as pl
from jax.experimental.pallas import tpu as pltpu
from jax.sharding import PartitionSpec as P

AXES = ("sector", "axial")
F32 = jnp.float32
BF16 = jnp.bfloat16
VMEM = pl.BlockSpec(memory_space=pltpu.VMEM)
HBM = pl.BlockSpec(memory_space=pltpu.HBM)
SMEM = pl.BlockSpec(memory_space=pltpu.SMEM)
NT = (((1,), (1,)), ((), ()))
CHUNK = 64
GROUP = 16
LIMIT = 14 << 20
WIDE = 60 << 20
STRIPES = 4


def struct(*shape, dtype=F32):
    return jax.ShapeDtypeStruct(shape, dtype)


def iota(shape, dim):
    return lax.broadcasted_iota(jnp.int32, shape, dim)


def split(value):
    high = value.astype(BF16)
    return high, (value - high.astype(F32)).astype(BF16)


def dot(left, right, dims=(((1,), (0,)), ((), ()))):
    return lax.dot_general(left, right, dims, preferred_element_type=F32)


def pack_kernel(slots_each, owners, patches, counts, kbb, inner, nodes, payload, meta, blocks, node_rows, tally):
    step = pl.program_id(0)
    chunk, bn, _ = inner.shape
    half, quarter = bn // 2, bn // 4
    elems = kbb.shape[2]

    @pl.when(step == 0)
    def _():
        for i in range(half):
            blocks[pl.ds(i, elems, stride=half), :] = jnp.concatenate([kbb[i], kbb[i + half]], axis=0).T
        node_rows[...] = nodes[...].T
        meta[...] = jnp.zeros_like(meta)

        def clear(i, carry):
            tally[i] = 0
            return carry

        lax.fori_loop(0, meta.shape[0] // slots_each, clear, 0)

    row_id = iota((bn, bn), 0)
    col_id = iota((bn, bn), 1)
    lower = (row_id > col_id)[:half, :half]
    upper = (row_id < col_id)[:half, :half]
    lane = iota((1, 128), 1)
    for first in range(0, chunk, GROUP):
        group = range(GROUP)
        where = [step * chunk + first + e for e in group]
        grams = [dot(inner[first + e], inner[first + e], NT) for e in group]
        picks = [(node_rows[pl.ds(i, 1), :] == row_id).astype(F32).astype(BF16) for i in where]
        pairs = []
        for e in group:
            both = blocks[pl.ds(pl.multiple_of(where[e] * half, half), half), :]
            block = jnp.concatenate([both[:, :bn], both[:, bn:]], axis=0)
            pairs.append(split(block - grams[e]))
        lefts = [dot(jnp.concatenate([picks[e], picks[e]], axis=1), jnp.concatenate(pairs[e], axis=0)) for e in group]
        pairs = [split(left) for left in lefts]
        placed_all = [dot(pairs[e][0], picks[e], NT) + dot(pairs[e][1], picks[e], NT) for e in group]
        for e in group:
            placed, index = placed_all[e], where[e]
            triangles = jnp.where(lower, placed[:half, :half], jnp.where(upper, placed[half:, half:], 0.0))
            packed = jnp.concatenate([triangles, placed[:half, half:]], axis=1)
            packed = jnp.concatenate([packed[:quarter], packed[quarter:]], axis=1)
            diag = jnp.sum(jnp.where(row_id == col_id, placed, 0.0), axis=0, keepdims=True)
            owner = owners[index]
            rank = tally[owner]
            tally[owner] = rank + 1
            slot = owner * slots_each + rank
            payload[pl.ds(pl.multiple_of(slot * quarter, quarter), quarter), :] = packed
            tag = jnp.where(index < counts[0], patches[index] + 1, 0).astype(F32)
            meta[pl.ds(slot, 1), :] = jnp.where(
                lane < bn, jnp.concatenate([diag, diag], axis=1), jnp.where(lane == bn, tag, 0.0)
            )


def pack_call(devices, owners, patches, counts, kbb, inner, nodes):
    elems, bn, ni = inner.shape
    slots_each = 2 * elems // devices
    slots = devices * slots_each
    whole = lambda *shape: pl.BlockSpec(shape, lambda i: (0,) * len(shape))
    return pl.pallas_call(
        functools.partial(pack_kernel, slots_each),
        grid=(elems // CHUNK,),
        in_specs=[
            SMEM,
            SMEM,
            SMEM,
            whole(bn, bn, elems),
            pl.BlockSpec((CHUNK, bn, ni), lambda i: (i, 0, 0)),
            whole(bn, elems),
        ],
        out_specs=[whole(slots * bn // 4, 128), whole(slots, 128)],
        out_shape=[struct(slots * bn // 4, 128), struct(slots, 128)],
        scratch_shapes=[
            pltpu.VMEM((elems * bn // 2, 128), F32),
            pltpu.VMEM((elems, bn), jnp.int32),
            pltpu.SMEM((devices,), jnp.int32),
        ],
        compiler_params=pltpu.CompilerParams(vmem_limit_bytes=WIDE),
        name="pack",
    )(owners, patches, counts, kbb, inner, nodes)


def send_values(picked, gains, field, sends):
    count = sends[0].shape[0]
    for which, send in enumerate(sends):

        def one(k, carry):
            send[k] = gains[which * count + k] * field[picked[which * count + k]]
            return carry

        lax.fori_loop(0, count, one, 0, unroll=4)


def take_values(placed, received, result):
    count = received[0].shape[0]
    for which, got in enumerate(received):

        def one(k, carry):
            patch = placed[which * count + k]
            result[patch] = result[patch] - got[k]
            return carry

        lax.fori_loop(0, count, one, 0, unroll=4)


def own_kernel(table, loads, gains, out0, out1, sems):
    bn = loads.shape[1]
    count = out0.shape[0]
    copies = []
    for which, out in enumerate((out0, out1)):
        for k in range(count):
            copies.append(
                pltpu.make_async_copy(loads.at[table[which, 0, k]], out.at[k, pl.ds(0, bn)], sems.at[which])
            )
    for copy in copies:
        copy.start()
    lane = iota((1, 128), 1)
    for which, out in enumerate((out0, out1)):
        rows = jnp.concatenate([gains[which], gains[which]], axis=1)
        for k in range(count):
            row = jnp.where(lane < bn, rows[k : k + 1], table[which, 1, k].astype(F32))
            out[k, pl.ds(bn, 8), :] = jnp.broadcast_to(row, (8, 128))
    for copy in copies:
        copy.wait()


def far_kernel(index, loads, out, sem):
    copies = []
    for k in range(out.shape[0]):
        at = index[0, 1, k] if len(index.shape) == 3 else index[k]
        copies.append(pltpu.make_async_copy(loads.at[at], out.at[k], sem))
    for copy in copies:
        copy.start()
    for copy in copies:
        copy.wait()


def own_call(table, loads, gains):
    out = struct(table.shape[2], loads.shape[1] + 8, loads.shape[2])
    return pl.pallas_call(
        own_kernel,
        in_specs=[SMEM, pl.BlockSpec(memory_space=pl.ANY), VMEM],
        out_specs=[VMEM, VMEM],
        out_shape=[out, out],
        scratch_shapes=[pltpu.SemaphoreType.DMA((2,))],
        compiler_params=pltpu.CompilerParams(vmem_limit_bytes=WIDE),
        name="own",
    )(table, loads, gains)


def far_call(index, loads):
    return pl.pallas_call(
        far_kernel,
        in_specs=[SMEM, pl.BlockSpec(memory_space=pl.ANY)],
        out_specs=VMEM,
        out_shape=struct(index.shape[-1], *loads.shape[1:]),
        scratch_shapes=[pltpu.SemaphoreType.DMA(())],
        compiler_params=pltpu.CompilerParams(vmem_limit_bytes=WIDE),
        name="far",
    )(index, loads)


def diagonal_kernel(tags, picked, meta, capacity, conduct, g0, g2, over, gain_rows, t0, t1, t2, t3, total):
    patch_dev, bn = capacity.shape
    count = conduct.shape[1]
    for which, got in enumerate((g0, g2)):
        gain_rows[pl.ds(2 * which * count, count), :] = jnp.concatenate([conduct[which], conduct[which]], axis=1)
        for k in range(count):
            gain_rows[pl.ds((2 * which + 1) * count + k, 1), :] = got[k, pl.ds(bn, 1), :]
    total[pl.ds(0, patch_dev), :] = jnp.concatenate([capacity[...], capacity[...]], axis=1)

    def add(i, carry):
        patch = tags[i]
        total[pl.ds(patch, 1), :] = total[pl.ds(patch, 1), :] + meta[pl.ds(i, 1), :]
        return carry

    lax.fori_loop(0, meta.shape[0], add, 0, unroll=4)

    def link(i, carry):
        patch = picked[i]
        total[pl.ds(patch, 1), :] = total[pl.ds(patch, 1), :] + gain_rows[pl.ds(i, 1), :]
        return carry

    lax.fori_loop(0, gain_rows.shape[0], link, 0, unroll=4)
    over[...] = 1.0 / total[pl.ds(0, patch_dev), :]
    for which, rows in enumerate((t0, t1, t2, t3)):
        for k in range(count):
            i = which * count + k
            rows[pl.ds(k, 1), :] = over[pl.ds(picked[i], 1), :] * gain_rows[pl.ds(i, 1), :]


def expand_kernel(over, gain_rows, loads, inverse, field, gains):
    bn = loads.shape[1]
    columns = over[...][:, :bn].T
    for p in range(over.shape[0]):
        column = jnp.broadcast_to(columns[:, p : p + 1], (bn, 128))
        inverse[p] = column
        field[p] = column * loads[p]
    columns = gain_rows[...][:, :bn].T
    for k in range(gain_rows.shape[0]):
        gains[k] = jnp.broadcast_to(columns[:, k : k + 1], (bn, 128))


def edges_kernel(t0, t1, t2, t3, g0, g1, g2, g3, p0, p1, p2, p3):
    count, bn, _ = p0.shape
    for rows, got, product in ((t0, g0, p0), (t1, g1, p1), (t2, g2, p2), (t3, g3, p3)):
        columns = rows[...][:, :bn].T
        for k in range(count):
            product[k] = jnp.broadcast_to(columns[:, k : k + 1], (bn, 128)) * got[k, pl.ds(0, bn), :]


def stacked(value):
    high, low = split(value)
    return jnp.concatenate([high, high, low], axis=0)


def folded(value):
    total = value[0:8]
    for i in range(8, value.shape[0], 8):
        total = total + value[i : i + 8]
    return total


def publish(partial, sums):
    rows = [jnp.sum(s, axis=0, keepdims=True) for s in sums]
    block = jnp.concatenate(rows + [jnp.zeros((partial.shape[1] - len(rows), 128), F32)], axis=0)
    for d in range(partial.shape[0]):
        partial[d] = block


def gathered(received):
    return jnp.sum(received[...], axis=0)


def zeros(n):
    return (jnp.zeros((8, 128), F32),) * n


def three_parts(folds):
    half, bn = folds[0].shape[0] * 2, folds[0].shape[1] // 2
    row_id = iota((half, bn), 0)
    col_id = iota((half, bn), 1)
    kept = (col_id >= half) | (row_id > col_id)
    moved = (col_id < half) & (row_id < col_id)
    wholes = []
    for both in folds:
        rows = jnp.concatenate([both[:, :bn], both[:, bn:]], axis=0)
        second = jnp.where(moved, rows, 0.0)[:, :half]
        second = jnp.concatenate([jnp.zeros((half, half), F32), second], axis=1)
        wholes.append(jnp.concatenate([jnp.where(kept, rows, 0.0), second], axis=0))
    wholes = [w + w.T for w in wholes]
    pairs = [split(w) for w in wholes]
    return [jnp.concatenate([high, low, high], axis=1) for high, low in pairs]


def lead_kernel(
    tags, picked, placed, payload, loads_in, field_in, inverse_in, gains_in, p0_in, p1_in, p2_in, p3_in,
    image, folded_blocks, s0, s1, field, inverse, gains, packed, p0, p1, p2, p3, sems,
):
    patch_dev, bn, _ = image.shape
    quarter = bn // 4
    banks = packed.shape[0]
    products = ((p0_in, p0), (p1_in, p1), (p2_in, p2), (p3_in, p3))
    pairs = ((loads_in, image), *products, (field_in, field), (inverse_in, inverse), (gains_in, gains))
    fetches = [pltpu.make_async_copy(src, dst, sems.at[i]) for i, (src, dst) in enumerate(pairs)]
    for copy in fetches:
        copy.start()
    packed[...] = jnp.zeros_like(packed)

    def add(j, carry):
        for bank in range(banks):
            i = j * banks + bank
            patch = tags[i]
            packed[bank, patch] = packed[bank, patch] + payload[pl.ds(pl.multiple_of(i * quarter, quarter), quarter), :]
        return carry

    lax.fori_loop(0, tags.shape[0] // banks, add, 0, unroll=8)

    def join(p, carry):
        both = packed[0, p]
        for bank in range(1, banks):
            both = both + packed[bank, p]
        folded_blocks[p] = both
        return carry

    lax.fori_loop(0, patch_dev, join, 0, unroll=4)
    for copy in fetches[:6]:
        copy.wait()
    take_values(placed, (p0, p1, p2, p3), image)
    count = s0.shape[0]
    for which, send in enumerate((s0, s1)):
        for first in range(0, count, GROUP):
            group = [which * count + first + g for g in range(min(GROUP, count - first))]
            patches = [picked[i] for i in group]
            threes = three_parts([folded_blocks[p] for p in patches])
            values = [dot(three, stacked(field[p])) for p, three in zip(patches, threes)]
            if which == 0 and first == 0:
                fetches[6].wait()
                fetches[7].wait()
            for i, p, product in zip(group, patches, values):
                send[i - which * count] = gains[i] * (inverse[p] * (image[p] + product))


def assemble_kernel(picked, folded_blocks, start, field, inverse, gains, image, blocks, after, s2, s3):
    patch_dev = start.shape[0]

    def build(j, carry):
        group = [j * GROUP + g for g in range(GROUP)]
        threes = three_parts([folded_blocks[p] for p in group])
        products = [dot(three, stacked(field[p])) for p, three in zip(group, threes)]
        for p, three, product in zip(group, threes, products):
            blocks[p] = three
            here = start[p] + product
            image[p] = here
            after[p] = inverse[p] * here
        return carry

    lax.fori_loop(0, patch_dev // GROUP, build, 0)
    count = s2.shape[0]
    for which, send in ((2, s2), (3, s3)):

        def one(k, carry):
            send[k] = gains[which * count + k] * after[picked[which * count + k]]
            return carry

        lax.fori_loop(0, count, one, 0, unroll=4)


def times_all(blocks, field, base, result):
    def some(j, carry):
        group = [j * GROUP + g for g in range(GROUP)]
        products = [dot(blocks[p], stacked(field[p])) for p in group]
        for p, product in zip(group, products):
            result[p] = base[p] + product
        return carry

    lax.fori_loop(0, field.shape[0] // GROUP, some, 0)


def first_local_kernel(blocks, after, image, loads, field, result, partial):
    times_all(blocks, after, image, result)

    def one(p, carry):
        value = field[p]
        return carry[0] + folded(loads[p] * value), carry[1] + folded(image[p] * value)

    publish(partial, lax.fori_loop(0, loads.shape[0], one, zeros(2), unroll=2))


def second_kernel(picked, placed, inverse, gains, g0, g1, g2, g3, base, result, after, s0, s1, s2, s3):
    take_values(placed, (g0, g1, g2, g3), result)

    def scale(p, carry):
        after[p] = inverse[p] * result[p]
        return carry

    lax.fori_loop(0, inverse.shape[0], scale, 0, unroll=2)
    send_values(picked, gains, after, (s0, s1, s2, s3))


SUMS = 14


def first_step_kernel(sums, blocks, after, loads, field, image, second, inverse, result, left, left_image, totals):
    times_all(blocks, after, second, result)
    first = gathered(sums)
    alpha = first[0:1] / first[1:2]
    bn = loads.shape[1]

    def one(p, carry):
        carry = list(carry)
        for i in range(0, bn, 8):
            rows = pl.ds(i, 8)
            w0, n0, u0, over = image[p, rows], second[p, rows], field[p, rows], inverse[p, rows]
            r1 = loads[p, rows] - alpha * w0
            w1 = w0 - alpha * n0
            n1 = n0 - alpha * result[p, rows]
            left[p, rows] = r1
            left_image[p, rows] = w1
            u1, m1, m0 = over * r1, over * w1, over * w0
            terms = (
                r1 * u1, u1 * w1, u1 * w0, u0 * w1, w1 * m1, w1 * m0, w0 * m0,
                u1 * n1, u1 * n0, m1 * n1, m1 * n0 + m0 * n1, m0 * n0, u0 * n1, u0 * n0,
            )
            carry = [c + t for c, t in zip(carry, terms)]
        return tuple(carry)

    for i, value in enumerate(lax.fori_loop(0, loads.shape[0], one, zeros(SUMS))):
        totals[i] = value


def links_kernel(
    sums0, placed, totals, far_u0, far_u2, far_m0, far_m2, far_q0, far_q2, field, image, after, r1, w1, inverse, partial
):
    first = gathered(sums0)
    alpha = first[0:1] / first[1:2]
    count = far_u0.shape[0]
    sums = zeros(4)
    for which, (far_u, far_m, far_q) in ((1, (far_u0, far_m0, far_q0)), (3, (far_u2, far_m2, far_q2))):

        def link(k, carry):
            p = placed[which * count + k]
            u, m, q = far_u[k], far_m[k], far_q[k]
            over, here = inverse[p], after[p]
            ends = (
                (field[p], u),
                (over * image[p], m),
                (over * r1[p], u - alpha * m),
                (over * w1[p], m - alpha * q),
            )
            return tuple(c + folded(own * q + far * here) for c, (own, far) in zip(carry, ends))

        sums = lax.fori_loop(0, count, link, sums, unroll=2)
    u0n, m0n, u1n, m1n = (alpha * value for value in sums)
    added = {7: u1n, 9: m1n, 10: m0n, 12: u0n}
    publish(partial, [totals[i] + added[i] if i in added else totals[i] for i in range(SUMS)])


def last_kernel(
    sums0, sums1, placed, g0, g1, g2, g3, field, image, inverse, second, base, r1, w1,
    estimate_out, left_out, estimate, left, sems,
):
    first, then = gathered(sums0), gathered(sums1)
    alpha0 = first[0:1] / first[1:2]
    (r1u1, u1w1, u1w0, u0w1, w1m1, w1m0, w0m0, u1n1, u1n0, m1n1, mixed, m0n0, u0n1, u0n0) = (
        then[i : i + 1] for i in range(SUMS)
    )
    beta1 = r1u1 / first[0:1]
    curve1 = u1w1 + beta1 * (u1w0 + u0w1 + beta1 * first[1:2])
    a = r1u1 / curve1
    c = a * beta1
    r2u2 = r1u1 - 2.0 * (a * u1w1 + c * u1w0) + a * a * w1m1 + 2.0 * a * c * w1m0 + c * c * w0m0
    u2w2 = u1w1 - a * (u1n1 + w1m1) - c * (u1n0 + w1m0) + a * a * m1n1 + a * c * mixed + c * c * m0n0
    cross = (u1w1 - a * w1m1 - c * w1m0) + beta1 * (u1w0 - a * w1m0 - c * w0m0)
    cross = cross + (u1w1 - a * u1n1 - c * u1n0) + beta1 * (u0w1 - a * u0n1 - c * u0n0)
    beta2 = r2u2 / r1u1
    alpha2 = r2u2 / (u2w2 + beta2 * (cross + beta2 * curve1))
    steps = a + alpha2 * beta2
    for_u0 = alpha0 + steps * beta1
    part = alpha2 * alpha0 * a
    size = field.shape[0] // STRIPES
    copies = []

    def one(p, carry):
        w1p, w0p = w1[p], image[p]
        r2 = r1[p] - a * w1p - c * w0p
        estimate[p] = for_u0 * field[p] + inverse[p] * (steps * r1[p] + alpha2 * r2)
        n0 = second[p]
        w2 = w1p - a * (n0 - alpha0 * base[p]) - c * n0
        left[p] = r2 - alpha2 * (w2 + beta2 * (w1p + beta1 * w0p))
        return carry

    for k in range(STRIPES):
        lax.fori_loop(k * size, (k + 1) * size, one, 0, unroll=2)
        rows = pl.ds(k * size, size)
        copies.append(pltpu.make_async_copy(estimate.at[rows], estimate_out.at[rows], sems.at[k]))
        copies[-1].start()
    count = g0.shape[0]
    for which, got in enumerate((g0, g1, g2, g3)):

        def link(k, carry):
            patch = placed[which * count + k]
            left[patch] = left[patch] + part * got[k]
            return carry

        lax.fori_loop(0, count, link, 0, unroll=4)
    copies.append(pltpu.make_async_copy(left, left_out, sems.at[STRIPES]))
    copies[-1].start()
    for copy in copies:
        copy.wait()


def call(kernel, name, ins, outs, scratch=(), flops=0, alias=None, limit=None, far=(), out=VMEM):
    ints = lambda a: a.ndim == 1 and a.dtype == jnp.int32
    moved = sum(a.size * a.dtype.itemsize for a in ins) + sum(s.size * s.dtype.itemsize for s in outs)
    return pl.pallas_call(
        kernel,
        in_specs=[SMEM if ints(a) else HBM if i in far else VMEM for i, a in enumerate(ins)],
        out_specs=[out] * len(outs),
        out_shape=list(outs),
        scratch_shapes=list(scratch),
        input_output_aliases=alias or {},
        cost_estimate=pl.CostEstimate(flops=flops, bytes_accessed=moved, transcendentals=0),
        compiler_params=pltpu.CompilerParams(vmem_limit_bytes=limit or LIMIT),
        name=name,
    )(*[pltpu.with_memory_space_constraint(a, pltpu.HBM) if i in far else a for i, a in enumerate(ins)])


def everywhere(partial):
    return lax.all_to_all(partial, AXES, split_axis=0, concat_axis=0, tiled=True)


def onward(value, axis, wrap):
    n = lax.axis_size(axis)
    return lax.ppermute(value, axis, [(i, (i + 1) % n) for i in range(n) if wrap or i + 1 < n])


def back(value, axis, wrap):
    n = lax.axis_size(axis)
    return lax.ppermute(value, axis, [((i + 1) % n, i) for i in range(n) if wrap or i + 1 < n])


def exchange(s0, s1, s2, s3):
    return (
        onward(s0, "sector", True),
        back(s1, "sector", True),
        onward(s2, "axial", False),
        back(s3, "axial", False),
    )


def shards(kbb, interior, node_lists, owners, patch_ids, counts, capacity, links, conduct, loads):
    elems, bn = node_lists.shape
    devices = lax.axis_size("sector") * lax.axis_size("axial")
    points, cases = loads.shape
    patch_dev = points // bn
    count = conduct.shape[1]
    loads = loads.reshape(patch_dev, bn, cases)
    vec = struct(patch_dev, bn, cases)
    buf = struct(count, bn, cases)
    total = struct(devices, 8, cases)

    table = links.transpose(0, 2, 1)
    s0, s2 = own_call(table, loads, conduct)
    owners, later, s0, s2 = lax.optimization_barrier((owners, table, s0, s2))
    g0, g2 = onward(s0, "sector", True), onward(s2, "axial", False)
    behind = onward(later, "sector", True)
    payload, meta = pack_call(
        devices, owners.reshape(elems), patch_ids, counts,
        kbb.transpose(1, 2, 0), interior.transpose(0, 2, 1), node_lists.T,
    )
    slots = meta.shape[0]
    payload, meta, behind = lax.optimization_barrier((payload, meta, behind))
    s1 = far_call(behind, loads)
    meta, s1 = lax.optimization_barrier((meta, s1))
    g1 = back(s1, "sector", True)
    payload, g0, g2 = lax.optimization_barrier((payload, g0, g2))
    far_axial = g2[:, bn, bn].astype(jnp.int32)
    s3 = far_call(far_axial, loads)
    meta = everywhere(meta.reshape(devices, slots // devices, 128)).reshape(slots, 128)
    payload, g1, s3 = lax.optimization_barrier((payload, g1, s3))
    g3 = back(s3, "axial", False)
    payload = everywhere(payload.reshape(devices, -1, 128)).reshape(slots * bn // 4, 128)
    own_sector, own_axial, far_sector = later[0, 0], later[1, 0], behind[0, 1]
    picked = jnp.concatenate([own_sector, far_sector, own_axial, far_axial])
    placed = jnp.concatenate([far_sector, own_sector, far_axial, own_axial])
    tags = meta[:, bn].astype(jnp.int32)
    tags = jnp.where(tags > 0, tags - 1, patch_dev)
    row = struct(count, 128)
    table_out = struct(patch_dev, 128)
    over, gain_rows, *rows = call(
        diagonal_kernel, "diagonal",
        (tags, picked, meta, capacity.reshape(patch_dev, bn), conduct, g0, g2),
        (table_out, struct(4 * count, 128), row, row, row, row),
        (pltpu.VMEM((patch_dev + 8, 128), F32),), limit=WIDE,
    )
    rows = exchange(*rows)
    inverse, field, gains = call(
        expand_kernel, "expand", (over, gain_rows, loads), (vec, vec, struct(4 * count, bn, cases)), limit=WIDE
    )
    edges = call(edges_kernel, "edges", (*rows, g0, g1, g2, g3), (buf, buf, buf, buf), limit=WIDE)
    far_u1, far_u3 = edges[1], edges[3]
    start, folded_blocks, s0, s1, field, inverse, gains = call(
        lead_kernel, "lead",
        (tags, picked, placed, payload, loads, field, inverse, gains, *edges),
        (vec, struct(patch_dev, bn // 4, 128), buf, buf, vec, vec, struct(4 * count, bn, cases)),
        (pltpu.VMEM((2, patch_dev + 1, bn // 4, 128), F32), *[pltpu.VMEM((count, bn, cases), F32)] * 4,
         pltpu.SemaphoreType.DMA((8,))),
        far=(4, 5, 6, 7, 8, 9, 10, 11),
    )
    got0, got1 = onward(s0, "sector", True), back(s1, "sector", True)
    image, blocks, after, s2, s3 = call(
        assemble_kernel, "assemble", (picked, folded_blocks, start, field, inverse, gains),
        (vec, struct(patch_dev, bn, 3 * bn, dtype=BF16), vec, buf, buf),
    )
    got = (got0, got1, onward(s2, "axial", False), back(s3, "axial", False))
    base, partial = call(first_local_kernel, "first_local", (blocks, after, image, loads, field), (vec, total))
    sums0 = everywhere(partial)
    base, sums0 = lax.optimization_barrier((base, sums0))
    m1, m3 = got[1], got[3]
    second, after, *sends = call(
        second_kernel, "second", (picked, placed, inverse, gains, *got, base),
        (vec, vec, buf, buf, buf, buf), alias={8: 0},
    )
    s0, s1, s2, s3 = sends
    q1, q3 = back(s1, "sector", True), back(s3, "axial", False)
    q0, q2 = onward(s0, "sector", True), onward(s2, "axial", False)
    base, r1, w1, totals = call(
        first_step_kernel, "first_step",
        (sums0, blocks, after, loads, field, image, second, inverse), (vec, vec, vec, struct(16, 8, cases)),
    )
    (partial,) = call(
        links_kernel, "links",
        (sums0, placed, totals, far_u1, far_u3, m1, m3, q1, q3, field, image, after, r1, w1, inverse),
        (struct(devices, 16, cases),),
    )
    sums1 = everywhere(partial)
    base, sums1 = lax.optimization_barrier((base, sums1))
    estimate, left = call(
        last_kernel, "last",
        (sums0, sums1, placed, q0, q1, q2, q3, field, image, inverse, second, base, r1, w1), (vec, vec),
        (pltpu.VMEM(loads.shape, F32), pltpu.VMEM(loads.shape, F32), pltpu.SemaphoreType.DMA((STRIPES + 1,))),
        out=pl.BlockSpec(memory_space=pl.ANY),
    )
    return estimate.reshape(points, cases), left.reshape(points, cases)


def solution(mesh):
    wide = P(AXES, None)
    deep = P(AXES, None, None)
    return jax.shard_map(
        shards,
        mesh=mesh,
        in_specs=(
            deep, deep, wide, wide, P(AXES), P(AXES), P(AXES),
            P(None, AXES, None), P(None, AXES, None), wide,
        ),
        out_specs=(wide, wide),
        check_vma=False,
    )
```
